32 devices in a mesh: grp: 2 (over core), tile: 16 (over z, y, x).
Axes of the slice: x: 2, y: 2, z: 4, core: 2. Of those that a mesh axis runs over, the one named last changes fastest.
Arguments:
- basis: bfloat16 [32, 5, 64, 16, 128], P(None, None, 'tile'), may hold values from -18 to 18
- snapshots: bfloat16 [2, 4, 64, 16, 128], P('grp', None, 'tile'), may hold values from -1.5 to 1.5
- coupling: float32 [5, 5], replicated, may hold values from -2.5 to 2.5
Outputs:
- new_vector: float32 [2, 5, 64, 16, 128], P('grp', None, 'tile')
- coefficients: float32 [2, 32], P('grp')
- norms: float32 [2], P('grp')
The draws below stay inside these ranges and needn't reach their ends.
All inputs are finite; a program needn't handle non-finite values.
Results may differ from the reference program's by a relative error of at most 0.0003.
Values may be sent and summed in bfloat16 or wider, within the bound.
A program may use at most 64 MiB of HBM per device.

```python
import jax
import jax.numpy as jnp
from jax import lax

NY = 16
NZ = 128
KRYLOV = 32
NX = 64
STEPS = 2
N_GRP = 2


def draw_basis(key, part):
    extent = (KRYLOV, 5, NX, NY, NZ)
    position = jnp.arange(NX, dtype=jnp.float32).reshape(1, 1, NX, 1, 1) / max(NX - 1, 1)
    values = jnp.clip(jax.random.normal(key, extent, jnp.float32), -6.0, 6.0) * jnp.exp(jnp.log(3.0) * position)
    return values.astype(jnp.bfloat16)


def levels(own_key, dims, pieces, least, high):
    level = 1.0
    for axis_at, parts in pieces:
        draws = jax.random.uniform(jax.random.fold_in(jax.random.fold_in(own_key, 6), axis_at), (parts,), jnp.float32, least / len(pieces), high / len(pieces))
        level = level * jnp.repeat(jnp.exp(draws), dims[axis_at] // parts).reshape((-1,) + (1,) * (len(dims) - 1 - axis_at))
    return level


def noise(stream_key, dims, width, reach, kind=jnp.bfloat16):
    values = width * jax.random.normal(stream_key, dims, jnp.float32)
    return jnp.clip(values, min=-reach, max=reach).astype(kind)


def setup_inputs(seed: int = 0) -> dict:
    key_list = jax.random.split(jax.random.key(seed), 4)
    basis = draw_basis(jax.random.fold_in(key_list[3], 71), 0)
    snapshots = jnp.clip(jax.random.uniform(key_list[1], (STEPS, 4, NX, NY, NZ), jnp.float32, -1.5, 1.5) * levels(key_list[1], (STEPS, 4, NX, NY, NZ), ((0, 2), (2, 16)), -0.4, 0.0), -1.5, 1.5).astype(jnp.bfloat16)
    coupling = noise(key_list[2], (5, 5), 5 ** -0.5, 2.5, jnp.float32)
    return {"basis": basis, "snapshots": snapshots, "coupling": coupling}


viscosity = 0.5
time_step = 0.3

def tendency(extended, base, coupling):
    center = extended[:, 1:-1]
    slope_x = 0.5 * (extended[:, 2:] - extended[:, :-2])
    walled = jnp.pad(center, ((0, 0), (0, 0), (1, 1), (0, 0)))
    upper_y = walled[:, :, 2:]
    lower_y = walled[:, :, :-2]
    slope_y = 0.5 * (upper_y - lower_y)
    upper_z = jnp.roll(center, -1, axis=3)
    lower_z = jnp.roll(center, 1, axis=3)
    slope_z = 0.5 * (upper_z - lower_z)
    laplace = extended[:, 2:] + extended[:, :-2] + upper_y + lower_y + upper_z + lower_z - 6.0 * center
    advect = base[0] * slope_x + base[1] * slope_y + base[2] * slope_z
    coupled = jnp.einsum('kj,jxyz->kxyz', coupling, center, precision=lax.Precision.HIGHEST)
    return viscosity * laplace - advect - base[3] * coupled

def periodic(field):
    return jnp.concatenate([field[:, -1:], field, field[:, :1]], axis=1)

def runge_kutta(state, base, coupling):
    first = state + time_step * tendency(periodic(state), base, coupling)
    second = 0.75 * state + 0.25 * (first + time_step * tendency(periodic(first), base, coupling))
    return state / 3.0 + 2.0 / 3.0 * (second + time_step * tendency(periodic(second), base, coupling))

def project(basis, field, count):
    return lax.map(lambda vector: jnp.sum(vector.astype(jnp.float32) * field) / count, basis)

def expand(basis, weights, field):

    def accumulate(total, pair):
        vector, weight = pair
        return (total - weight * vector.astype(jnp.float32), None)
    result, unused = lax.scan(accumulate, field, (basis, weights))
    return result

def reference(basis, snapshots, coupling):
    krylov = basis.shape[0]
    count = jnp.float32(basis[0].size)
    outputs = []
    coefs = []
    norm_list = []
    for member in range(N_GRP):
        state = basis[krylov - N_GRP + member].astype(jnp.float32)
        for step_index in range(snapshots.shape[0]):
            state = runge_kutta(state, snapshots[step_index].astype(jnp.float32), coupling)
        first_coef = project(basis, state, count)
        first_left = expand(basis, first_coef, state)
        second_coef = project(basis, first_left, count)
        second_left = expand(basis, second_coef, first_left)
        norm_value = jnp.sqrt(jnp.sum(second_left * second_left) / count)
        outputs.append(second_left / norm_value)
        coefs.append(first_coef + second_coef)
        norm_list.append(norm_value)
    return (jnp.stack(outputs), jnp.stack(coefs), jnp.stack(norm_list))
```

```python
import functools

import jax
import jax.numpy as jnp
from jax import lax
from jax.experimental import pallas as pl
from jax.experimental.pallas import tpu as pltpu
from jax.sharding import PartitionSpec as P

viscosity = 0.5
time_step = 0.3
cancel_limit = 0.01
f32 = jnp.float32
bf16 = jnp.bfloat16
MESH = pl.DeviceIdType.MESH
HIGHEST = lax.Precision.HIGHEST


def spans(slab, rim):
    found = {}
    reach = -(-rim // slab)
    for d in range(1, reach + 1):
        width = min(slab, rim - (d - 1) * slab)
        found[-d] = (slab - width, slab)
        found[d] = (0, width)
    return found


def gram_blocks(krylov, lanes):
    blocks = max(lanes // krylov, 1)
    return (blocks, krylov // blocks) if krylov % (8 * blocks) == 0 else (1, krylov)


def stage(src, old, dst, snap, step, coupling, lo, hi, keep, gain):
    rows, lanes = src.shape[2], src.shape[3]
    row = lax.broadcasted_iota(jnp.int32, (rows, lanes), 0)
    first = row == 0
    last = row == rows - 1
    step_gain = time_step * gain
    mix = [[coupling[k, j] for j in range(5)] for k in range(5)]

    def body(i, carry):
        p = lo + i
        base = [snap[step, n, p].astype(f32) for n in range(4)]
        half = [(0.5 * step_gain) * base[n] for n in range(3)]
        edge = viscosity * step_gain
        x_up, x_low = edge - half[0], edge + half[0]
        y_up = jnp.where(last, 0.0, edge - half[1])
        y_low = jnp.where(first, 0.0, edge + half[1])
        z_up, z_low = edge - half[2], edge + half[2]
        pull = step_gain * base[3]
        center = [src[k, p] for k in range(5)]
        own = gain - 6.0 * viscosity * step_gain
        for k in range(5):
            q = center[k]
            coupled = mix[k][0] * center[0]
            for j in range(1, 5):
                coupled = coupled + mix[k][j] * center[j]
            total = own * q - pull * coupled
            total = total + (x_up * src[k, p + 1] + x_low * src[k, p - 1])
            total = total + (y_up * pltpu.roll(q, rows - 1, 0) + y_low * pltpu.roll(q, 1, 0))
            total = total + (z_up * pltpu.roll(q, lanes - 1, 1) + z_low * pltpu.roll(q, 1, 1))
            if keep:
                total = total + keep * old[k, p]
            dst[k, p] = total
        return carry

    lax.fori_loop(0, hi - lo, body, 0, unroll=4)


def kernel(
    groups, tiles, coupling_in, basis, snapshots,
    left_out, coef_out, square_out, margin_out,
    coupling, held, plain, start, snap, state, one, two, left, cross, rows_k, spread,
    gram_send, gram_all, coef_send, coef_all, margin_send, margin_all, coefs, square_row, margin_row,
    load_sem, start_send, start_recv, snap_send, snap_recv,
    share_send, share_recv, margin_ssem, margin_rsem, out_sem, ready,
):
    g = lax.axis_index("grp")
    t = lax.axis_index("tile")
    krylov, parts, slab, ny, nz = basis.shape
    local = snapshots.shape[0]
    steps = local * groups
    rim = 3 * steps
    planes = slab + 2 * rim
    near = spans(slab, rim)
    offsets = sorted(near)
    position = krylov - groups + g
    levels = [b for b in range(tiles.bit_length() - 1) if (1 << b) in offsets]
    stride = 1 << len(levels)
    length = tiles // stride
    link = t // stride

    def at(group, offset):
        return {"grp": group, "tile": lax.rem(t + (offset % tiles), tiles)}

    def flipped(level):
        bit = 1 << level
        return {"grp": g, "tile": t + bit - 2 * bit * lax.rem(t // bit, 2)}

    def partner(other):
        return {"grp": lax.rem(g + other, groups), "tile": t}

    barrier = pltpu.get_barrier_semaphore()
    greeted = [at(g, -d) for d in offsets] + [partner(other) for other in range(1, groups)]
    if length > 1:
        greeted += [at(g, stride), at(g, -stride)]
    for peer in greeted:
        pl.semaphore_signal(barrier, inc=1, device_id=peer, device_id_type=MESH)

    chunk = 8 if krylov % 8 == 0 else 1
    loads = []
    own = pltpu.make_async_copy(basis.at[position], start.at[:, pl.ds(rim, slab)], load_sem.at[0])
    own.start()
    mix = pltpu.make_async_copy(coupling_in, coupling, load_sem.at[1])
    mix.start()
    for n in range(krylov // chunk):
        part = pl.ds(n * chunk, chunk)
        copy = pltpu.make_async_copy(basis.at[part], held.at[part], load_sem.at[2 + n])
        copy.start()
        loads.append(copy)

    def target(d, first, last):
        return pl.ds(rim + d * slab + first, last - first)

    start_copies = []
    for n, d in enumerate(offsets):
        first, last = near[d]
        start_copies.append(
            pltpu.make_async_remote_copy(
                src_ref=basis.at[position, :, pl.ds(first, last - first)],
                dst_ref=start.at[:, target(d, first, last)],
                send_sem=start_send.at[n],
                recv_sem=start_recv.at[n],
                device_id=at(g, -d),
                device_id_type=MESH,
            )
        )

    def snap_copy(s, n, d, other):
        first, last = (0, slab) if d == 0 else spans(slab, rim - 3 * s - 1)[d]
        return pltpu.make_async_remote_copy(
            src_ref=snapshots.at[s % local, :, pl.ds(first, last - first)],
            dst_ref=snap.at[s, :, target(d, first, last)],
            send_sem=snap_send.at[s % local, other, n],
            recv_sem=snap_recv.at[s, n],
            device_id=at(lax.rem(g + other, groups), -d),
            device_id_type=MESH,
        )

    def local_snap(s):
        return pltpu.make_async_copy(
            snapshots.at[s % local], snap.at[s, :, pl.ds(rim, slab)], load_sem.at[2 + krylov // chunk + s % local]
        )

    def snap_offsets(s):
        inside = spans(slab, rim - 3 * s - 1)
        return [(n, d) for n, d in enumerate([0] + offsets) if d == 0 or d in inside]

    def send_snap(s):
        @pl.when(g == s // local)
        def _():
            for n, d in snap_offsets(s):
                for other in range(1 if d else groups):
                    if d or other:
                        snap_copy(s, n, d, other).start()

    def relay_copy(s, n, d, other):
        first, last = spans(slab, rim - 3 * s - 1)[d]
        cells = snap.at[s, :, target(d, first, last)]
        return pltpu.make_async_remote_copy(
            src_ref=cells,
            dst_ref=cells,
            send_sem=snap_send.at[s % local, other, n],
            recv_sem=snap_recv.at[s, n],
            device_id=at(lax.rem(g + other, groups), 0),
            device_id_type=MESH,
        )

    def relay(s):
        @pl.when(g == s // local)
        def _():
            for n, d in snap_offsets(s):
                if d:
                    snap_copy(s, n, d, 0).wait_recv()
                    for other in range(1, groups):
                        relay_copy(s, n, d, other).start()
            local_snap(s).wait()

    def receive(s):
        if groups > 1:
            @pl.when(g != s // local)
            def _():
                snap_copy(s, 0, 0, 1).wait_recv()
                for n, d in snap_offsets(s):
                    if d:
                        relay_copy(s, n, d, 1).wait_recv()

    for s in range(steps):
        @pl.when(g == s // local)
        def _():
            local_snap(s).start()

    pl.semaphore_wait(barrier, len(greeted))
    for s in range(local):
        send_snap(s)
    for copy in start_copies:
        copy.start()
    for s in range(local, steps):
        send_snap(s)

    def tell(n, peer):
        pl.semaphore_signal(ready.at[n], inc=1, device_id=peer, device_id_type=MESH)

    def flip_step(n):
        if n:
            pl.semaphore_wait(ready.at[n - 1], 1)
        if n < len(levels):
            tell(n, flipped(levels[n]))

    def pass_on(sem, way):
        head = link == (0 if way > 0 else length - 1)
        tail = link == (length - 1 if way > 0 else 0)

        @pl.when(jnp.logical_not(head))
        def _():
            pl.semaphore_wait(ready.at[sem], 1)

        @pl.when(jnp.logical_not(tail))
        def _():
            tell(sem, at(g, way * stride))

    def chain_step(n):
        if length > 1:
            upper = link >= length // 2
            for way in (1, -1):
                @pl.when(upper == (way < 0))
                def _():
                    mine = -way if n else way
                    pass_on(len(levels) + (mine < 0), mine)

    pending = [functools.partial(flip_step, n) for n in range(len(levels) + 1)]
    pending += [functools.partial(chain_step, n) for n in range(2)]
    pending.pop(0)()

    def advance():
        if pending:
            pending.pop(0)()

    for copy in loads:
        copy.wait()
    size = krylov * ny
    for c in range(parts):
        wide = jnp.concatenate([held[:, c, x].reshape(size, nz) for x in range(slab)], axis=1)
        piece = lax.dot_general(wide, wide, (((1,), (1,)), ((), ())), preferred_element_type=f32)
        cross[...] = cross[...] + piece if c else piece
        advance()
    line = lax.broadcasted_iota(jnp.int32, (size, size), 0)
    column = lax.broadcasted_iota(jnp.int32, (size, size), 1)
    kept = jnp.where(lax.rem(line, ny) == lax.rem(column, ny), cross[...], 0.0)
    kept = jnp.sum(kept.reshape(krylov, ny, size), axis=1)
    pick = (
        lax.broadcasted_iota(jnp.int32, (size, krylov), 0) // ny
        == lax.broadcasted_iota(jnp.int32, (size, krylov), 1)
    ).astype(f32)
    gram = jnp.dot(kept, pick, precision=HIGHEST, preferred_element_type=f32)
    blocks, height = gram_blocks(krylov, nz)
    gram_send[...] = jnp.concatenate(
        [gram[n * height : (n + 1) * height] for n in range(blocks)], axis=1
    )
    while pending:
        advance()

    def spread_out(n, send, everyone):
        way = 2 * (t // max(tiles // 2, 1)) - 1
        others = everyone.at[pl.ds(0, tiles - 1)]

        def begin():
            def one(i, carry):
                peer = lax.rem(2 * tiles - 1 - t + way * i, tiles)

                @pl.when(peer != t)
                def _():
                    pltpu.make_async_remote_copy(
                        src_ref=send,
                        dst_ref=everyone.at[t],
                        send_sem=share_send.at[n],
                        recv_sem=share_recv.at[n],
                        device_id={"grp": g, "tile": peer},
                        device_id_type=MESH,
                    ).start()

                return carry

            lax.fori_loop(0, tiles, one, 0)
            everyone[t] = send[...]

        def arrive():
            pltpu.make_async_copy(others, others, share_recv.at[n]).wait()

        def drain():
            pltpu.make_async_copy(others, others, share_send.at[n]).wait()

        return begin, arrive, drain

    gram_begin, gram_arrive, gram_drain = spread_out(0, gram_send, gram_all)
    coef_begin, coef_arrive, coef_drain = spread_out(1, coef_send, coef_all)
    gram_begin()

    def expand(k, carry):
        plain[k] = held[k].astype(f32)
        return carry

    lax.fori_loop(0, krylov, expand, 0)

    relay(0)
    own.wait()
    for copy in start_copies:
        copy.wait_recv()
    mix.wait()

    def widen(p, carry):
        for k in range(parts):
            state[k, p] = start[k, p].astype(f32)
        return carry

    lax.fori_loop(0, planes, widen, 0)
    lo, hi = 0, planes
    for s in range(steps):
        receive(s)
        stage(state, state, one, snap, s, coupling, lo + 1, hi - 1, 0.0, 1.0)
        if s == 0:
            for later in range(1, steps):
                relay(later)
        stage(one, state, two, snap, s, coupling, lo + 2, hi - 2, 0.75, 0.25)
        stage(two, state, state, snap, s, coupling, lo + 3, hi - 3, 1.0 / 3.0, 2.0 / 3.0)
        lo, hi = lo + 3, hi - 3

    count = f32(parts * slab * ny * nz * tiles)

    group = 4 if krylov % 4 == 0 else 1

    def project(i, carry):
        totals = [jnp.zeros((ny, nz), f32) for _ in range(group)]
        for c in range(parts):
            for x in range(slab):
                field = state[c, rim + x]
                for n in range(group):
                    totals[n] = totals[n] + plain[i * group + n, c, x] * field
        for n in range(group):
            rows_k[pl.ds(i * group + n, 1), :] = jnp.sum(totals[n], axis=0, keepdims=True)
        return carry

    lax.fori_loop(0, krylov // group, project, 0)
    ones = jnp.ones((8, nz), f32)
    inner = lax.dot_general(
        ones, rows_k[...], (((1,), (1,)), ((), ())), precision=HIGHEST, preferred_element_type=f32
    )
    own_square = jnp.zeros((ny, nz), f32)
    for c in range(parts):
        for x in range(slab):
            own_square = own_square + state[c, rim + x] * state[c, rim + x]
    own_square = jnp.sum(jnp.sum(own_square, axis=0, keepdims=True), axis=1, keepdims=True)
    coef_send[...] = jnp.concatenate(
        [inner[0:1], jnp.broadcast_to(own_square, (1, coef_send.shape[1] - krylov))], axis=1
    )
    coef_begin()
    for copy in start_copies:
        copy.wait_send()
    for s in range(steps):
        @pl.when(g == s // local)
        def _():
            for n, d in snap_offsets(s):
                for other in range(groups):
                    if d and other:
                        relay_copy(s, n, d, other).wait_send()
                    elif d or other:
                        snap_copy(s, n, d, other).wait_send()
    gram_drain()
    gram_arrive()
    packed = jnp.sum(gram_all[...], axis=0) / count
    gram = jnp.concatenate(
        [packed[:, n * krylov : (n + 1) * krylov] for n in range(blocks)], axis=0
    )
    same = lax.broadcasted_iota(jnp.int32, gram.shape, 0) == lax.broadcasted_iota(jnp.int32, gram.shape, 1)
    times = functools.partial(jnp.dot, precision=HIGHEST, preferred_element_type=f32)
    twice = jnp.where(same, 2.0, 0.0) - gram
    both = jnp.concatenate([twice, times(twice, gram)], axis=1)
    coef_arrive()
    sums = jnp.sum(coef_all[...], axis=0) / count
    first_row = jnp.broadcast_to(sums, (8, sums.shape[1]))
    work_square = first_row[:, krylov : krylov + 1]
    first_row = first_row[:, :krylov]
    mixed = times(first_row, both)
    every, turned = mixed[:, :krylov], mixed[:, krylov:]
    for k in range(krylov):
        spread[k] = jnp.broadcast_to(every[:, k : k + 1], (8, nz))
    linear = 2.0 * every * first_row
    bent = every * turned
    bound = 2.0 * jnp.abs(every * first_row) + jnp.abs(every) * times(jnp.abs(every), jnp.abs(gram))
    square = work_square + jnp.sum(bent - linear, axis=1, keepdims=True)
    bound = work_square + jnp.sum(bound, axis=1, keepdims=True)
    margin = square - cancel_limit * bound
    margin_send[...] = jnp.broadcast_to(margin[0:1], margin_send.shape)

    def margin_copy(other, sender):
        return pltpu.make_async_remote_copy(
            src_ref=margin_send,
            dst_ref=margin_all.at[sender],
            send_sem=margin_ssem.at[other],
            recv_sem=margin_rsem.at[other],
            device_id=partner(other),
            device_id_type=MESH,
        )

    for other in range(1, groups):
        margin_copy(other, g).start()
    margin_all[g] = margin_send[...]

    square_row[...] = jnp.broadcast_to(square[0:1], square_row.shape)
    coefs[...] = every[0:1]
    outs = [
        pltpu.make_async_copy(coefs, coef_out, out_sem.at[0]),
        pltpu.make_async_copy(square_row, square_out, out_sem.at[1]),
    ]
    for copy in outs:
        copy.start()
    for x in range(slab):
        removed = [jnp.zeros((ny // 8, 8, nz), f32) for _ in range(parts)]
        for k in range(krylov):
            factor = spread[k][None]
            for c in range(parts):
                removed[c] = removed[c] + factor * plain[k, c, x].reshape(ny // 8, 8, nz)
        for c in range(parts):
            left[c, x] = state[c, rim + x] - removed[c].reshape(ny, nz)
        copy = pltpu.make_async_copy(left.at[:, x], left_out.at[0, :, x], out_sem.at[3 + x])
        copy.start()
        outs.append(copy)
    for other in range(1, groups):
        margin_copy(other, lax.rem(g - other + groups, groups)).wait_recv()
    margin_row[...] = jnp.min(margin_all[...], axis=0)
    copy = pltpu.make_async_copy(margin_row, margin_out, out_sem.at[2])
    copy.start()
    outs.append(copy)
    coef_drain()
    for other in range(1, groups):
        margin_copy(other, g).wait_send()
    for copy in outs:
        copy.wait()


def square_kernel(tiles, left, square_out, send, everyone, ssem, rsem):
    g = lax.axis_index("grp")
    t = lax.axis_index("tile")
    _, parts, slab, ny, nz = left.shape
    barrier = pltpu.get_barrier_semaphore()

    def peer(r):
        return {"grp": g, "tile": lax.rem(t + r, tiles)}

    def greet(r, carry):
        pl.semaphore_signal(barrier, inc=1, device_id=peer(r), device_id_type=MESH)
        return carry

    lax.fori_loop(1, tiles, greet, 0)
    pl.semaphore_wait(barrier, tiles - 1)
    total = jnp.zeros((ny, nz), f32)
    for c in range(parts):
        for x in range(slab):
            total = total + left[0, c, x] * left[0, c, x]
    send[...] = jnp.sum(total, axis=0, keepdims=True)

    def copy(r, sender):
        return pltpu.make_async_remote_copy(
            src_ref=send,
            dst_ref=everyone.at[sender],
            send_sem=ssem.at[r],
            recv_sem=rsem.at[r],
            device_id=peer(r),
            device_id_type=MESH,
        )

    lax.fori_loop(1, tiles, lambda r, c: (copy(r, t).start(), c)[1], 0)
    everyone[t] = send[...]
    lax.fori_loop(
        1, tiles, lambda r, c: (copy(r, lax.rem(t - r + tiles, tiles)).wait_recv(), c)[1], 0
    )
    count = f32(parts * slab * ny * nz * tiles)
    square = jnp.sum(jnp.sum(everyone[...], axis=0), axis=1, keepdims=True) / count
    square_out[...] = jnp.broadcast_to(square, square_out.shape)
    lax.fori_loop(1, tiles, lambda r, c: (copy(r, t).wait_send(), c)[1], 0)


def finish(left, coefs, square, out, coef_out, norm_out, held, row, norm_row, line, sem):
    loads = [
        pltpu.make_async_copy(square, row, sem.at[0]),
        pltpu.make_async_copy(left, held, sem.at[1]),
        pltpu.make_async_copy(coefs, line, sem.at[2]),
    ]
    for copy in loads:
        copy.start()
    loads[0].wait()
    norm = jnp.sqrt(row[...])
    norm_row[...] = norm
    loads[2].wait()
    stores = [
        pltpu.make_async_copy(norm_row, norm_out, sem.at[0]),
        pltpu.make_async_copy(line, coef_out, sem.at[2]),
    ]
    for copy in stores:
        copy.start()
    inverse = jnp.broadcast_to(1.0 / norm, left.shape[3:])
    loads[1].wait()
    for c in range(left.shape[1]):
        for x in range(left.shape[2]):
            held[0, c, x] = held[0, c, x] * inverse
    last = pltpu.make_async_copy(held, out, sem.at[1])
    last.start()
    for copy in stores:
        copy.wait()
    last.wait()


def on_device(groups, tiles, basis, snapshots, coupling):
    krylov, parts, slab, ny, nz = basis.shape
    local, fields = snapshots.shape[:2]
    steps = local * groups
    rim = 3 * steps
    planes = slab + 2 * rim
    count = len(spans(slab, rim))
    blocks, height = gram_blocks(krylov, nz)
    width = -(-(krylov + 1) // nz) * nz
    dma = pltpu.SemaphoreType.DMA
    field = pltpu.VMEM((parts, planes, ny, nz), f32)
    whole = pl.BlockSpec(memory_space=pltpu.VMEM)
    anywhere = pl.BlockSpec(memory_space=pl.ANY)
    results = pl.pallas_call(
        functools.partial(kernel, groups, tiles),
        name="propagate",
        out_shape=(
            jax.ShapeDtypeStruct((1, parts, slab, ny, nz), f32),
            jax.ShapeDtypeStruct((1, krylov), f32),
            jax.ShapeDtypeStruct((1, nz), f32),
            jax.ShapeDtypeStruct((1, nz), f32),
        ),
        in_specs=[anywhere] * 3,
        out_specs=(anywhere,) * 4,
        scratch_shapes=[
            pltpu.SMEM(coupling.shape, f32),
            pltpu.VMEM(basis.shape, bf16),
            pltpu.VMEM(basis.shape, f32),
            pltpu.VMEM((parts, planes, ny, nz), bf16),
            pltpu.VMEM((steps, fields, planes, ny, nz), bf16),
            field,
            field,
            field,
            pltpu.VMEM((parts, slab, ny, nz), f32),
            pltpu.VMEM((krylov * ny, krylov * ny), f32),
            pltpu.VMEM((krylov, nz), f32),
            pltpu.VMEM((krylov, 8, nz), f32),
            pltpu.VMEM((height, blocks * krylov), f32),
            pltpu.VMEM((tiles, height, blocks * krylov), f32),
            pltpu.VMEM((1, width), f32),
            pltpu.VMEM((tiles, 1, width), f32),
            pltpu.VMEM((1, nz), f32),
            pltpu.VMEM((groups, 1, nz), f32),
            pltpu.VMEM((1, krylov), f32),
            pltpu.VMEM((1, nz), f32),
            pltpu.VMEM((1, nz), f32),
            dma((2 + (krylov // 8 if krylov % 8 == 0 else krylov) + local,)),
            dma((count,)),
            dma((count,)),
            dma((local, groups, count + 1)),
            dma((steps, count + 1)),
            dma((2,)),
            dma((2,)),
            dma((groups,)),
            dma((groups,)),
            dma((slab + 3,)),
            pltpu.SemaphoreType.REGULAR((tiles.bit_length() + 2,)),
        ],
        compiler_params=pltpu.CompilerParams(
            collective_id=0, has_side_effects=True, vmem_limit_bytes=67043328
        ),
    )(coupling, basis, snapshots)
    left, coefs, square, margin = results

    def scaled(left, coefs, square):
        return pl.pallas_call(
            finish,
            name="finish",
            out_shape=tuple(jax.ShapeDtypeStruct(a.shape, f32) for a in (left, coefs, square)),
            in_specs=[anywhere] * 3,
            out_specs=(anywhere,) * 3,
            scratch_shapes=[
                pltpu.VMEM(left.shape, f32),
                pltpu.VMEM(square.shape, f32),
                pltpu.VMEM(square.shape, f32),
                pltpu.VMEM(coefs.shape, f32),
                dma((3,)),
            ],
        )(left, coefs, square)

    def summed(left, coefs, square):
        exact = pl.pallas_call(
            functools.partial(square_kernel, tiles),
            name="exact_square",
            out_shape=jax.ShapeDtypeStruct((1, nz), f32),
            in_specs=[whole],
            out_specs=whole,
            scratch_shapes=[
                pltpu.VMEM((1, nz), f32),
                pltpu.VMEM((tiles, 1, nz), f32),
                dma((tiles,)),
                dma((tiles,)),
            ],
            compiler_params=pltpu.CompilerParams(collective_id=1, has_side_effects=True),
        )(left)
        return scaled(left, coefs, exact)

    new_vector, coefs, norms = lax.cond(margin[0, 0] > 0.0, scaled, summed, left, coefs, square)
    return new_vector, coefs, norms[0, :1]


def solution(mesh):
    placed = (P(None, None, "tile", None, None), P("grp", None, "tile", None, None), P())
    return jax.shard_map(
        functools.partial(on_device, mesh.shape["grp"], mesh.shape["tile"]),
        mesh=mesh,
        in_specs=placed,
        out_specs=(P("grp", None, "tile", None, None), P("grp", None), P("grp")),
        check_vma=False,
    )
```

```python
import functools

import jax
import jax.numpy as jnp
from jax import lax
from jax.experimental import pallas as pl
from jax.experimental.pallas import tpu as pltpu
from jax.sharding import PartitionSpec as P

viscosity = 0.5
time_step = 0.3
cancel_limit = 0.01
f32 = jnp.float32
bf16 = jnp.bfloat16
MESH = pl.DeviceIdType.MESH
HIGHEST = lax.Precision.HIGHEST


def spans(slab, rim):
    found = {}
    reach = -(-rim // slab)
    for d in range(1, reach + 1):
        width = min(slab, rim - (d - 1) * slab)
        found[-d] = (slab - width, slab)
        found[d] = (0, width)
    return found


def gram_blocks(krylov, lanes):
    blocks = max(lanes // krylov, 1)
    return (blocks, krylov // blocks) if krylov % (8 * blocks) == 0 else (1, krylov)


def stage(src, old, dst, snap, step, coupling, first_planes, planes, keep, gain):
    rows, lanes = src.shape[2], src.shape[3]
    row = lax.broadcasted_iota(jnp.int32, (rows, lanes), 0)
    top = row == 0
    last = row == rows - 1
    step_gain = time_step * gain
    mix = [[coupling[k, j] for j in range(5)] for k in range(5)]

    def one_plane(p):
        base = [snap[step, n, p].astype(f32) for n in range(4)]
        half = [(0.5 * step_gain) * base[n] for n in range(3)]
        edge = viscosity * step_gain
        x_up, x_low = edge - half[0], edge + half[0]
        y_up = jnp.where(last, 0.0, edge - half[1])
        y_low = jnp.where(top, 0.0, edge + half[1])
        z_up, z_low = edge - half[2], edge + half[2]
        pull = step_gain * base[3]
        center = [src[k, p] for k in range(5)]
        own = gain - 6.0 * viscosity * step_gain
        for k in range(5):
            q = center[k]
            coupled = mix[k][0] * center[0]
            for j in range(1, 5):
                coupled = coupled + mix[k][j] * center[j]
            total = own * q - pull * coupled
            total = total + (x_up * src[k, p + 1] + x_low * src[k, p - 1])
            total = total + (y_up * pltpu.roll(q, rows - 1, 0) + y_low * pltpu.roll(q, 1, 0))
            total = total + (z_up * pltpu.roll(q, lanes - 1, 1) + z_low * pltpu.roll(q, 1, 1))
            if keep:
                total = total + keep * old[k, p]
            dst[k, p] = total

    def body(i, carry):
        for lo in first_planes:
            one_plane(lo + i)
        return carry

    unroll = max(n for n in range(1, 6) if planes % n == 0)
    lax.fori_loop(0, planes, body, 0, unroll=unroll)


def kernel(
    groups, tiles, coupling_in, basis, snapshots,
    left_out, coef_out, square_out, margin_out,
    coupling, held, plain, start, snap, state, one, two, left, cross, rows_k, spread,
    gram_send, gram_all, coef_send, coef_all, margin_send, margin_all, coefs, square_row, margin_row,
    load_sem, start_send, start_recv, snap_send, relay_send, snap_recv,
    share_send, share_recv, margin_ssem, margin_rsem, out_sem, ready,
):
    g = lax.axis_index("grp")
    t = lax.axis_index("tile")
    krylov, parts, slab, ny, nz = basis.shape
    local = snapshots.shape[0]
    steps = local * groups
    rim = 3 * steps
    planes = slab + 2 * rim
    near = spans(slab, rim)
    offsets = sorted(near)
    position = krylov - groups + g
    levels = [b for b in range(tiles.bit_length() - 1) if (1 << b) in offsets]
    stride = 1 << len(levels)
    length = tiles // stride
    link = t // stride

    def at(group, offset):
        return {"grp": group, "tile": lax.rem(t + (offset % tiles), tiles)}

    def flipped(level):
        bit = 1 << level
        return {"grp": g, "tile": t + bit - 2 * bit * lax.rem(t // bit, 2)}

    def partner(other):
        return {"grp": lax.rem(g + other, groups), "tile": t}

    barrier = pltpu.get_barrier_semaphore()
    def crosses(d):
        return t + d >= tiles if d > 0 else t + d < 0

    def greet(peer):
        pl.semaphore_signal(barrier, inc=1, device_id=peer, device_id_type=MESH)

    greeters = groups - 1
    for d in sorted(offsets, key=abs, reverse=True):
        if d > 0:
            greet(at(g, -d))
            greeters = greeters + 1
        else:
            pl.when(jnp.logical_not(crosses(-d)))(functools.partial(greet, at(g, -d)))
            greeters = greeters + jnp.where(crosses(d), 0, 1)
    for other in range(1, groups):
        greet(partner(other))
    for way in (1, -1):
        last = link == (length - 1 if way > 0 else 0)
        greeters = greeters + jnp.where(last, 0, 1)

        @pl.when(jnp.logical_not(last))
        def _():
            greet(at(g, way * stride))

    chunk = 8 if krylov % 8 == 0 else 1
    own = pltpu.make_async_copy(basis.at[position], start.at[:, pl.ds(rim, slab)], load_sem.at[0])
    own.start()
    mix = pltpu.make_async_copy(coupling_in, coupling, load_sem.at[1])
    mix.start()
    for n in range(krylov // chunk):
        part = pl.ds(n * chunk, chunk)
        pltpu.make_async_copy(basis.at[part], held.at[part], load_sem.at[2]).start()

    def target(d, first, last):
        return pl.ds(rim + d * slab + first, last - first)

    start_copies = []
    for n, d in enumerate(offsets):
        first, last = near[d]
        start_copies.append(
            pltpu.make_async_remote_copy(
                src_ref=basis.at[position, :, pl.ds(first, last - first)],
                dst_ref=start.at[:, target(d, first, last)],
                send_sem=start_send.at[0],
                recv_sem=start_recv.at[n],
                device_id=at(g, -d),
                device_id_type=MESH,
            )
        )

    def snap_copy(s, n, d, other):
        first, last = (0, slab) if d == 0 else spans(slab, rim - 3 * s - 1)[d]
        return pltpu.make_async_remote_copy(
            src_ref=snapshots.at[s % local, :, pl.ds(first, last - first)],
            dst_ref=snap.at[s, :, target(d, first, last)],
            send_sem=snap_send.at[s % local],
            recv_sem=snap_recv.at[s, n],
            device_id=at(lax.rem(g + other, groups), -d),
            device_id_type=MESH,
        )

    def local_snap(s):
        return pltpu.make_async_copy(
            snapshots.at[s % local], snap.at[s, :, pl.ds(rim, slab)], load_sem.at[3 + s % local]
        )

    def snap_offsets(s):
        inside = spans(slab, rim - 3 * s - 1)
        return [(n, d) for n, d in enumerate([0] + offsets) if d == 0 or d in inside]

    def snap_each(s, ds, act):
        inside = {d: n for n, d in snap_offsets(s)}

        @pl.when(g == s // local)
        def _():
            for d in ds:
                if d in inside:
                    for other in range(1 if d else groups):
                        if d or other:
                            act(snap_copy(s, inside[d], d, other))

    def relay_copy(s, n, d, other):
        first, last = spans(slab, rim - 3 * s - 1)[d]
        cells = snap.at[s, :, target(d, first, last)]
        return pltpu.make_async_remote_copy(
            src_ref=cells,
            dst_ref=cells,
            send_sem=relay_send.at[s % local],
            recv_sem=snap_recv.at[s, n],
            device_id=at(lax.rem(g + other, groups), 0),
            device_id_type=MESH,
        )

    def relay(s, ds):
        @pl.when(g == s // local)
        def _():
            for n, d in snap_offsets(s):
                if d and d in ds:
                    snap_copy(s, n, d, 0).wait_recv()
                    for other in range(1, groups):
                        relay_copy(s, n, d, other).start()
            if 0 in ds:
                local_snap(s).wait()

    def receive(s, ds):
        if groups > 1:
            @pl.when(g != s // local)
            def _():
                for n, d in snap_offsets(s):
                    if d in ds:
                        (relay_copy if d else snap_copy)(s, n, d, 1).wait_recv()

    for s in range(steps):
        @pl.when(g == s // local)
        def _():
            local_snap(s).start()

    pl.semaphore_wait(barrier, greeters)
    def send(s, ds):
        snap_each(s, ds, lambda copy: copy.start())
        if s == 0:
            for d in ds:
                if d:
                    start_copies[offsets.index(d)].start()

    def tell(n, peer):
        pl.semaphore_signal(ready.at[n], inc=1, device_id=peer, device_id_type=MESH)

    edge = len(levels) + 3

    for d in offsets:
        if d < 0:
            pl.when(crosses(-d))(functools.partial(tell, edge - d - 1, at(g, -d)))
    upper = t >= tiles // 2
    ahead = [d for d in offsets if d < 0]
    back = [-d for d in ahead]

    def send_near(s):
        if s == 0:
            snap_each(0, [0], lambda copy: copy.start())
        else:
            snap_each(s, [0], lambda copy: copy.start())
        for d in sorted(offsets, key=abs):
            if d < 0:
                send(s, [d])
            else:
                pl.when(jnp.logical_not(crosses(-d)))(functools.partial(send, s, [d]))

    def send_late():
        for d in sorted(back):
            @pl.when(crosses(-d))
            def _():
                pl.semaphore_wait(ready.at[edge + d - 1], 1)
                send(0, [d])
                for s in range(1, steps):
                    send(s, [d])

    for s in range(steps):
        send_near(s)

    def flip_step(n):
        if n:
            pl.semaphore_wait(ready.at[n - 1], 1)
        if n < len(levels):
            tell(n, flipped(levels[n]))

    def pass_on(sem, way):
        head = link == (0 if way > 0 else length - 1)
        tail = link == (length - 1 if way > 0 else 0)

        @pl.when(jnp.logical_not(head))
        def _():
            pl.semaphore_wait(ready.at[sem], 1)

        @pl.when(jnp.logical_not(tail))
        def _():
            tell(sem, at(g, way * stride))

    def chain_step(n):
        if length > 1:
            upper = link >= length // 2
            for way in (1, -1):
                @pl.when(upper == (way < 0))
                def _():
                    mine = -way if n else way
                    pass_on(len(levels) + (mine < 0), mine)

    def tell_group():
        for other in range(1, groups):
            tell(len(levels) + 2, partner(other))

    pending = [functools.partial(flip_step, n) for n in range(len(levels) + 1)]
    pending += [functools.partial(chain_step, n) for n in range(2)] + [tell_group]

    def advance():
        if pending:
            pl.when(g == groups - 1)(pending.pop(0))

    def all_ready():
        while pending:
            advance()
        if groups > 1:
            @pl.when(g != groups - 1)
            def _():
                pl.semaphore_wait(ready.at[len(levels) + 2], 1)

    advance()
    pltpu.make_async_copy(basis, held, load_sem.at[2]).wait()
    size = krylov * ny
    for c in range(parts):
        wide = jnp.concatenate([held[:, c, x].reshape(size, nz) for x in range(slab)], axis=1)
        piece = lax.dot_general(wide, wide, (((1,), (1,)), ((), ())), preferred_element_type=f32)
        cross[...] = cross[...] + piece if c else piece
        if c == min(3, parts - 1):
            send_late()
        advance()
    line = lax.broadcasted_iota(jnp.int32, (size, size), 0)
    column = lax.broadcasted_iota(jnp.int32, (size, size), 1)
    kept = jnp.where(lax.rem(line, ny) == lax.rem(column, ny), cross[...], 0.0)
    kept = jnp.sum(kept.reshape(krylov, ny, size), axis=1)
    pick = (
        lax.broadcasted_iota(jnp.int32, (size, krylov), 0) // ny
        == lax.broadcasted_iota(jnp.int32, (size, krylov), 1)
    ).astype(f32)
    gram = jnp.dot(kept, pick, precision=HIGHEST, preferred_element_type=f32)
    blocks, height = gram_blocks(krylov, nz)
    gram_send[...] = jnp.concatenate(
        [gram[n * height : (n + 1) * height] for n in range(blocks)], axis=1
    )
    def spread_out(n, send, everyone):
        way = 2 * (t // max(tiles // 2, 1)) - 1
        others = everyone.at[pl.ds(0, tiles - 1)]

        def begin():
            def one(i, carry):
                peer = lax.rem(2 * tiles - 1 - t + way * i, tiles)

                @pl.when(peer != t)
                def _():
                    pltpu.make_async_remote_copy(
                        src_ref=send,
                        dst_ref=everyone.at[t],
                        send_sem=share_send.at[n],
                        recv_sem=share_recv.at[n],
                        device_id={"grp": g, "tile": peer},
                        device_id_type=MESH,
                    ).start()

                return carry

            lax.fori_loop(0, tiles, one, 0)
            everyone[t] = send[...]

        def arrive():
            pltpu.make_async_copy(others, others, share_recv.at[n]).wait()

        def drain():
            pltpu.make_async_copy(others, others, share_send.at[n]).wait()

        return begin, arrive, drain

    gram_begin, gram_arrive, gram_drain = spread_out(0, gram_send, gram_all)
    coef_begin, coef_arrive, coef_drain = spread_out(1, coef_send, coef_all)

    def expand(k, carry):
        plain[k] = held[k].astype(f32)
        return carry

    lax.fori_loop(0, krylov, expand, 0)

    def widen(d):
        def one(p, carry):
            for k in range(parts):
                state[k, p] = start[k, p].astype(f32)
            return carry

        lo, width = (rim, slab) if d == 0 else (rim + d * slab + near[d][0], near[d][1] - near[d][0])
        lax.fori_loop(lo, lo + width, one, 0)

    def arrive(ds):
        for d in ds:
            if d:
                start_copies[offsets.index(d)].wait_recv()
            else:
                own.wait()
                mix.wait()
            widen(d)

    weights = ((0.0, 1.0), (0.75, 0.25), (1.0 / 3.0, 2.0 / 3.0))
    ways = ((state, one), (one, two), (two, state))

    def march(s, known, new):
        for n, (src, dst) in enumerate(ways):
            k = 3 * s + n + 1
            lo, hi = max(k, known - k), new - k
            if hi > lo:
                first = jnp.where(upper, lo, planes - hi)
                stage(src, state, dst, snap, s, coupling, [first], hi - lo, *weights[n])

    def sided(act, *ds):
        for way, on in ((1, upper), (-1, jnp.logical_not(upper))):
            @pl.when(on)
            def _():
                act([way * d for d in ds])

    near_ds, far_ds = sorted(ahead, key=abs), sorted(back)
    sided(lambda ds: (relay(0, [0] + ds), arrive(ds)), *near_ds)
    arrive([0])
    for s in range(1, steps):
        sided(lambda ds: relay(s, [0] + ds), *near_ds)
    sided(lambda ds: receive(0, [0] + ds), *near_ds)
    known = 0
    for piece in range(len(far_ds) + 1):
        if piece:
            sided(lambda ds: (relay(0, ds), arrive(ds)), far_ds[piece - 1])
            for s in range(1, steps):
                sided(lambda ds: relay(s, ds), far_ds[piece - 1])
            sided(lambda ds: receive(0, ds), far_ds[piece - 1])
        new = rim + slab + sum(near[d][1] - near[d][0] for d in far_ds[:piece])
        for s in range(steps):
            if s:
                sided(lambda ds: receive(s, ds), *(([0] + near_ds) if piece == 0 else far_ds[piece - 1 : piece]))
            march(s, known, new)
        known = new
        if piece == 0:
            all_ready()
            gram_begin()

    count = f32(parts * slab * ny * nz * tiles)

    group = 4 if krylov % 4 == 0 else 1

    def project(i, carry):
        totals = [jnp.zeros((ny, nz), f32) for _ in range(group)]
        for c in range(parts):
            for x in range(slab):
                field = state[c, rim + x]
                for n in range(group):
                    totals[n] = totals[n] + plain[i * group + n, c, x] * field
        for n in range(group):
            rows_k[pl.ds(i * group + n, 1), :] = jnp.sum(totals[n], axis=0, keepdims=True)
        return carry

    lax.fori_loop(0, krylov // group, project, 0)
    ones = jnp.ones((8, nz), f32)
    inner = lax.dot_general(
        ones, rows_k[...], (((1,), (1,)), ((), ())), precision=HIGHEST, preferred_element_type=f32
    )
    own_square = jnp.zeros((ny, nz), f32)
    for c in range(parts):
        for x in range(slab):
            own_square = own_square + state[c, rim + x] * state[c, rim + x]
    own_square = jnp.sum(jnp.sum(own_square, axis=0, keepdims=True), axis=1, keepdims=True)
    coef_send[...] = jnp.concatenate(
        [inner[0:1], jnp.broadcast_to(own_square, (1, coef_send.shape[1] - krylov))], axis=1
    )
    coef_begin()
    def all_sent(cells, sem):
        pltpu.make_async_copy(cells, cells, sem).wait()

    all_sent(start.at[:, pl.ds(0, 2 * rim)], start_send.at[0])
    for s in range(steps):
        around = 2 * (rim - 3 * s - 1)

        @pl.when(g == s // local)
        def _():
            all_sent(snap.at[s, :, pl.ds(0, around)], snap_send.at[s % local])
            for other in range(1, groups):
                all_sent(snap.at[s, :, pl.ds(0, slab)], snap_send.at[s % local])
                all_sent(snap.at[s, :, pl.ds(0, around)], relay_send.at[s % local])

    gram_drain()
    gram_arrive()
    packed = jnp.sum(gram_all[...], axis=0) / count
    gram = jnp.concatenate(
        [packed[:, n * krylov : (n + 1) * krylov] for n in range(blocks)], axis=0
    )
    same = lax.broadcasted_iota(jnp.int32, gram.shape, 0) == lax.broadcasted_iota(jnp.int32, gram.shape, 1)
    times = functools.partial(jnp.dot, precision=HIGHEST, preferred_element_type=f32)
    twice = jnp.where(same, 2.0, 0.0) - gram
    both = jnp.concatenate([twice, times(twice, gram)], axis=1)
    coef_arrive()
    sums = jnp.sum(coef_all[...], axis=0) / count
    first_row = jnp.broadcast_to(sums, (8, sums.shape[1]))
    work_square = first_row[:, krylov : krylov + 1]
    first_row = first_row[:, :krylov]
    mixed = times(first_row, both)
    every, turned = mixed[:, :krylov], mixed[:, krylov:]
    for k in range(krylov):
        spread[k] = jnp.broadcast_to(every[:, k : k + 1], (8, nz))
    linear = 2.0 * every * first_row
    bent = every * turned
    bound = 2.0 * jnp.abs(every * first_row) + jnp.abs(every) * times(jnp.abs(every), jnp.abs(gram))
    square = work_square + jnp.sum(bent - linear, axis=1, keepdims=True)
    bound = work_square + jnp.sum(bound, axis=1, keepdims=True)
    margin = square - cancel_limit * bound
    margin_send[...] = jnp.broadcast_to(margin[0:1], margin_send.shape)

    def margin_copy(other, sender):
        return pltpu.make_async_remote_copy(
            src_ref=margin_send,
            dst_ref=margin_all.at[sender],
            send_sem=margin_ssem.at[other],
            recv_sem=margin_rsem.at[other],
            device_id=partner(other),
            device_id_type=MESH,
        )

    for other in range(1, groups):
        margin_copy(other, g).start()
    margin_all[g] = margin_send[...]

    square_row[...] = jnp.broadcast_to(square[0:1], square_row.shape)
    coefs[...] = every[0:1]
    outs = [
        pltpu.make_async_copy(coefs, coef_out, out_sem.at[0]),
        pltpu.make_async_copy(square_row, square_out, out_sem.at[1]),
    ]
    for copy in outs:
        copy.start()
    for x in range(slab):
        removed = [jnp.zeros((ny // 8, 8, nz), f32) for _ in range(parts)]
        for k in range(krylov):
            factor = spread[k][None]
            for c in range(parts):
                removed[c] = removed[c] + factor * plain[k, c, x].reshape(ny // 8, 8, nz)
        for c in range(parts):
            left[c, x] = state[c, rim + x] - removed[c].reshape(ny, nz)
        copy = pltpu.make_async_copy(left.at[:, x], left_out.at[0, :, x], out_sem.at[3])
        copy.start()
    for other in range(1, groups):
        margin_copy(other, lax.rem(g - other + groups, groups)).wait_recv()
    margin_row[...] = jnp.min(margin_all[...], axis=0)
    copy = pltpu.make_async_copy(margin_row, margin_out, out_sem.at[2])
    copy.start()
    outs.append(copy)
    coef_drain()
    for other in range(1, groups):
        margin_copy(other, g).wait_send()
    for copy in outs:
        copy.wait()
    pltpu.make_async_copy(left, left_out.at[0], out_sem.at[3]).wait()


def square_kernel(tiles, left, square_out, send, everyone, ssem, rsem):
    g = lax.axis_index("grp")
    t = lax.axis_index("tile")
    _, parts, slab, ny, nz = left.shape
    barrier = pltpu.get_barrier_semaphore()

    def peer(r):
        return {"grp": g, "tile": lax.rem(t + r, tiles)}

    def greet(r, carry):
        pl.semaphore_signal(barrier, inc=1, device_id=peer(r), device_id_type=MESH)
        return carry

    lax.fori_loop(1, tiles, greet, 0)
    pl.semaphore_wait(barrier, tiles - 1)
    total = jnp.zeros((ny, nz), f32)
    for c in range(parts):
        for x in range(slab):
            total = total + left[0, c, x] * left[0, c, x]
    send[...] = jnp.sum(total, axis=0, keepdims=True)

    def copy(r, sender):
        return pltpu.make_async_remote_copy(
            src_ref=send,
            dst_ref=everyone.at[sender],
            send_sem=ssem.at[r],
            recv_sem=rsem.at[r],
            device_id=peer(r),
            device_id_type=MESH,
        )

    lax.fori_loop(1, tiles, lambda r, c: (copy(r, t).start(), c)[1], 0)
    everyone[t] = send[...]
    lax.fori_loop(
        1, tiles, lambda r, c: (copy(r, lax.rem(t - r + tiles, tiles)).wait_recv(), c)[1], 0
    )
    count = f32(parts * slab * ny * nz * tiles)
    square = jnp.sum(jnp.sum(everyone[...], axis=0), axis=1, keepdims=True) / count
    square_out[...] = jnp.broadcast_to(square, square_out.shape)
    lax.fori_loop(1, tiles, lambda r, c: (copy(r, t).wait_send(), c)[1], 0)


def finish(left, coefs, square, out, coef_out, norm_out, held, row, norm_row, line, sem):
    loads = [
        pltpu.make_async_copy(square, row, sem.at[0]),
        pltpu.make_async_copy(left, held, sem.at[1]),
        pltpu.make_async_copy(coefs, line, sem.at[2]),
    ]
    for copy in loads:
        copy.start()
    loads[0].wait()
    norm = jnp.sqrt(row[...])
    norm_row[...] = norm
    loads[2].wait()
    stores = [
        pltpu.make_async_copy(norm_row, norm_out, sem.at[0]),
        pltpu.make_async_copy(line, coef_out, sem.at[2]),
    ]
    for copy in stores:
        copy.start()
    inverse = jnp.broadcast_to(1.0 / norm, left.shape[3:])
    loads[1].wait()
    for c in range(left.shape[1]):
        for x in range(left.shape[2]):
            held[0, c, x] = held[0, c, x] * inverse
    last = pltpu.make_async_copy(held, out, sem.at[1])
    last.start()
    for copy in stores:
        copy.wait()
    last.wait()


def on_device(groups, tiles, basis, snapshots, coupling):
    krylov, parts, slab, ny, nz = basis.shape
    local, fields = snapshots.shape[:2]
    steps = local * groups
    rim = 3 * steps
    planes = slab + 2 * rim
    count = len(spans(slab, rim))
    blocks, height = gram_blocks(krylov, nz)
    width = -(-(krylov + 1) // nz) * nz
    dma = pltpu.SemaphoreType.DMA
    field = pltpu.VMEM((parts, planes, ny, nz), f32)
    whole = pl.BlockSpec(memory_space=pltpu.VMEM)
    anywhere = pl.BlockSpec(memory_space=pl.ANY)
    results = pl.pallas_call(
        functools.partial(kernel, groups, tiles),
        name="propagate",
        out_shape=(
            jax.ShapeDtypeStruct((1, parts, slab, ny, nz), f32),
            jax.ShapeDtypeStruct((1, krylov), f32),
            jax.ShapeDtypeStruct((1, nz), f32),
            jax.ShapeDtypeStruct((1, nz), f32),
        ),
        in_specs=[anywhere] * 3,
        out_specs=(anywhere,) * 4,
        scratch_shapes=[
            pltpu.SMEM(coupling.shape, f32),
            pltpu.VMEM(basis.shape, bf16),
            pltpu.VMEM(basis.shape, f32),
            pltpu.VMEM((parts, planes, ny, nz), bf16),
            pltpu.VMEM((steps, fields, planes, ny, nz), bf16),
            field,
            field,
            field,
            pltpu.VMEM((parts, slab, ny, nz), f32),
            pltpu.VMEM((krylov * ny, krylov * ny), f32),
            pltpu.VMEM((krylov, nz), f32),
            pltpu.VMEM((krylov, 8, nz), f32),
            pltpu.VMEM((height, blocks * krylov), f32),
            pltpu.VMEM((tiles, height, blocks * krylov), f32),
            pltpu.VMEM((1, width), f32),
            pltpu.VMEM((tiles, 1, width), f32),
            pltpu.VMEM((1, nz), f32),
            pltpu.VMEM((groups, 1, nz), f32),
            pltpu.VMEM((1, krylov), f32),
            pltpu.VMEM((1, nz), f32),
            pltpu.VMEM((1, nz), f32),
            dma((3 + local,)),
            dma((1,)),
            dma((count,)),
            dma((local,)),
            dma((local,)),
            dma((steps, count + 1)),
            dma((2,)),
            dma((2,)),
            dma((groups,)),
            dma((groups,)),
            dma((4,)),
            pltpu.SemaphoreType.REGULAR((tiles.bit_length() + 2 + -(-rim // slab),)),
        ],
        compiler_params=pltpu.CompilerParams(
            collective_id=0, has_side_effects=True, vmem_limit_bytes=67043328
        ),
    )(coupling, basis, snapshots)
    left, coefs, square, margin = results

    def scaled(left, coefs, square):
        return pl.pallas_call(
            finish,
            name="finish",
            out_shape=tuple(jax.ShapeDtypeStruct(a.shape, f32) for a in (left, coefs, square)),
            in_specs=[anywhere] * 3,
            out_specs=(anywhere,) * 3,
            scratch_shapes=[
                pltpu.VMEM(left.shape, f32),
                pltpu.VMEM(square.shape, f32),
                pltpu.VMEM(square.shape, f32),
                pltpu.VMEM(coefs.shape, f32),
                dma((3,)),
            ],
        )(left, coefs, square)

    def summed(left, coefs, square):
        exact = pl.pallas_call(
            functools.partial(square_kernel, tiles),
            name="exact_square",
            out_shape=jax.ShapeDtypeStruct((1, nz), f32),
            in_specs=[whole],
            out_specs=whole,
            scratch_shapes=[
                pltpu.VMEM((1, nz), f32),
                pltpu.VMEM((tiles, 1, nz), f32),
                dma((tiles,)),
                dma((tiles,)),
            ],
            compiler_params=pltpu.CompilerParams(collective_id=1, has_side_effects=True),
        )(left)
        return scaled(left, coefs, exact)

    new_vector, coefs, norms = lax.cond(margin[0, 0] > 0.0, scaled, summed, left, coefs, square)
    return new_vector, coefs, norms[0, :1]


def solution(mesh):
    placed = (P(None, None, "tile", None, None), P("grp", None, "tile", None, None), P())
    return jax.shard_map(
        functools.partial(on_device, mesh.shape["grp"], mesh.shape["tile"]),
        mesh=mesh,
        in_specs=placed,
        out_specs=(P("grp", None, "tile", None, None), P("grp", None), P("grp")),
        check_vma=False,
    )
```

```python
import functools

import jax
import jax.numpy as jnp
from jax import lax
from jax.experimental import pallas as pl
from jax.experimental.pallas import tpu as pltpu
from jax.sharding import PartitionSpec as P

viscosity = 0.5
time_step = 0.3
cancel_limit = 0.01
f32 = jnp.float32
bf16 = jnp.bfloat16
MESH = pl.DeviceIdType.MESH
HIGHEST = lax.Precision.HIGHEST


def spans(slab, rim):
    found = {}
    reach = -(-rim // slab)
    for d in range(1, reach + 1):
        width = min(slab, rim - (d - 1) * slab)
        found[-d] = (slab - width, slab)
        found[d] = (0, width)
    return found


def gram_blocks(krylov, lanes):
    blocks = max(lanes // krylov, 1)
    return (blocks, krylov // blocks) if krylov % (8 * blocks) == 0 else (1, krylov)


def stage(src, old, dst, rates, snap, step, coupling, lo, planes, keep, scale):
    rows, lanes = snap.shape[3], snap.shape[4]
    row = lax.broadcasted_iota(jnp.int32, (rows, lanes), 0)
    top = row == 0
    bottom = row == rows - 1
    mix = [[coupling[k, j] for j in range(5)] for k in range(5)]
    edge = viscosity * time_step

    def cells(field, k, p, shift=0):
        return field[k, pl.ds(p * rows + shift, rows)]

    def make_rates(p):
        base = [snap[step, n, p].astype(f32) for n in range(4)]
        half = [(0.5 * time_step) * base[n] for n in range(3)]
        pull = time_step * base[3]
        found = [edge - half[0], edge + half[0]]
        found += [jnp.where(bottom, 0.0, edge - half[1]), jnp.where(top, 0.0, edge + half[1])]
        found += [edge - half[2], edge + half[2], pull]
        own = 1.0 - 6.0 * edge
        found += [own - pull * mix[k][k] for k in range(5)]
        for n, rate in enumerate(found):
            rates[step, n, p] = rate
        return found

    def body(i, carry):
        p = lo + i
        now = [rates[step, n, p] for n in range(12)] if keep else make_rates(p)
        x_up, x_low, y_up, y_low, z_up, z_low, pull = now[:7]
        center = [cells(src, k, p) for k in range(5)]
        for k in range(5):
            q = center[k]
            others = [j for j in range(5) if j != k]
            coupled = mix[k][others[0]] * center[others[0]]
            for j in others[1:]:
                coupled = coupled + mix[k][j] * center[j]
            total = now[7 + k] * q - pull * coupled
            total = total + (x_up * cells(src, k, p + 1) + x_low * cells(src, k, p - 1))
            total = total + (y_up * cells(src, k, p, 1) + y_low * cells(src, k, p, -1))
            total = total + (z_up * pltpu.roll(q, lanes - 1, 1) + z_low * pltpu.roll(q, 1, 1))
            if keep:
                total = total + keep * cells(old, k, p)
            if scale != 1.0:
                total = total * scale
            dst[k, pl.ds(p * rows, rows)] = total
        return carry

    unroll = max(n for n in range(1, 5) if planes % n == 0)
    lax.fori_loop(0, planes, body, 0, unroll=unroll)


def kernel(
    groups, tiles, coupling_in, basis, snapshots,
    left_out, coef_out, square_out, margin_out,
    coupling, held, plain, start, snap, state, one, two, rates, cross, rows_k, spread,
    gram_send, gram_all, coef_send, coef_all,
    load_sem, start_send, start_recv, snap_send, relay_send, snap_recv,
    share_send, share_recv, pass_send, pass_recv, ready,
):
    g = lax.axis_index("grp")
    t = lax.axis_index("tile")
    krylov, parts, slab, ny, nz = basis.shape
    local = snapshots.shape[0]
    steps = local * groups
    rim = 3 * steps
    planes = slab + 2 * rim
    near = spans(slab, rim)
    offsets = sorted(near)
    position = krylov - groups + g
    levels = [b for b in range(tiles.bit_length() - 1) if (1 << b) in offsets]
    stride = 1 << len(levels)
    length = tiles // stride
    link = t // stride

    def at(group, offset):
        return {"grp": group, "tile": lax.rem(t + (offset % tiles), tiles)}

    def flipped(level):
        bit = 1 << level
        return {"grp": g, "tile": t + bit - 2 * bit * lax.rem(t // bit, 2)}

    def partner(other):
        return {"grp": lax.rem(g + other, groups), "tile": t}

    barrier = pltpu.get_barrier_semaphore()
    reach = max(offsets)

    def crosses(d):
        return t + d >= tiles if d > 0 else t + d < 0

    def greet(peer):
        pl.semaphore_signal(barrier, inc=1, device_id=peer, device_id_type=MESH)

    greeters = groups - 1
    for d in sorted(offsets, key=abs, reverse=True):
        if d > 0:
            greet(at(g, -d))
            greeters = greeters + 1 + jnp.where(crosses(d), groups - 1, 0)

            @pl.when(crosses(-d))
            def _():
                for other in range(1, groups):
                    greet(at(lax.rem(g + other, groups), -d))
        else:
            pl.when(jnp.logical_not(crosses(-d)))(functools.partial(greet, at(g, -d)))
            greeters = greeters + jnp.where(crosses(d), 0, 1)
    for other in range(1, groups):
        greet(partner(other))
    for way in (1, -1):
        last = link == (length - 1 if way > 0 else 0)
        greeters = greeters + jnp.where(last, 0, 1)

        @pl.when(jnp.logical_not(last))
        def _():
            greet(at(g, way * stride))

    chunk = 8 if krylov % 8 == 0 else 1
    own = pltpu.make_async_copy(basis.at[position], start.at[:, pl.ds(rim, slab)], load_sem.at[0])
    own.start()
    mix = pltpu.make_async_copy(coupling_in, coupling, load_sem.at[1])
    mix.start()
    for n in range(krylov // chunk):
        part = pl.ds(n * chunk, chunk)
        pltpu.make_async_copy(basis.at[part], held.at[part], load_sem.at[2]).start()

    def target(d, first, last):
        return pl.ds(rim + d * slab + first, last - first)

    start_copies = []
    for n, d in enumerate(offsets):
        first, last = near[d]
        start_copies.append(
            pltpu.make_async_remote_copy(
                src_ref=basis.at[position, :, pl.ds(first, last - first)],
                dst_ref=start.at[:, target(d, first, last)],
                send_sem=start_send.at[0],
                recv_sem=start_recv.at[n],
                device_id=at(g, -d),
                device_id_type=MESH,
            )
        )

    def snap_copy(s, n, d, other):
        first, last = (0, slab) if d == 0 else spans(slab, rim - 3 * s - 1)[d]
        return pltpu.make_async_remote_copy(
            src_ref=snapshots.at[s % local, :, pl.ds(first, last - first)],
            dst_ref=snap.at[s, :, target(d, first, last)],
            send_sem=snap_send.at[s % local],
            recv_sem=snap_recv.at[s, n],
            device_id=at(lax.rem(g + other, groups), -d),
            device_id_type=MESH,
        )

    def local_snap(s):
        return pltpu.make_async_copy(
            snapshots.at[s % local], snap.at[s, :, pl.ds(rim, slab)], load_sem.at[3 + s % local]
        )

    def snap_offsets(s):
        inside = spans(slab, rim - 3 * s - 1)
        return [(n, d) for n, d in enumerate([0] + offsets) if d == 0 or d in inside]

    def snap_each(s, ds, act):
        inside = {d: n for n, d in snap_offsets(s)}

        @pl.when(g == s // local)
        def _():
            for d in ds:
                if d in inside:
                    for other in range(1 if d else groups):
                        if d or other:
                            act(snap_copy(s, inside[d], d, other))
                    if d == reach:
                        @pl.when(crosses(-d))
                        def _():
                            for other in range(1, groups):
                                act(snap_copy(s, inside[d], d, other))

    def relay_copy(s, n, d, other):
        first, last = spans(slab, rim - 3 * s - 1)[d]
        cells = snap.at[s, :, target(d, first, last)]
        return pltpu.make_async_remote_copy(
            src_ref=cells,
            dst_ref=cells,
            send_sem=relay_send.at[s % local],
            recv_sem=snap_recv.at[s, n],
            device_id=at(lax.rem(g + other, groups), 0),
            device_id_type=MESH,
        )

    def relay(s, ds):
        @pl.when(g == s // local)
        def _():
            for n, d in snap_offsets(s):
                if d and d in ds:
                    snap_copy(s, n, d, 0).wait_recv()

                    def forward():
                        for other in range(1, groups):
                            relay_copy(s, n, d, other).start()

                    if d == reach:
                        pl.when(jnp.logical_not(crosses(d)))(forward)
                    else:
                        forward()
            if 0 in ds:
                local_snap(s).wait()

    def receive(s, ds):
        if groups > 1:
            @pl.when(g != s // local)
            def _():
                for n, d in snap_offsets(s):
                    if d in ds:
                        (relay_copy if d else snap_copy)(s, n, d, 1).wait_recv()

    for s in range(steps):
        @pl.when(g == s // local)
        def _():
            local_snap(s).start()

    pl.semaphore_wait(barrier, greeters)
    def send(s, ds):
        snap_each(s, ds, lambda copy: copy.start())
        if s == 0:
            for d in ds:
                if d:
                    start_copies[offsets.index(d)].start()

    def tell(n, peer):
        pl.semaphore_signal(ready.at[n], inc=1, device_id=peer, device_id_type=MESH)

    edge = len(levels) + 3

    for d in offsets:
        if d < 0:
            @pl.when(crosses(-d))
            def _():
                for other in range(groups):
                    tell(edge - d - 1, at(lax.rem(g + other, groups), -d))

    upper = t >= tiles // 2
    ahead = [d for d in offsets if d < 0]
    back = [-d for d in ahead]

    def send_near(s, ds):
        for d in ds:
            if d < 0:
                send(s, [d])
            else:
                pl.when(jnp.logical_not(crosses(-d)))(functools.partial(send, s, [d]))

    def sided(act, *ds):
        for way, on in ((1, upper), (-1, jnp.logical_not(upper))):
            @pl.when(on)
            def _():
                act([way * d for d in ds])

    near_ds, far_ds = sorted(ahead, key=abs), sorted(back)

    turn = edge + len(back)

    def wait_far(d):
        pl.semaphore_wait(ready.at[edge + d - 1], groups)

    def send_first():
        wait_far(1)
        one_start = start_copies[offsets.index(1)]
        snap_each(0, [1], lambda copy: copy.start())
        pl.when(g != 0)(one_start.start)
        for s in range(1, steps):
            send(s, [1])
        for d in sorted(back)[1:]:
            wait_far(d)
            for s in range(steps):
                send(s, [d])
        pl.when(g == 0)(one_start.start)

    def send_late():
        @pl.when((t > 0) & (t < reach))
        def _():
            pl.semaphore_wait(ready.at[turn], 1)

        for d in sorted(back)[1:]:
            @pl.when((t > 0) & crosses(-d))
            def _():
                wait_far(d)
                for s in range(steps):
                    send(s, [d])

        pl.when((t > 0) & (t + 1 < reach))(functools.partial(tell, turn, at(g, 1)))

    for s in range(steps):
        snap_each(s, [0], lambda copy: copy.start())
        sided(functools.partial(send_near, s), *near_ds, *far_ds)

    def flip_step(n):
        if n:
            pl.semaphore_wait(ready.at[n - 1], 1)
        if n < len(levels):
            tell(n, flipped(levels[n]))

    def pass_on(sem, way):
        head = link == (0 if way > 0 else length - 1)
        tail = link == (length - 1 if way > 0 else 0)

        @pl.when(jnp.logical_not(head))
        def _():
            pl.semaphore_wait(ready.at[sem], 1)

        @pl.when(jnp.logical_not(tail))
        def _():
            tell(sem, at(g, way * stride))

    def chain_step(n):
        if length > 1:
            upper = link >= length // 2
            for way in (1, -1):
                @pl.when(upper == (way < 0))
                def _():
                    mine = -way if n else way
                    pass_on(len(levels) + (mine < 0), mine)

    def tell_group():
        for other in range(1, groups):
            tell(len(levels) + 2, partner(other))

    pltpu.make_async_copy(basis, held, load_sem.at[2]).wait()

    def expand(k, carry):
        plain[k] = held[k].astype(f32)
        return carry

    lax.fori_loop(0, krylov, expand, 0)
    size = krylov * ny
    blocks, height = gram_blocks(krylov, nz)

    def gram_copy(other):
        return pltpu.make_async_remote_copy(
            src_ref=gram_send,
            dst_ref=gram_send,
            send_sem=pass_send.at[other],
            recv_sem=pass_recv.at[0],
            device_id=partner(other),
            device_id_type=MESH,
        )

    @pl.when(g == 0)
    def _():
        for c in range(parts):
            wide = jnp.concatenate([held[:, c, x].reshape(size, nz) for x in range(slab)], axis=1)
            piece = lax.dot_general(wide, wide, (((1,), (1,)), ((), ())), preferred_element_type=f32)
            cross[...] = cross[...] + piece if c else piece
        line = lax.broadcasted_iota(jnp.int32, (size, size), 0)
        column = lax.broadcasted_iota(jnp.int32, (size, size), 1)
        kept = jnp.where(lax.rem(line, ny) == lax.rem(column, ny), cross[...], 0.0)
        kept = jnp.sum(kept.reshape(krylov, ny, size), axis=1)
        pick = (
            lax.broadcasted_iota(jnp.int32, (size, krylov), 0) // ny
            == lax.broadcasted_iota(jnp.int32, (size, krylov), 1)
        ).astype(f32)
        gram = jnp.dot(kept, pick, precision=HIGHEST, preferred_element_type=f32)
        gram_send[...] = jnp.concatenate(
            [gram[n * height : (n + 1) * height] for n in range(blocks)], axis=1
        )
        for other in range(1, groups):
            gram_copy(other).start()

    @pl.when(g == groups - 1)
    def _():
        for n in range(len(levels) + 1):
            flip_step(n)
        chain_step(0)

    pl.when(t == 0)(send_first)
    @pl.when(g == groups - 1)
    def _():
        chain_step(1)
        for other in range(1, groups):
            tell(len(levels) + 2, partner(other))

    def spread_out(n, send, everyone, reached):
        way = 2 * (t // max(tiles // 2, 1)) - 1
        others = everyone.at[pl.ds(0, reached * tiles - 1)]
        place = t if reached == 1 else g * tiles + t

        def begin():
            def one(i, carry):
                peer = lax.rem(2 * tiles - 1 - t + way * i, tiles)

                def to(other):
                    pltpu.make_async_remote_copy(
                        src_ref=send,
                        dst_ref=everyone.at[place],
                        send_sem=share_send.at[n],
                        recv_sem=share_recv.at[n],
                        device_id={"grp": lax.rem(g + other, groups), "tile": peer},
                        device_id_type=MESH,
                    ).start()

                pl.when(peer != t)(functools.partial(to, 0))
                for other in range(1, reached):
                    to(other)
                return carry

            lax.fori_loop(0, tiles, one, 0)
            everyone[place] = send[...]

        def arrive():
            pltpu.make_async_copy(others, others, share_recv.at[n]).wait()

        def drain():
            pltpu.make_async_copy(others, others, share_send.at[n]).wait()

        return begin, arrive, drain

    gram_begin, gram_arrive, gram_drain = spread_out(0, gram_send, gram_all, 1)
    coef_begin, coef_arrive, coef_drain = spread_out(1, coef_send, coef_all, groups)
    def widen(d):
        def one(p, carry):
            for k in range(parts):
                state[k, pl.ds(p * ny, ny)] = start[k, p].astype(f32)
            return carry

        lo, width = (rim, slab) if d == 0 else (rim + d * slab + near[d][0], near[d][1] - near[d][0])
        lax.fori_loop(lo, lo + width, one, 0)

    def arrive(ds):
        for d in ds:
            if d:
                start_copies[offsets.index(d)].wait_recv()
            else:
                own.wait()
                mix.wait()
            widen(d)

    keeps = (0.0, 3.0, 2.0)
    ways = ((state, one), (one, two), (two, state))

    def march(s, known, new):
        for n, (src, dst) in enumerate(ways):
            k = 3 * s + n + 1
            lo, hi = max(k, known - k), new - k
            if hi > lo:
                first = jnp.where(upper, lo, planes - hi)
                scale = 6.0 ** -steps if k == 3 * steps else 1.0
                stage(src, state, dst, rates, snap, s, coupling, first, hi - lo, keeps[n], scale)

    def relay_far(s, d, early):
        for way, on in ((1, upper), (-1, jnp.logical_not(upper))):
            seam = crosses(way * d)

            @pl.when(on & (jnp.logical_not(seam) if early else seam))
            def _():
                relay(s, [way * d])

    sided(lambda ds: relay(0, [0] + ds), *near_ds)
    sided(arrive, *near_ds)
    arrive([0])
    for s in range(1, steps):
        sided(lambda ds: relay(s, [0] + ds), *near_ds)
    relay_far(0, far_ds[0], True)
    sided(lambda ds: receive(0, [0] + ds), *near_ds)
    if reach > 1:
        pl.when(t == 0)(functools.partial(tell, turn, at(g, 1)))
    known = 0
    for piece in range(len(far_ds) + 1):
        if piece:
            d = far_ds[piece - 1]
            if piece == 1:
                relay_far(0, d, False)
            sided(arrive, d)
            for s in range(1, steps):
                relay_far(s, d, False)
            sided(lambda ds: receive(0, ds), d)
        new = rim + slab + sum(near[d][1] - near[d][0] for d in far_ds[:piece])
        for s in range(steps):
            if s:
                sided(lambda ds: receive(s, ds), *(([0] + near_ds) if piece == 0 else far_ds[piece - 1 : piece]))
            march(s, known, new)
            if piece and s == 0 and piece < len(far_ds):
                relay_far(0, far_ds[piece], False)
            if piece == 0 and s == 0:
                send_late()
                for d in far_ds[1:]:
                    relay_far(0, d, True)
                for later in range(1, steps):
                    for d in far_ds:
                        relay_far(later, d, True)
        known = new
        if piece == 0:
            if groups > 1:
                @pl.when(g != groups - 1)
                def _():
                    pl.semaphore_wait(ready.at[len(levels) + 2], 1)

                @pl.when(g != 0)
                def _():
                    gram_copy(0).wait_recv()

            gram_begin()

    count = f32(parts * slab * ny * nz * tiles)

    group = 4 if krylov % 4 == 0 else 1

    def project(i, carry):
        totals = [jnp.zeros((ny, nz), f32) for _ in range(group)]
        for c in range(parts):
            for x in range(slab):
                field = state[c, pl.ds((rim + x) * ny, ny)]
                for n in range(group):
                    totals[n] = totals[n] + plain[i * group + n, c, x] * field
        for n in range(group):
            rows_k[pl.ds(i * group + n, 1), :] = jnp.sum(totals[n], axis=0, keepdims=True)
        return carry

    lax.fori_loop(0, krylov // group, project, 0)
    ones = jnp.ones((8, nz), f32)
    inner = lax.dot_general(
        ones, rows_k[...], (((1,), (1,)), ((), ())), precision=HIGHEST, preferred_element_type=f32
    )
    own_square = jnp.zeros((ny, nz), f32)
    for c in range(parts):
        for x in range(slab):
            own_square = own_square + state[c, pl.ds((rim + x) * ny, ny)] * state[c, pl.ds((rim + x) * ny, ny)]
    own_square = jnp.sum(jnp.sum(own_square, axis=0, keepdims=True), axis=1, keepdims=True)
    coef_send[...] = jnp.concatenate(
        [inner[0:1], jnp.broadcast_to(own_square, (1, coef_send.shape[1] - krylov))], axis=1
    )
    coef_begin()
    def all_sent(cells, sem):
        pltpu.make_async_copy(cells, cells, sem).wait()

    all_sent(start.at[:, pl.ds(0, 2 * rim)], start_send.at[0])
    for s in range(steps):
        around = 2 * (rim - 3 * s - 1)

        @pl.when(g == s // local)
        def _():
            all_sent(snap.at[s, :, pl.ds(0, around)], snap_send.at[s % local])
            last = spans(slab, rim - 3 * s - 1).get(reach, (0, 0))
            last = last[1] - last[0]
            for other in range(1, groups):
                all_sent(snap.at[s, :, pl.ds(0, slab)], snap_send.at[s % local])
                all_sent(snap.at[s, :, pl.ds(0, around - last)], relay_send.at[s % local])
                if last:
                    @pl.when(crosses(-reach))
                    def _():
                        all_sent(snap.at[s, :, pl.ds(0, last)], snap_send.at[s % local])

                    @pl.when(jnp.logical_not(crosses(reach)))
                    def _():
                        all_sent(snap.at[s, :, pl.ds(0, last)], relay_send.at[s % local])

    gram_drain()

    @pl.when(g == 0)
    def _():
        for other in range(1, groups):
            gram_copy(other).wait_send()

    gram_arrive()
    packed = jnp.sum(gram_all[...], axis=0) / count
    gram = jnp.concatenate(
        [packed[:, n * krylov : (n + 1) * krylov] for n in range(blocks)], axis=0
    )
    same = lax.broadcasted_iota(jnp.int32, gram.shape, 0) == lax.broadcasted_iota(jnp.int32, gram.shape, 1)
    times = functools.partial(jnp.dot, precision=HIGHEST, preferred_element_type=f32)
    twice = jnp.where(same, 2.0, 0.0) - gram
    both = jnp.concatenate([twice, times(twice, gram)], axis=1)
    reach_row = jnp.sum(jnp.abs(gram), axis=0, keepdims=True)
    coef_arrive()
    sums = [jnp.sum(coef_all[n * tiles : (n + 1) * tiles], axis=0) / count for n in range(groups)]
    sums = jnp.concatenate(sums + [jnp.zeros((-groups % 8, sums[0].shape[1]), f32)], axis=0)
    first_rows, work_square = sums[:, :krylov], sums[:, krylov : krylov + 1]
    mixed = times(first_rows, both)
    every, turned = mixed[:, :krylov], mixed[:, krylov:]
    group_row = lax.broadcasted_iota(jnp.int32, work_square.shape, 0)
    own_every = jnp.sum(jnp.where(group_row == g, every, 0.0), axis=0, keepdims=True)
    for k in range(krylov):
        spread[k] = jnp.broadcast_to(own_every[:, k : k + 1], (8, nz))
    linear = 2.0 * every * first_rows
    bent = every * turned
    bound = jnp.abs(linear) + every * every * reach_row
    square = work_square + jnp.sum(bent - linear, axis=1, keepdims=True)
    bound = work_square + jnp.sum(bound, axis=1, keepdims=True)
    margin = jnp.where(group_row < groups, square - cancel_limit * bound, jnp.inf)
    margin_out[...] = jnp.broadcast_to(jnp.min(margin, axis=0, keepdims=True), margin_out.shape)
    square = jnp.sum(jnp.where(group_row == g, square, 0.0), axis=0, keepdims=True)
    square_out[...] = jnp.broadcast_to(square, square_out.shape)
    coef_out[...] = own_every
    for x in range(slab):
        removed = [jnp.zeros((ny // 8, 8, nz), f32) for _ in range(parts)]
        for k in range(krylov):
            factor = spread[k][None]
            for c in range(parts):
                removed[c] = removed[c] + factor * plain[k, c, x].reshape(ny // 8, 8, nz)
        for c in range(parts):
            left_out[0, c, x] = state[c, pl.ds((rim + x) * ny, ny)] - removed[c].reshape(ny, nz)
    coef_drain()


def square_kernel(tiles, left, square_out, send, everyone, ssem, rsem):
    g = lax.axis_index("grp")
    t = lax.axis_index("tile")
    _, parts, slab, ny, nz = left.shape
    barrier = pltpu.get_barrier_semaphore()

    def peer(r):
        return {"grp": g, "tile": lax.rem(t + r, tiles)}

    def greet(r, carry):
        pl.semaphore_signal(barrier, inc=1, device_id=peer(r), device_id_type=MESH)
        return carry

    lax.fori_loop(1, tiles, greet, 0)
    pl.semaphore_wait(barrier, tiles - 1)
    total = jnp.zeros((ny, nz), f32)
    for c in range(parts):
        for x in range(slab):
            total = total + left[0, c, x] * left[0, c, x]
    send[...] = jnp.sum(total, axis=0, keepdims=True)

    def copy(r, sender):
        return pltpu.make_async_remote_copy(
            src_ref=send,
            dst_ref=everyone.at[sender],
            send_sem=ssem.at[r],
            recv_sem=rsem.at[r],
            device_id=peer(r),
            device_id_type=MESH,
        )

    lax.fori_loop(1, tiles, lambda r, c: (copy(r, t).start(), c)[1], 0)
    everyone[t] = send[...]
    lax.fori_loop(
        1, tiles, lambda r, c: (copy(r, lax.rem(t - r + tiles, tiles)).wait_recv(), c)[1], 0
    )
    count = f32(parts * slab * ny * nz * tiles)
    square = jnp.sum(jnp.sum(everyone[...], axis=0), axis=1, keepdims=True) / count
    square_out[...] = jnp.broadcast_to(square, square_out.shape)
    lax.fori_loop(1, tiles, lambda r, c: (copy(r, t).wait_send(), c)[1], 0)


def finish(left, coefs, square, out, coef_out, norm_out, held, norm_row, sem):
    norm = jnp.sqrt(square[...])
    norm_row[...] = norm
    inverse = jnp.broadcast_to(1.0 / norm, left.shape[3:])
    copies = [
        pltpu.make_async_copy(norm_row, norm_out, sem.at[0]),
        pltpu.make_async_copy(coefs, coef_out, sem.at[1]),
    ]
    for c in range(left.shape[1]):
        for x in range(left.shape[2]):
            held[0, c, x] = left[0, c, x] * inverse
    copies.append(pltpu.make_async_copy(held, out, sem.at[2]))
    for copy in copies:
        copy.start()
    for copy in copies:
        copy.wait()


def on_device(groups, tiles, basis, snapshots, coupling):
    krylov, parts, slab, ny, nz = basis.shape
    local, fields = snapshots.shape[:2]
    steps = local * groups
    rim = 3 * steps
    planes = slab + 2 * rim
    count = len(spans(slab, rim))
    blocks, height = gram_blocks(krylov, nz)
    width = -(-(krylov + 1) // nz) * nz
    dma = pltpu.SemaphoreType.DMA
    field = pltpu.VMEM((parts, planes * ny, nz), f32)
    whole = pl.BlockSpec(memory_space=pltpu.VMEM)
    outside = pl.BlockSpec(memory_space=pltpu.HBM)
    results = pl.pallas_call(
        functools.partial(kernel, groups, tiles),
        name="propagate",
        out_shape=(
            jax.ShapeDtypeStruct((1, parts, slab, ny, nz), f32),
            jax.ShapeDtypeStruct((1, krylov), f32),
            jax.ShapeDtypeStruct((1, nz), f32),
            jax.ShapeDtypeStruct((1, nz), f32),
        ),
        in_specs=[outside] * 3,
        out_specs=(whole,) * 4,
        scratch_shapes=[
            pltpu.SMEM(coupling.shape, f32),
            pltpu.VMEM(basis.shape, bf16),
            pltpu.VMEM(basis.shape, f32),
            pltpu.VMEM((parts, planes, ny, nz), bf16),
            pltpu.VMEM((steps, fields, planes, ny, nz), bf16),
            field,
            field,
            field,
            pltpu.VMEM((steps, 12, planes, ny, nz), f32),
            pltpu.VMEM((krylov * ny, krylov * ny), f32),
            pltpu.VMEM((krylov, nz), f32),
            pltpu.VMEM((krylov, 8, nz), f32),
            pltpu.VMEM((height, blocks * krylov), f32),
            pltpu.VMEM((tiles, height, blocks * krylov), f32),
            pltpu.VMEM((1, width), f32),
            pltpu.VMEM((groups * tiles, 1, width), f32),
            dma((3 + local,)),
            dma((1,)),
            dma((count,)),
            dma((local,)),
            dma((local,)),
            dma((steps, count + 1)),
            dma((2,)),
            dma((2,)),
            dma((groups,)),
            dma((1,)),
            pltpu.SemaphoreType.REGULAR((tiles.bit_length() + 3 + -(-rim // slab),)),
        ],
        compiler_params=pltpu.CompilerParams(
            collective_id=0, has_side_effects=True, vmem_limit_bytes=48 << 20
        ),
    )(*(pltpu.with_memory_space_constraint(a, pltpu.HBM) for a in (coupling, basis, snapshots)))
    left, coefs, square, margin = results

    def scaled(left, coefs, square):
        return pl.pallas_call(
            finish,
            name="finish",
            out_shape=tuple(jax.ShapeDtypeStruct(a.shape, f32) for a in (left, coefs, square)),
            in_specs=[whole] * 3,
            out_specs=(outside,) * 3,
            scratch_shapes=[
                pltpu.VMEM(left.shape, f32),
                pltpu.VMEM(square.shape, f32),
                dma((3,)),
            ],
        )(left, coefs, square)

    def summed(left, coefs, square):
        exact = pl.pallas_call(
            functools.partial(square_kernel, tiles),
            name="exact_square",
            out_shape=jax.ShapeDtypeStruct((1, nz), f32),
            in_specs=[whole],
            out_specs=whole,
            scratch_shapes=[
                pltpu.VMEM((1, nz), f32),
                pltpu.VMEM((tiles, 1, nz), f32),
                dma((tiles,)),
                dma((tiles,)),
            ],
            compiler_params=pltpu.CompilerParams(collective_id=1, has_side_effects=True),
        )(left)
        return scaled(left, coefs, exact)

    new_vector, coefs, norms = lax.cond(margin[0, 0] > 0.0, scaled, summed, left, coefs, square)
    return new_vector, coefs, norms[0, :1]


def solution(mesh):
    placed = (P(None, None, "tile", None, None), P("grp", None, "tile", None, None), P())
    return jax.shard_map(
        functools.partial(on_device, mesh.shape["grp"], mesh.shape["tile"]),
        mesh=mesh,
        in_specs=placed,
        out_specs=(P("grp", None, "tile", None, None), P("grp", None), P("grp")),
        check_vma=False,
    )
```

```python
import functools

import jax
import jax.numpy as jnp
from jax import lax
from jax.experimental import pallas as pl
from jax.experimental.pallas import tpu as pltpu
from jax.sharding import PartitionSpec as P

viscosity = 0.5
time_step = 0.3
cancel_limit = 0.01
f32 = jnp.float32
bf16 = jnp.bfloat16
MESH = pl.DeviceIdType.MESH
HIGHEST = lax.Precision.HIGHEST


def spans(slab, rim):
    found = {}
    reach = -(-rim // slab)
    for d in range(1, reach + 1):
        width = min(slab, rim - (d - 1) * slab)
        found[-d] = (slab - width, slab)
        found[d] = (0, width)
    return found


def gram_blocks(krylov, lanes):
    blocks = max(lanes // krylov, 1)
    return (blocks, krylov // blocks) if krylov % (8 * blocks) == 0 else (1, krylov)


def stage(src, old, dst, rates, snap, step, coupling, lo, planes, keep, scale):
    rows, lanes = snap.shape[3], snap.shape[4]
    row = lax.broadcasted_iota(jnp.int32, (rows, lanes), 0)
    top = row == 0
    bottom = row == rows - 1
    mix = [[coupling[k, j] for j in range(5)] for k in range(5)]
    edge = viscosity * time_step

    def cells(field, k, p, shift=0):
        return field[k, pl.ds(p * rows + shift, rows)]

    def make_rates(p):
        base = [snap[step, n, p].astype(f32) for n in range(4)]
        half = [(0.5 * time_step) * base[n] for n in range(3)]
        pull = time_step * base[3]
        found = [edge - half[0], edge + half[0]]
        found += [jnp.where(bottom, 0.0, edge - half[1]), jnp.where(top, 0.0, edge + half[1])]
        found += [edge - half[2], edge + half[2], pull]
        own = 1.0 - 6.0 * edge
        found += [own - pull * mix[k][k] for k in range(5)]
        for n, rate in enumerate(found):
            rates[step, n, p] = rate
        return found

    def body(i, carry):
        p = lo + i
        now = [rates[step, n, p] for n in range(12)] if keep else make_rates(p)
        x_up, x_low, y_up, y_low, z_up, z_low, pull = now[:7]
        center = [cells(src, k, p) for k in range(5)]
        for k in range(5):
            q = center[k]
            others = [j for j in range(5) if j != k]
            coupled = mix[k][others[0]] * center[others[0]]
            for j in others[1:]:
                coupled = coupled + mix[k][j] * center[j]
            total = now[7 + k] * q - pull * coupled
            total = total + (x_up * cells(src, k, p + 1) + x_low * cells(src, k, p - 1))
            total = total + (y_up * cells(src, k, p, 1) + y_low * cells(src, k, p, -1))
            total = total + (z_up * pltpu.roll(q, lanes - 1, 1) + z_low * pltpu.roll(q, 1, 1))
            if keep:
                total = total + keep * cells(old, k, p)
            if scale != 1.0:
                total = total * scale
            dst[k, pl.ds(p * rows, rows)] = total
        return carry

    unroll = max(n for n in range(1, 5) if planes % n == 0)
    lax.fori_loop(0, planes, body, 0, unroll=unroll)


def kernel(
    groups, tiles, coupling_in, basis, snapshots,
    left_out, coef_out, square_out, margin_out,
    coupling, held, plain, start, snap, state, one, two, rates, cross, rows_k, spread,
    gram_send, gram_all, coef_send, coef_all,
    load_sem, start_send, start_recv, snap_send, relay_send, snap_recv,
    share_send, share_recv, pass_send, pass_recv, ready,
):
    g = lax.axis_index("grp")
    t = lax.axis_index("tile")
    krylov, parts, slab, ny, nz = basis.shape
    local = snapshots.shape[0]
    steps = local * groups
    rim = 3 * steps
    planes = slab + 2 * rim
    near = spans(slab, rim)
    offsets = sorted(near)
    position = krylov - groups + g
    levels = [b for b in range(tiles.bit_length() - 1) if (1 << b) in offsets]
    stride = 1 << len(levels)
    length = tiles // stride
    link = t // stride

    def at(group, offset):
        return {"grp": group, "tile": lax.rem(t + (offset % tiles), tiles)}

    def flipped(level):
        bit = 1 << level
        return {"grp": g, "tile": t + bit - 2 * bit * lax.rem(t // bit, 2)}

    def partner(other):
        return {"grp": lax.rem(g + other, groups), "tile": t}

    barrier = pltpu.get_barrier_semaphore()
    reach = max(offsets)

    def crosses(d):
        return t + d >= tiles if d > 0 else t + d < 0

    def greet(peer):
        pl.semaphore_signal(barrier, inc=1, device_id=peer, device_id_type=MESH)

    greeters = groups - 1
    for d in sorted(offsets, key=abs, reverse=True):
        if d > 0:
            greet(at(g, -d))
            greeters = greeters + 1 + jnp.where(crosses(d), groups - 1, 0)

            @pl.when(crosses(-d))
            def _():
                for other in range(1, groups):
                    greet(at(lax.rem(g + other, groups), -d))
        else:
            pl.when(jnp.logical_not(crosses(-d)))(functools.partial(greet, at(g, -d)))
            greeters = greeters + jnp.where(crosses(d), 0, 1)
    held_back = near[reach][1] - near[reach][0]
    carried = reach > 1 and held_back < slab and 2 * reach < tiles
    if carried:
        pl.when(t == reach)(functools.partial(greet, {"grp": g, "tile": tiles - 1}))
        greeters = greeters + jnp.where(t == tiles - 1, 1, 0)
    for other in range(1, groups):
        greet(partner(other))
    for way in (1, -1):
        last = link == (length - 1 if way > 0 else 0)
        greeters = greeters + jnp.where(last, 0, 1)

        @pl.when(jnp.logical_not(last))
        def _():
            greet(at(g, way * stride))

    chunk = 8 if krylov % 8 == 0 else 1
    own = pltpu.make_async_copy(basis.at[position], start.at[:, pl.ds(rim, slab)], load_sem.at[0])
    own.start()
    mix = pltpu.make_async_copy(coupling_in, coupling, load_sem.at[1])
    mix.start()
    for n in range(krylov // chunk):
        part = pl.ds(n * chunk, chunk)
        pltpu.make_async_copy(basis.at[part], held.at[part], load_sem.at[2]).start()

    def target(d, first, last):
        return pl.ds(rim + d * slab + first, last - first)

    start_copies = []
    for n, d in enumerate(offsets):
        first, last = near[d]
        start_copies.append(
            pltpu.make_async_remote_copy(
                src_ref=basis.at[position, :, pl.ds(first, last - first)],
                dst_ref=start.at[:, target(d, first, last)],
                send_sem=start_send.at[0],
                recv_sem=start_recv.at[n],
                device_id=at(g, -d),
                device_id_type=MESH,
            )
        )

    def snap_copy(s, n, d, other):
        first, last = (0, slab) if d == 0 else spans(slab, rim - 3 * s - 1)[d]
        return pltpu.make_async_remote_copy(
            src_ref=snapshots.at[s % local, :, pl.ds(first, last - first)],
            dst_ref=snap.at[s, :, target(d, first, last)],
            send_sem=snap_send.at[s % local],
            recv_sem=snap_recv.at[s, n],
            device_id=at(lax.rem(g + other, groups), -d),
            device_id_type=MESH,
        )

    def local_snap(s):
        return pltpu.make_async_copy(
            snapshots.at[s % local], snap.at[s, :, pl.ds(rim, slab)], load_sem.at[3 + s % local]
        )

    def snap_offsets(s):
        inside = spans(slab, rim - 3 * s - 1)
        return [(n, d) for n, d in enumerate([0] + offsets) if d == 0 or d in inside]

    def snap_each(s, ds, act):
        inside = {d: n for n, d in snap_offsets(s)}

        @pl.when(g == s // local)
        def _():
            for d in ds:
                if d in inside:
                    for other in range(1 if d else groups):
                        if d or other:
                            act(snap_copy(s, inside[d], d, other))
                    if d == reach:
                        @pl.when(crosses(-d))
                        def _():
                            for other in range(1, groups):
                                act(snap_copy(s, inside[d], d, other))

    def relay_copy(s, n, d, other):
        first, last = spans(slab, rim - 3 * s - 1)[d]
        cells = snap.at[s, :, target(d, first, last)]
        return pltpu.make_async_remote_copy(
            src_ref=cells,
            dst_ref=cells,
            send_sem=relay_send.at[s % local],
            recv_sem=snap_recv.at[s, n],
            device_id=at(lax.rem(g + other, groups), 0),
            device_id_type=MESH,
        )

    def relay(s, ds):
        @pl.when(g == s // local)
        def _():
            for n, d in snap_offsets(s):
                if d and d in ds:
                    snap_copy(s, n, d, 0).wait_recv()

                    def forward():
                        for other in range(1, groups):
                            relay_copy(s, n, d, other).start()

                    if d == reach:
                        pl.when(jnp.logical_not(crosses(d)))(forward)
                    else:
                        forward()
            if 0 in ds:
                local_snap(s).wait()

    def receive(s, ds):
        if groups > 1:
            @pl.when(g != s // local)
            def _():
                for n, d in snap_offsets(s):
                    if d in ds:
                        (relay_copy if d else snap_copy)(s, n, d, 1).wait_recv()

    for s in range(steps):
        @pl.when(g == s // local)
        def _():
            local_snap(s).start()

    pl.semaphore_wait(barrier, greeters)
    def send(s, ds):
        snap_each(s, ds, lambda copy: copy.start())
        if s == 0:
            for d in ds:
                if d:
                    start_copies[offsets.index(d)].start()

    def tell(n, peer):
        pl.semaphore_signal(ready.at[n], inc=1, device_id=peer, device_id_type=MESH)

    edge = len(levels) + 3

    for d in offsets:
        if d < 0:
            @pl.when(crosses(-d))
            def _():
                for other in range(groups):
                    tell(edge - d - 1, at(lax.rem(g + other, groups), -d))

    upper = t >= tiles // 2
    ahead = [d for d in offsets if d < 0]
    back = [-d for d in ahead]

    def send_near(s, ds):
        for d in ds:
            if d < 0:
                send(s, [d])
            else:
                pl.when(jnp.logical_not(crosses(-d)))(functools.partial(send, s, [d]))

    def sided(act, *ds):
        for way, on in ((1, upper), (-1, jnp.logical_not(upper))):
            @pl.when(on)
            def _():
                act([way * d for d in ds])

    near_ds, far_ds = sorted(ahead, key=abs), sorted(back)

    turn = edge + len(back)
    if carried:
        pl.when(t == tiles - 1)(functools.partial(tell, turn, {"grp": g, "tile": reach}))

    def wait_far(d):
        pl.semaphore_wait(ready.at[edge + d - 1], groups)

    def start_copy(d, group, last):
        first = near[d][0]
        return pltpu.make_async_remote_copy(
            src_ref=basis.at[krylov - groups + group, :, pl.ds(first, last - first)],
            dst_ref=start.at[:, target(d, first, last)],
            send_sem=start_send.at[0],
            recv_sem=start_recv.at[offsets.index(d)],
            device_id=at(group, -d),
            device_id_type=MESH,
        )

    def send_first():
        wait_far(1)
        snap_each(0, [1], lambda copy: copy.start())
        start_copy(1, g, slab - held_back if carried else slab).start()
        for s in range(1, steps):
            send(s, [1])
        for d in sorted(back)[1:]:
            wait_far(d)
            for s in range(steps):
                snap_each(s, [d], lambda copy: copy.start())

    def send_second():
        for d in sorted(back)[1:]:
            for group in range(groups):
                start_copy(d, group, near[d][1]).start()

    def send_carried():
        start_copies[offsets.index(-reach)].wait_recv()
        pl.semaphore_wait(ready.at[turn], 1)
        pltpu.make_async_remote_copy(
            src_ref=start.at[:, target(-reach, slab - held_back, slab)],
            dst_ref=start.at[:, target(1, slab - held_back, slab)],
            send_sem=start_send.at[0],
            recv_sem=start_recv.at[offsets.index(1)],
            device_id={"grp": g, "tile": tiles - 1},
            device_id_type=MESH,
        ).start()

    def send_late():
        for d in sorted(back)[1:]:
            @pl.when((t > 0) & crosses(-d))
            def _():
                wait_far(d)
                for s in range(steps):
                    send(s, [d])

    for s in range(steps):
        snap_each(s, [0], lambda copy: copy.start())
        sided(functools.partial(send_near, s), *near_ds, *far_ds)

    def flip_step(n):
        if n:
            pl.semaphore_wait(ready.at[n - 1], 1)
        if n < len(levels):
            tell(n, flipped(levels[n]))

    def pass_on(sem, way):
        head = link == (0 if way > 0 else length - 1)
        tail = link == (length - 1 if way > 0 else 0)

        @pl.when(jnp.logical_not(head))
        def _():
            pl.semaphore_wait(ready.at[sem], 1)

        @pl.when(jnp.logical_not(tail))
        def _():
            tell(sem, at(g, way * stride))

    def chain_step(n):
        if length > 1:
            upper = link >= length // 2
            for way in (1, -1):
                @pl.when(upper == (way < 0))
                def _():
                    mine = -way if n else way
                    pass_on(len(levels) + (mine < 0), mine)

    def tell_group():
        for other in range(1, groups):
            tell(len(levels) + 2, partner(other))

    pltpu.make_async_copy(basis, held, load_sem.at[2]).wait()

    def expand(k, carry):
        plain[k] = held[k].astype(f32)
        return carry

    lax.fori_loop(0, krylov, expand, 0)
    size = krylov * ny
    blocks, height = gram_blocks(krylov, nz)

    def gram_copy(other):
        return pltpu.make_async_remote_copy(
            src_ref=gram_send,
            dst_ref=gram_send,
            send_sem=pass_send.at[other],
            recv_sem=pass_recv.at[0],
            device_id=partner(other),
            device_id_type=MESH,
        )

    @pl.when(g == 0)
    def _():
        for c in range(parts):
            wide = jnp.concatenate([held[:, c, x].reshape(size, nz) for x in range(slab)], axis=1)
            piece = lax.dot_general(wide, wide, (((1,), (1,)), ((), ())), preferred_element_type=f32)
            cross[...] = cross[...] + piece if c else piece
        line = lax.broadcasted_iota(jnp.int32, (size, size), 0)
        column = lax.broadcasted_iota(jnp.int32, (size, size), 1)
        kept = jnp.where(lax.rem(line, ny) == lax.rem(column, ny), cross[...], 0.0)
        kept = jnp.sum(kept.reshape(krylov, ny, size), axis=1)
        pick = (
            lax.broadcasted_iota(jnp.int32, (size, krylov), 0) // ny
            == lax.broadcasted_iota(jnp.int32, (size, krylov), 1)
        ).astype(f32)
        gram = jnp.dot(kept, pick, precision=HIGHEST, preferred_element_type=f32)
        gram_send[...] = jnp.concatenate(
            [gram[n * height : (n + 1) * height] for n in range(blocks)], axis=1
        )
        for other in range(1, groups):
            gram_copy(other).start()

    @pl.when(g == groups - 1)
    def _():
        for n in range(len(levels) + 1):
            flip_step(n)
        chain_step(0)

    pl.when(t == 0)(send_first)
    send_late()
    if carried:
        pl.when(t == reach)(send_carried)
    @pl.when(g == groups - 1)
    def _():
        chain_step(1)
        for other in range(1, groups):
            tell(len(levels) + 2, partner(other))

    def spread_out(n, send, everyone, reached):
        way = 2 * (t // max(tiles // 2, 1)) - 1
        others = everyone.at[pl.ds(0, reached * tiles - 1)]
        place = t if reached == 1 else g * tiles + t

        def begin():
            def one(i, carry):
                peer = lax.rem(2 * tiles - 1 - t + way * i, tiles)

                def to(other):
                    pltpu.make_async_remote_copy(
                        src_ref=send,
                        dst_ref=everyone.at[place],
                        send_sem=share_send.at[n],
                        recv_sem=share_recv.at[n],
                        device_id={"grp": lax.rem(g + other, groups), "tile": peer},
                        device_id_type=MESH,
                    ).start()

                pl.when(peer != t)(functools.partial(to, 0))
                for other in range(1, reached):
                    to(other)
                return carry

            lax.fori_loop(0, tiles, one, 0)
            everyone[place] = send[...]

        def arrive():
            pltpu.make_async_copy(others, others, share_recv.at[n]).wait()

        def drain():
            pltpu.make_async_copy(others, others, share_send.at[n]).wait()

        return begin, arrive, drain

    gram_begin, gram_arrive, gram_drain = spread_out(0, gram_send, gram_all, 1)
    coef_begin, coef_arrive, coef_drain = spread_out(1, coef_send, coef_all, groups)
    def widen(d):
        def one(p, carry):
            for k in range(parts):
                state[k, pl.ds(p * ny, ny)] = start[k, p].astype(f32)
            return carry

        lo, width = (rim, slab) if d == 0 else (rim + d * slab + near[d][0], near[d][1] - near[d][0])
        lax.fori_loop(lo, lo + width, one, 0)

    def arrive(ds):
        for d in ds:
            if d == -reach and carried:
                pl.when(t != reach)(start_copies[offsets.index(d)].wait_recv)
            elif d:
                start_copies[offsets.index(d)].wait_recv()
            else:
                own.wait()
                mix.wait()
            widen(d)

    keeps = (0.0, 3.0, 2.0)
    ways = ((state, one), (one, two), (two, state))

    def march(s, known, new):
        for n, (src, dst) in enumerate(ways):
            k = 3 * s + n + 1
            lo, hi = max(k, known - k), new - k
            if hi > lo:
                first = jnp.where(upper, lo, planes - hi)
                scale = 6.0 ** -steps if k == 3 * steps else 1.0
                stage(src, state, dst, rates, snap, s, coupling, first, hi - lo, keeps[n], scale)

    def relay_far(s, d, early):
        for way, on in ((1, upper), (-1, jnp.logical_not(upper))):
            seam = crosses(way * d)

            @pl.when(on & (jnp.logical_not(seam) if early else seam))
            def _():
                relay(s, [way * d])

    sided(lambda ds: relay(0, [0] + ds), *near_ds)
    sided(arrive, *near_ds)
    arrive([0])
    for s in range(1, steps):
        sided(lambda ds: relay(s, [0] + ds), *near_ds)
    relay_far(0, far_ds[0], True)
    sided(lambda ds: receive(0, [0] + ds), *near_ds)
    pl.when((t == 0) & (g == groups - 1))(send_second)
    known = 0
    for piece in range(len(far_ds) + 1):
        if piece:
            d = far_ds[piece - 1]
            if piece == 1:
                relay_far(0, d, False)
            sided(arrive, d)
            for s in range(1, steps):
                relay_far(s, d, False)
            sided(lambda ds: receive(0, ds), d)
        new = rim + slab + sum(near[d][1] - near[d][0] for d in far_ds[:piece])
        for s in range(steps):
            if s:
                sided(lambda ds: receive(s, ds), *(([0] + near_ds) if piece == 0 else far_ds[piece - 1 : piece]))
            march(s, known, new)
            if piece and s == 0 and piece < len(far_ds):
                relay_far(0, far_ds[piece], False)
            if piece == 0 and s == 0:
                for d in far_ds[1:]:
                    relay_far(0, d, True)
                for later in range(1, steps):
                    for d in far_ds:
                        relay_far(later, d, True)
        known = new
        if piece == 0:
            if groups > 1:
                @pl.when(g != groups - 1)
                def _():
                    pl.semaphore_wait(ready.at[len(levels) + 2], 1)

                @pl.when(g != 0)
                def _():
                    gram_copy(0).wait_recv()

            gram_begin()

    count = f32(parts * slab * ny * nz * tiles)

    group = 4 if krylov % 4 == 0 else 1

    def project(i, carry):
        totals = [jnp.zeros((ny, nz), f32) for _ in range(group)]
        for c in range(parts):
            for x in range(slab):
                field = state[c, pl.ds((rim + x) * ny, ny)]
                for n in range(group):
                    totals[n] = totals[n] + plain[i * group + n, c, x] * field
        for n in range(group):
            rows_k[pl.ds(i * group + n, 1), :] = jnp.sum(totals[n], axis=0, keepdims=True)
        return carry

    lax.fori_loop(0, krylov // group, project, 0)
    ones = jnp.ones((8, nz), f32)
    inner = lax.dot_general(
        ones, rows_k[...], (((1,), (1,)), ((), ())), precision=HIGHEST, preferred_element_type=f32
    )
    own_square = jnp.zeros((ny, nz), f32)
    for c in range(parts):
        for x in range(slab):
            own_square = own_square + state[c, pl.ds((rim + x) * ny, ny)] * state[c, pl.ds((rim + x) * ny, ny)]
    own_square = jnp.sum(jnp.sum(own_square, axis=0, keepdims=True), axis=1, keepdims=True)
    coef_send[...] = jnp.concatenate(
        [inner[0:1], jnp.broadcast_to(own_square, (1, coef_send.shape[1] - krylov))], axis=1
    )
    coef_begin()
    def all_sent(cells, sem):
        pltpu.make_async_copy(cells, cells, sem).wait()

    moved = sum(near[d][1] - near[d][0] for d in sorted(back)[1:])
    spare = held_back if carried else 0
    all_sent(start.at[:, pl.ds(0, 2 * rim - moved - spare)], start_send.at[0])
    if moved + spare:
        @pl.when(t > 0)
        def _():
            all_sent(start.at[:, pl.ds(0, moved + spare)], start_send.at[0])

        @pl.when((t == 0) & (g == groups - 1))
        def _():
            for _ in range(groups):
                all_sent(start.at[:, pl.ds(0, moved)], start_send.at[0])

    if spare:
        @pl.when(t == reach)
        def _():
            all_sent(start.at[:, pl.ds(0, spare)], start_send.at[0])

    for s in range(steps):
        around = 2 * (rim - 3 * s - 1)

        @pl.when(g == s // local)
        def _():
            all_sent(snap.at[s, :, pl.ds(0, around)], snap_send.at[s % local])
            last = spans(slab, rim - 3 * s - 1).get(reach, (0, 0))
            last = last[1] - last[0]
            for other in range(1, groups):
                all_sent(snap.at[s, :, pl.ds(0, slab)], snap_send.at[s % local])
                all_sent(snap.at[s, :, pl.ds(0, around - last)], relay_send.at[s % local])
                if last:
                    @pl.when(crosses(-reach))
                    def _():
                        all_sent(snap.at[s, :, pl.ds(0, last)], snap_send.at[s % local])

                    @pl.when(jnp.logical_not(crosses(reach)))
                    def _():
                        all_sent(snap.at[s, :, pl.ds(0, last)], relay_send.at[s % local])

    gram_drain()

    @pl.when(g == 0)
    def _():
        for other in range(1, groups):
            gram_copy(other).wait_send()

    gram_arrive()
    packed = jnp.sum(gram_all[...], axis=0) / count
    gram = jnp.concatenate(
        [packed[:, n * krylov : (n + 1) * krylov] for n in range(blocks)], axis=0
    )
    same = lax.broadcasted_iota(jnp.int32, gram.shape, 0) == lax.broadcasted_iota(jnp.int32, gram.shape, 1)
    times = functools.partial(jnp.dot, precision=HIGHEST, preferred_element_type=f32)
    twice = jnp.where(same, 2.0, 0.0) - gram
    both = jnp.concatenate([twice, times(twice, gram)], axis=1)
    reach_row = jnp.sum(jnp.abs(gram), axis=0, keepdims=True)
    coef_arrive()
    sums = [jnp.sum(coef_all[n * tiles : (n + 1) * tiles], axis=0) / count for n in range(groups)]
    sums = jnp.concatenate(sums + [jnp.zeros((-groups % 8, sums[0].shape[1]), f32)], axis=0)
    first_rows, work_square = sums[:, :krylov], sums[:, krylov : krylov + 1]
    mixed = times(first_rows, both)
    every, turned = mixed[:, :krylov], mixed[:, krylov:]
    group_row = lax.broadcasted_iota(jnp.int32, work_square.shape, 0)
    own_every = jnp.sum(jnp.where(group_row == g, every, 0.0), axis=0, keepdims=True)
    for k in range(krylov):
        spread[k] = jnp.broadcast_to(own_every[:, k : k + 1], (8, nz))
    linear = 2.0 * every * first_rows
    bent = every * turned
    bound = jnp.abs(linear) + every * every * reach_row
    square = work_square + jnp.sum(bent - linear, axis=1, keepdims=True)
    bound = work_square + jnp.sum(bound, axis=1, keepdims=True)
    margin = jnp.where(group_row < groups, square - cancel_limit * bound, jnp.inf)
    margin_out[...] = jnp.broadcast_to(jnp.min(margin, axis=0, keepdims=True), margin_out.shape)
    square = jnp.sum(jnp.where(group_row == g, square, 0.0), axis=0, keepdims=True)
    square_out[...] = jnp.broadcast_to(square, square_out.shape)
    coef_out[...] = own_every
    for x in range(slab):
        removed = [jnp.zeros((ny // 8, 8, nz), f32) for _ in range(parts)]
        for k in range(krylov):
            factor = spread[k][None]
            for c in range(parts):
                removed[c] = removed[c] + factor * plain[k, c, x].reshape(ny // 8, 8, nz)
        for c in range(parts):
            left_out[0, c, x] = state[c, pl.ds((rim + x) * ny, ny)] - removed[c].reshape(ny, nz)
    coef_drain()


def square_kernel(tiles, left, square_out, send, everyone, ssem, rsem):
    g = lax.axis_index("grp")
    t = lax.axis_index("tile")
    _, parts, slab, ny, nz = left.shape
    barrier = pltpu.get_barrier_semaphore()

    def peer(r):
        return {"grp": g, "tile": lax.rem(t + r, tiles)}

    def greet(r, carry):
        pl.semaphore_signal(barrier, inc=1, device_id=peer(r), device_id_type=MESH)
        return carry

    lax.fori_loop(1, tiles, greet, 0)
    pl.semaphore_wait(barrier, tiles - 1)
    total = jnp.zeros((ny, nz), f32)
    for c in range(parts):
        for x in range(slab):
            total = total + left[0, c, x] * left[0, c, x]
    send[...] = jnp.sum(total, axis=0, keepdims=True)

    def copy(r, sender):
        return pltpu.make_async_remote_copy(
            src_ref=send,
            dst_ref=everyone.at[sender],
            send_sem=ssem.at[r],
            recv_sem=rsem.at[r],
            device_id=peer(r),
            device_id_type=MESH,
        )

    lax.fori_loop(1, tiles, lambda r, c: (copy(r, t).start(), c)[1], 0)
    everyone[t] = send[...]
    lax.fori_loop(
        1, tiles, lambda r, c: (copy(r, lax.rem(t - r + tiles, tiles)).wait_recv(), c)[1], 0
    )
    count = f32(parts * slab * ny * nz * tiles)
    square = jnp.sum(jnp.sum(everyone[...], axis=0), axis=1, keepdims=True) / count
    square_out[...] = jnp.broadcast_to(square, square_out.shape)
    lax.fori_loop(1, tiles, lambda r, c: (copy(r, t).wait_send(), c)[1], 0)


def finish(left, coefs, square, out, coef_out, norm_out, held, norm_row, sem):
    norm = jnp.sqrt(square[...])
    norm_row[...] = norm
    inverse = jnp.broadcast_to(1.0 / norm, left.shape[3:])
    copies = [
        pltpu.make_async_copy(norm_row, norm_out, sem.at[0]),
        pltpu.make_async_copy(coefs, coef_out, sem.at[1]),
    ]
    for c in range(left.shape[1]):
        for x in range(left.shape[2]):
            held[0, c, x] = left[0, c, x] * inverse
    copies.append(pltpu.make_async_copy(held, out, sem.at[2]))
    for copy in copies:
        copy.start()
    for copy in copies:
        copy.wait()


def on_device(groups, tiles, basis, snapshots, coupling):
    krylov, parts, slab, ny, nz = basis.shape
    local, fields = snapshots.shape[:2]
    steps = local * groups
    rim = 3 * steps
    planes = slab + 2 * rim
    count = len(spans(slab, rim))
    blocks, height = gram_blocks(krylov, nz)
    width = -(-(krylov + 1) // nz) * nz
    dma = pltpu.SemaphoreType.DMA
    field = pltpu.VMEM((parts, planes * ny, nz), f32)
    whole = pl.BlockSpec(memory_space=pltpu.VMEM)
    outside = pl.BlockSpec(memory_space=pltpu.HBM)
    results = pl.pallas_call(
        functools.partial(kernel, groups, tiles),
        name="propagate",
        out_shape=(
            jax.ShapeDtypeStruct((1, parts, slab, ny, nz), f32),
            jax.ShapeDtypeStruct((1, krylov), f32),
            jax.ShapeDtypeStruct((1, nz), f32),
            jax.ShapeDtypeStruct((1, nz), f32),
        ),
        in_specs=[outside] * 3,
        out_specs=(whole,) * 4,
        scratch_shapes=[
            pltpu.SMEM(coupling.shape, f32),
            pltpu.VMEM(basis.shape, bf16),
            pltpu.VMEM(basis.shape, f32),
            pltpu.VMEM((parts, planes, ny, nz), bf16),
            pltpu.VMEM((steps, fields, planes, ny, nz), bf16),
            field,
            field,
            field,
            pltpu.VMEM((steps, 12, planes, ny, nz), f32),
            pltpu.VMEM((krylov * ny, krylov * ny), f32),
            pltpu.VMEM((krylov, nz), f32),
            pltpu.VMEM((krylov, 8, nz), f32),
            pltpu.VMEM((height, blocks * krylov), f32),
            pltpu.VMEM((tiles, height, blocks * krylov), f32),
            pltpu.VMEM((1, width), f32),
            pltpu.VMEM((groups * tiles, 1, width), f32),
            dma((3 + local,)),
            dma((1,)),
            dma((count,)),
            dma((local,)),
            dma((local,)),
            dma((steps, count + 1)),
            dma((2,)),
            dma((2,)),
            dma((groups,)),
            dma((1,)),
            pltpu.SemaphoreType.REGULAR((tiles.bit_length() + 3 + -(-rim // slab),)),
        ],
        compiler_params=pltpu.CompilerParams(
            collective_id=0, has_side_effects=True, vmem_limit_bytes=48 << 20
        ),
    )(*(pltpu.with_memory_space_constraint(a, pltpu.HBM) for a in (coupling, basis, snapshots)))
    left, coefs, square, margin = results

    def scaled(left, coefs, square):
        return pl.pallas_call(
            finish,
            name="finish",
            out_shape=tuple(jax.ShapeDtypeStruct(a.shape, f32) for a in (left, coefs, square)),
            in_specs=[whole] * 3,
            out_specs=(outside,) * 3,
            scratch_shapes=[
                pltpu.VMEM(left.shape, f32),
                pltpu.VMEM(square.shape, f32),
                dma((3,)),
            ],
        )(left, coefs, square)

    def summed(left, coefs, square):
        exact = pl.pallas_call(
            functools.partial(square_kernel, tiles),
            name="exact_square",
            out_shape=jax.ShapeDtypeStruct((1, nz), f32),
            in_specs=[whole],
            out_specs=whole,
            scratch_shapes=[
                pltpu.VMEM((1, nz), f32),
                pltpu.VMEM((tiles, 1, nz), f32),
                dma((tiles,)),
                dma((tiles,)),
            ],
            compiler_params=pltpu.CompilerParams(collective_id=1, has_side_effects=True),
        )(left)
        return scaled(left, coefs, exact)

    new_vector, coefs, norms = lax.cond(margin[0, 0] > 0.0, scaled, summed, left, coefs, square)
    return new_vector, coefs, norms[0, :1]


def solution(mesh):
    placed = (P(None, None, "tile", None, None), P("grp", None, "tile", None, None), P())
    return jax.shard_map(
        functools.partial(on_device, mesh.shape["grp"], mesh.shape["tile"]),
        mesh=mesh,
        in_specs=placed,
        out_specs=(P("grp", None, "tile", None, None), P("grp", None), P("grp")),
        check_vma=False,
    )
```

```python
import functools

import jax
import jax.numpy as jnp
from jax import lax
from jax.experimental import pallas as pl
from jax.experimental.pallas import tpu as pltpu
from jax.sharding import PartitionSpec as P

viscosity = 0.5
time_step = 0.3
cancel_limit = 0.01
f32 = jnp.float32
bf16 = jnp.bfloat16
MESH = pl.DeviceIdType.MESH
HIGHEST = lax.Precision.HIGHEST


def spans(slab, rim):
    found = {}
    reach = -(-rim // slab)
    for d in range(1, reach + 1):
        width = min(slab, rim - (d - 1) * slab)
        found[-d] = (slab - width, slab)
        found[d] = (0, width)
    return found


def gram_blocks(krylov, lanes):
    blocks = max(lanes // krylov, 1)
    return (blocks, krylov // blocks) if krylov % (8 * blocks) == 0 else (1, krylov)


def stage(src, old, dst, rates, snap, step, coupling, lo, planes, keep, scale):
    rows, lanes = snap.shape[3], snap.shape[4]
    row = lax.broadcasted_iota(jnp.int32, (rows, lanes), 0)
    top = row == 0
    bottom = row == rows - 1
    mix = [[coupling[k, j] for j in range(5)] for k in range(5)]
    edge = viscosity * time_step

    def cells(field, k, p, shift=0):
        return field[k, pl.ds(p * rows + shift, rows)]

    def make_rates(p):
        base = [snap[step, n, p].astype(f32) for n in range(4)]
        half = [(0.5 * time_step) * base[n] for n in range(3)]
        pull = time_step * base[3]
        found = [edge - half[0], edge + half[0]]
        found += [jnp.where(bottom, 0.0, edge - half[1]), jnp.where(top, 0.0, edge + half[1])]
        found += [edge - half[2], edge + half[2], pull]
        own = 1.0 - 6.0 * edge
        found += [own - pull * mix[k][k] for k in range(5)]
        for n, rate in enumerate(found):
            rates[step, n, p] = rate
        return found

    def body(i, carry):
        p = lo + i
        now = [rates[step, n, p] for n in range(12)] if keep else make_rates(p)
        x_up, x_low, y_up, y_low, z_up, z_low, pull = now[:7]
        center = [cells(src, k, p) for k in range(5)]
        for k in range(5):
            q = center[k]
            others = [j for j in range(5) if j != k]
            coupled = mix[k][others[0]] * center[others[0]]
            for j in others[1:]:
                coupled = coupled + mix[k][j] * center[j]
            total = now[7 + k] * q - pull * coupled
            total = total + (x_up * cells(src, k, p + 1) + x_low * cells(src, k, p - 1))
            total = total + (y_up * cells(src, k, p, 1) + y_low * cells(src, k, p, -1))
            total = total + (z_up * pltpu.roll(q, lanes - 1, 1) + z_low * pltpu.roll(q, 1, 1))
            if keep:
                total = total + keep * cells(old, k, p)
            if scale != 1.0:
                total = total * scale
            dst[k, pl.ds(p * rows, rows)] = total
        return carry

    unroll = max(n for n in range(1, 5) if planes % n == 0)
    lax.fori_loop(0, planes, body, 0, unroll=unroll)


def kernel(
    groups, tiles, coupling_in, basis, snapshots,
    left_out, coef_out, square_out, margin_out,
    coupling, held, plain, start, snap, state, one, two, rates, cross, rows_k, spread,
    gram_send, gram_all, coef_send, coef_all,
    load_sem, start_send, start_recv, snap_send, relay_send, snap_recv,
    share_send, share_recv, pass_send, pass_recv, ready,
):
    g = lax.axis_index("grp")
    t = lax.axis_index("tile")
    krylov, parts, slab, ny, nz = basis.shape
    local = snapshots.shape[0]
    steps = local * groups
    rim = 3 * steps
    planes = slab + 2 * rim
    near = spans(slab, rim)
    offsets = sorted(near)
    position = krylov - groups + g
    levels = [b for b in range(tiles.bit_length() - 1) if (1 << b) in offsets]
    stride = 1 << len(levels)
    length = tiles // stride
    link = t // stride

    def at(group, offset):
        return {"grp": group, "tile": lax.rem(t + (offset % tiles), tiles)}

    def flipped(level):
        bit = 1 << level
        return {"grp": g, "tile": t + bit - 2 * bit * lax.rem(t // bit, 2)}

    def partner(other):
        return {"grp": lax.rem(g + other, groups), "tile": t}

    barrier = pltpu.get_barrier_semaphore()
    reach = max(offsets)

    def crosses(d):
        return t + d >= tiles if d > 0 else t + d < 0

    def greet(peer):
        pl.semaphore_signal(barrier, inc=1, device_id=peer, device_id_type=MESH)

    greeters = groups - 1
    for d in sorted(offsets, key=abs, reverse=True):
        if d > 0:
            greet(at(g, -d))
            greeters = greeters + 1 + jnp.where(crosses(d), groups - 1, 0)

            @pl.when(crosses(-d))
            def _():
                for other in range(1, groups):
                    greet(at(lax.rem(g + other, groups), -d))
        else:
            pl.when(jnp.logical_not(crosses(-d)))(functools.partial(greet, at(g, -d)))
            greeters = greeters + jnp.where(crosses(d), 0, 1)
    held_back = near[reach][1] - near[reach][0]
    carried = reach > 1 and held_back < slab and 2 * reach < tiles
    if carried:
        pl.when(t == reach)(functools.partial(greet, {"grp": g, "tile": tiles - 1}))
        greeters = greeters + jnp.where(t == tiles - 1, 1, 0)
    for other in range(1, groups):
        greet(partner(other))
    for way in (1, -1):
        last = link == (length - 1 if way > 0 else 0)
        greeters = greeters + jnp.where(last, 0, 1)

        @pl.when(jnp.logical_not(last))
        def _():
            greet(at(g, way * stride))

    chunk = 8 if krylov % 8 == 0 else 1
    own = pltpu.make_async_copy(basis.at[position], start.at[:, pl.ds(rim, slab)], load_sem.at[0])
    own.start()
    mix = pltpu.make_async_copy(coupling_in, coupling, load_sem.at[1])
    mix.start()
    for n in range(krylov // chunk):
        part = pl.ds(n * chunk, chunk)
        pltpu.make_async_copy(basis.at[part], held.at[part], load_sem.at[2]).start()

    def target(d, first, last):
        return pl.ds(rim + d * slab + first, last - first)

    start_copies = []
    for n, d in enumerate(offsets):
        first, last = near[d]
        start_copies.append(
            pltpu.make_async_remote_copy(
                src_ref=basis.at[position, :, pl.ds(first, last - first)],
                dst_ref=start.at[:, target(d, first, last)],
                send_sem=start_send.at[0],
                recv_sem=start_recv.at[n],
                device_id=at(g, -d),
                device_id_type=MESH,
            )
        )

    def snap_copy(s, n, d, other):
        first, last = (0, slab) if d == 0 else spans(slab, rim - 3 * s - 1)[d]
        return pltpu.make_async_remote_copy(
            src_ref=snapshots.at[s % local, :, pl.ds(first, last - first)],
            dst_ref=snap.at[s, :, target(d, first, last)],
            send_sem=snap_send.at[s % local],
            recv_sem=snap_recv.at[s, n],
            device_id=at(lax.rem(g + other, groups), -d),
            device_id_type=MESH,
        )

    def local_snap(s):
        return pltpu.make_async_copy(
            snapshots.at[s % local], snap.at[s, :, pl.ds(rim, slab)], load_sem.at[3 + s % local]
        )

    def snap_offsets(s):
        inside = spans(slab, rim - 3 * s - 1)
        return [(n, d) for n, d in enumerate([0] + offsets) if d == 0 or d in inside]

    def snap_each(s, ds, act):
        inside = {d: n for n, d in snap_offsets(s)}

        @pl.when(g == s // local)
        def _():
            for d in ds:
                if d in inside:
                    for other in range(1 if d else groups):
                        if d or other:
                            act(snap_copy(s, inside[d], d, other))
                    if d == reach:
                        @pl.when(crosses(-d))
                        def _():
                            for other in range(1, groups):
                                act(snap_copy(s, inside[d], d, other))

    def relay_copy(s, n, d, other):
        first, last = spans(slab, rim - 3 * s - 1)[d]
        cells = snap.at[s, :, target(d, first, last)]
        return pltpu.make_async_remote_copy(
            src_ref=cells,
            dst_ref=cells,
            send_sem=relay_send.at[s % local],
            recv_sem=snap_recv.at[s, n],
            device_id=at(lax.rem(g + other, groups), 0),
            device_id_type=MESH,
        )

    def relay(s, ds):
        @pl.when(g == s // local)
        def _():
            for n, d in snap_offsets(s):
                if d and d in ds:
                    snap_copy(s, n, d, 0).wait_recv()

                    def forward():
                        for other in range(1, groups):
                            relay_copy(s, n, d, other).start()

                    if d == reach:
                        pl.when(jnp.logical_not(crosses(d)))(forward)
                    else:
                        forward()
            if 0 in ds:
                local_snap(s).wait()

    def receive(s, ds):
        if groups > 1:
            @pl.when(g != s // local)
            def _():
                for n, d in snap_offsets(s):
                    if d in ds:
                        (relay_copy if d else snap_copy)(s, n, d, 1).wait_recv()

    for s in range(steps):
        @pl.when(g == s // local)
        def _():
            local_snap(s).start()

    pl.semaphore_wait(barrier, greeters)
    def send(s, ds):
        snap_each(s, ds, lambda copy: copy.start())
        if s == 0:
            for d in ds:
                if d:
                    start_copies[offsets.index(d)].start()

    def tell(n, peer):
        pl.semaphore_signal(ready.at[n], inc=1, device_id=peer, device_id_type=MESH)

    edge = len(levels) + 3

    for d in offsets:
        if d < 0:
            @pl.when(crosses(-d))
            def _():
                for other in range(groups):
                    tell(edge - d - 1, at(lax.rem(g + other, groups), -d))

    upper = t >= tiles // 2
    ahead = [d for d in offsets if d < 0]
    back = [-d for d in ahead]

    def send_some(s, soon):
        for d in sorted(offsets, key=abs):
            wanted = t - d >= tiles // 2 if d < 0 else t - d < tiles // 2
            wanted = wanted if soon else jnp.logical_not(wanted)
            if d > 0:
                wanted = wanted & jnp.logical_not(crosses(-d))
            pl.when(wanted)(functools.partial(send, s, [d]))

    def sided(act, *ds):
        for way, on in ((1, upper), (-1, jnp.logical_not(upper))):
            @pl.when(on)
            def _():
                act([way * d for d in ds])

    near_ds, far_ds = sorted(ahead, key=abs), sorted(back)

    turn = edge + len(back)
    if carried:
        pl.when(t == tiles - 1)(functools.partial(tell, turn, {"grp": g, "tile": reach}))

    def wait_far(d):
        pl.semaphore_wait(ready.at[edge + d - 1], groups)

    def start_copy(d, group, last):
        first = near[d][0]
        return pltpu.make_async_remote_copy(
            src_ref=basis.at[krylov - groups + group, :, pl.ds(first, last - first)],
            dst_ref=start.at[:, target(d, first, last)],
            send_sem=start_send.at[0],
            recv_sem=start_recv.at[offsets.index(d)],
            device_id=at(group, -d),
            device_id_type=MESH,
        )

    def send_first():
        wait_far(1)
        snap_each(0, [1], lambda copy: copy.start())
        start_copy(1, g, slab - held_back if carried else slab).start()
        for s in range(1, steps):
            send(s, [1])
        for d in sorted(back)[1:]:
            wait_far(d)
            for s in range(steps):
                snap_each(s, [d], lambda copy: copy.start())

    def send_second():
        for d in sorted(back)[1:]:
            for group in range(groups):
                start_copy(d, group, near[d][1]).start()

    def send_carried():
        start_copies[offsets.index(-reach)].wait_recv()
        pl.semaphore_wait(ready.at[turn], 1)
        pltpu.make_async_remote_copy(
            src_ref=start.at[:, target(-reach, slab - held_back, slab)],
            dst_ref=start.at[:, target(1, slab - held_back, slab)],
            send_sem=start_send.at[0],
            recv_sem=start_recv.at[offsets.index(1)],
            device_id={"grp": g, "tile": tiles - 1},
            device_id_type=MESH,
        ).start()

    def send_late():
        for d in sorted(back)[1:]:
            @pl.when((t > 0) & crosses(-d))
            def _():
                wait_far(d)
                for s in range(steps):
                    send(s, [d])

    for s in range(steps):
        snap_each(s, [0], lambda copy: copy.start())
        send_some(s, True)

    def send_far():
        for s in range(steps):
            send_some(s, False)

    pl.when(t == 0)(send_far)

    def flip_step(n):
        if n:
            pl.semaphore_wait(ready.at[n - 1], 1)
        if n < len(levels):
            tell(n, flipped(levels[n]))

    def pass_on(sem, way):
        head = link == (0 if way > 0 else length - 1)
        tail = link == (length - 1 if way > 0 else 0)

        @pl.when(jnp.logical_not(head))
        def _():
            pl.semaphore_wait(ready.at[sem], 1)

        @pl.when(jnp.logical_not(tail))
        def _():
            tell(sem, at(g, way * stride))

    def chain_step(n):
        if length > 1:
            upper = link >= length // 2
            for way in (1, -1):
                @pl.when(upper == (way < 0))
                def _():
                    mine = -way if n else way
                    pass_on(len(levels) + (mine < 0), mine)

    def tell_group():
        for other in range(1, groups):
            tell(len(levels) + 2, partner(other))

    pltpu.make_async_copy(basis, held, load_sem.at[2]).wait()

    def expand(k, carry):
        plain[k] = held[k].astype(f32)
        return carry

    lax.fori_loop(0, krylov, expand, 0)
    size = krylov * ny
    blocks, height = gram_blocks(krylov, nz)

    def gram_copy(other):
        return pltpu.make_async_remote_copy(
            src_ref=gram_send,
            dst_ref=gram_send,
            send_sem=pass_send.at[other],
            recv_sem=pass_recv.at[0],
            device_id=partner(other),
            device_id_type=MESH,
        )

    @pl.when(g == 0)
    def _():
        for c in range(parts):
            wide = jnp.concatenate([held[:, c, x].reshape(size, nz) for x in range(slab)], axis=1)
            piece = lax.dot_general(wide, wide, (((1,), (1,)), ((), ())), preferred_element_type=f32)
            cross[...] = cross[...] + piece if c else piece
            if c == parts // 2:
                pl.when(t > 0)(send_far)
        line = lax.broadcasted_iota(jnp.int32, (size, size), 0)
        column = lax.broadcasted_iota(jnp.int32, (size, size), 1)
        kept = jnp.where(lax.rem(line, ny) == lax.rem(column, ny), cross[...], 0.0)
        kept = jnp.sum(kept.reshape(krylov, ny, size), axis=1)
        pick = (
            lax.broadcasted_iota(jnp.int32, (size, krylov), 0) // ny
            == lax.broadcasted_iota(jnp.int32, (size, krylov), 1)
        ).astype(f32)
        gram = jnp.dot(kept, pick, precision=HIGHEST, preferred_element_type=f32)
        gram_send[...] = jnp.concatenate(
            [gram[n * height : (n + 1) * height] for n in range(blocks)], axis=1
        )
        for other in range(1, groups):
            gram_copy(other).start()

    @pl.when(g == groups - 1)
    def _():
        for n in range(len(levels) + 1):
            flip_step(n)

    pl.when((t > 0) & (g != 0))(send_far)

    @pl.when(g == groups - 1)
    def _():
        chain_step(0)

    pl.when(t == 0)(send_first)
    send_late()
    if carried:
        pl.when(t == reach)(send_carried)
    @pl.when(g == groups - 1)
    def _():
        chain_step(1)
        for other in range(1, groups):
            tell(len(levels) + 2, partner(other))

    def spread_out(n, send, everyone, reached):
        way = 2 * (t // max(tiles // 2, 1)) - 1
        others = everyone.at[pl.ds(0, reached * tiles - 1)]
        place = t if reached == 1 else g * tiles + t

        def begin():
            def one(i, carry):
                peer = lax.rem(2 * tiles - 1 - t + way * i, tiles)

                def to(other):
                    pltpu.make_async_remote_copy(
                        src_ref=send,
                        dst_ref=everyone.at[place],
                        send_sem=share_send.at[n],
                        recv_sem=share_recv.at[n],
                        device_id={"grp": lax.rem(g + other, groups), "tile": peer},
                        device_id_type=MESH,
                    ).start()

                pl.when(peer != t)(functools.partial(to, 0))
                for other in range(1, reached):
                    to(other)
                return carry

            lax.fori_loop(0, tiles, one, 0)
            everyone[place] = send[...]

        def arrive():
            pltpu.make_async_copy(others, others, share_recv.at[n]).wait()

        def drain():
            pltpu.make_async_copy(others, others, share_send.at[n]).wait()

        return begin, arrive, drain

    gram_begin, gram_arrive, gram_drain = spread_out(0, gram_send, gram_all, 1)
    coef_begin, coef_arrive, coef_drain = spread_out(1, coef_send, coef_all, groups)
    def widen(d):
        def one(p, carry):
            for k in range(parts):
                state[k, pl.ds(p * ny, ny)] = start[k, p].astype(f32)
            return carry

        lo, width = (rim, slab) if d == 0 else (rim + d * slab + near[d][0], near[d][1] - near[d][0])
        lax.fori_loop(lo, lo + width, one, 0)

    def arrive(ds):
        for d in ds:
            if d == -reach and carried:
                pl.when(t != reach)(start_copies[offsets.index(d)].wait_recv)
            elif d:
                start_copies[offsets.index(d)].wait_recv()
            else:
                own.wait()
                mix.wait()
            widen(d)

    keeps = (0.0, 3.0, 2.0)
    ways = ((state, one), (one, two), (two, state))

    def march(s, known, new):
        for n, (src, dst) in enumerate(ways):
            k = 3 * s + n + 1
            lo, hi = max(k, known - k), new - k
            if hi > lo:
                first = jnp.where(upper, lo, planes - hi)
                scale = 6.0 ** -steps if k == 3 * steps else 1.0
                stage(src, state, dst, rates, snap, s, coupling, first, hi - lo, keeps[n], scale)

    def relay_far(s, d, early):
        for way, on in ((1, upper), (-1, jnp.logical_not(upper))):
            seam = crosses(way * d)

            @pl.when(on & (jnp.logical_not(seam) if early else seam))
            def _():
                relay(s, [way * d])

    sided(lambda ds: relay(0, [0] + ds), *near_ds)
    sided(arrive, *near_ds)
    arrive([0])
    for s in range(1, steps):
        sided(lambda ds: relay(s, [0] + ds), *near_ds)
    sided(lambda ds: receive(0, [0] + ds), *near_ds)
    pl.when((t == 0) & (g == groups - 1))(send_second)
    known = 0
    for far in (False, True):
        if far:
            for d in far_ds:
                relay_far(0, d, False)
            sided(arrive, *far_ds)
            for s in range(1, steps):
                for d in far_ds:
                    relay_far(s, d, False)
            sided(lambda ds: receive(0, ds), *far_ds)
        new = planes if far else rim + slab
        for s in range(steps):
            if s:
                sided(lambda ds: receive(s, ds), *(far_ds if far else [0] + near_ds))
            march(s, known, new)
            if not far and s == 0:
                for d in far_ds:
                    relay_far(0, d, True)
                for later in range(1, steps):
                    for d in far_ds:
                        relay_far(later, d, True)
        known = new
        if not far:
            if groups > 1:
                @pl.when(g != groups - 1)
                def _():
                    pl.semaphore_wait(ready.at[len(levels) + 2], 1)

                @pl.when(g != 0)
                def _():
                    gram_copy(0).wait_recv()

            gram_begin()

    count = f32(parts * slab * ny * nz * tiles)

    group = 8 if krylov % 8 == 0 else 1

    def project(i, carry):
        totals = [jnp.zeros((ny, nz), f32) for _ in range(group)]
        for c in range(parts):
            for x in range(slab):
                field = state[c, pl.ds((rim + x) * ny, ny)]
                for n in range(group):
                    totals[n] = totals[n] + plain[i * group + n, c, x] * field
        for n in range(group):
            rows_k[pl.ds(i * group + n, 1), :] = jnp.sum(totals[n], axis=0, keepdims=True)
        return carry

    lax.fori_loop(0, krylov // group, project, 0)
    ones = jnp.ones((8, nz), f32)
    inner = lax.dot_general(
        ones, rows_k[...], (((1,), (1,)), ((), ())), precision=HIGHEST, preferred_element_type=f32
    )
    own_square = jnp.zeros((ny, nz), f32)
    for c in range(parts):
        for x in range(slab):
            own_square = own_square + state[c, pl.ds((rim + x) * ny, ny)] * state[c, pl.ds((rim + x) * ny, ny)]
    own_square = jnp.sum(jnp.sum(own_square, axis=0, keepdims=True), axis=1, keepdims=True)
    coef_send[...] = jnp.concatenate(
        [inner[0:1], jnp.broadcast_to(own_square, (1, coef_send.shape[1] - krylov))], axis=1
    )
    coef_begin()
    def all_sent(cells, sem):
        pltpu.make_async_copy(cells, cells, sem).wait()

    moved = sum(near[d][1] - near[d][0] for d in sorted(back)[1:])
    spare = held_back if carried else 0
    all_sent(start.at[:, pl.ds(0, 2 * rim - moved - spare)], start_send.at[0])
    if moved + spare:
        @pl.when(t > 0)
        def _():
            all_sent(start.at[:, pl.ds(0, moved + spare)], start_send.at[0])

        @pl.when((t == 0) & (g == groups - 1))
        def _():
            for _ in range(groups):
                all_sent(start.at[:, pl.ds(0, moved)], start_send.at[0])

    if spare:
        @pl.when(t == reach)
        def _():
            all_sent(start.at[:, pl.ds(0, spare)], start_send.at[0])

    for s in range(steps):
        around = 2 * (rim - 3 * s - 1)

        @pl.when(g == s // local)
        def _():
            all_sent(snap.at[s, :, pl.ds(0, around)], snap_send.at[s % local])
            last = spans(slab, rim - 3 * s - 1).get(reach, (0, 0))
            last = last[1] - last[0]
            for other in range(1, groups):
                all_sent(snap.at[s, :, pl.ds(0, slab)], snap_send.at[s % local])
                all_sent(snap.at[s, :, pl.ds(0, around - last)], relay_send.at[s % local])
                if last:
                    @pl.when(crosses(-reach))
                    def _():
                        all_sent(snap.at[s, :, pl.ds(0, last)], snap_send.at[s % local])

                    @pl.when(jnp.logical_not(crosses(reach)))
                    def _():
                        all_sent(snap.at[s, :, pl.ds(0, last)], relay_send.at[s % local])

    gram_drain()

    @pl.when(g == 0)
    def _():
        for other in range(1, groups):
            gram_copy(other).wait_send()

    gram_arrive()
    packed = jnp.sum(gram_all[...], axis=0) / count
    gram = jnp.concatenate(
        [packed[:, n * krylov : (n + 1) * krylov] for n in range(blocks)], axis=0
    )
    same = lax.broadcasted_iota(jnp.int32, gram.shape, 0) == lax.broadcasted_iota(jnp.int32, gram.shape, 1)
    times = functools.partial(jnp.dot, precision=HIGHEST, preferred_element_type=f32)
    twice = jnp.where(same, 2.0, 0.0) - gram
    both = jnp.concatenate([twice, times(twice, gram)], axis=1)
    reach_row = jnp.sum(jnp.abs(gram), axis=0, keepdims=True)
    coef_arrive()
    sums = [jnp.sum(coef_all[n * tiles : (n + 1) * tiles], axis=0) / count for n in range(groups)]
    sums = jnp.concatenate(sums + [jnp.zeros((-groups % 8, sums[0].shape[1]), f32)], axis=0)
    first_rows, work_square = sums[:, :krylov], sums[:, krylov : krylov + 1]
    mixed = times(first_rows, both)
    every, turned = mixed[:, :krylov], mixed[:, krylov:]
    group_row = lax.broadcasted_iota(jnp.int32, work_square.shape, 0)
    own_every = jnp.sum(jnp.where(group_row == g, every, 0.0), axis=0, keepdims=True)
    for k in range(krylov):
        spread[k] = jnp.broadcast_to(own_every[:, k : k + 1], (8, nz))
    linear = 2.0 * every * first_rows
    bent = every * turned
    bound = jnp.abs(linear) + every * every * reach_row
    square = work_square + jnp.sum(bent - linear, axis=1, keepdims=True)
    bound = work_square + jnp.sum(bound, axis=1, keepdims=True)
    margin = jnp.where(group_row < groups, square - cancel_limit * bound, jnp.inf)
    margin_out[...] = jnp.broadcast_to(jnp.min(margin, axis=0, keepdims=True), margin_out.shape)
    square = jnp.sum(jnp.where(group_row == g, square, 0.0), axis=0, keepdims=True)
    square_out[...] = jnp.broadcast_to(square, square_out.shape)
    coef_out[...] = own_every
    for x in range(slab):
        removed = [jnp.zeros((ny // 8, 8, nz), f32) for _ in range(parts)]
        for k in range(krylov):
            factor = spread[k][None]
            for c in range(parts):
                removed[c] = removed[c] + factor * plain[k, c, x].reshape(ny // 8, 8, nz)
        for c in range(parts):
            left_out[0, c, x] = state[c, pl.ds((rim + x) * ny, ny)] - removed[c].reshape(ny, nz)
    coef_drain()


def square_kernel(tiles, left, square_out, send, everyone, ssem, rsem):
    g = lax.axis_index("grp")
    t = lax.axis_index("tile")
    _, parts, slab, ny, nz = left.shape
    barrier = pltpu.get_barrier_semaphore()

    def peer(r):
        return {"grp": g, "tile": lax.rem(t + r, tiles)}

    def greet(r, carry):
        pl.semaphore_signal(barrier, inc=1, device_id=peer(r), device_id_type=MESH)
        return carry

    lax.fori_loop(1, tiles, greet, 0)
    pl.semaphore_wait(barrier, tiles - 1)
    total = jnp.zeros((ny, nz), f32)
    for c in range(parts):
        for x in range(slab):
            total = total + left[0, c, x] * left[0, c, x]
    send[...] = jnp.sum(total, axis=0, keepdims=True)

    def copy(r, sender):
        return pltpu.make_async_remote_copy(
            src_ref=send,
            dst_ref=everyone.at[sender],
            send_sem=ssem.at[r],
            recv_sem=rsem.at[r],
            device_id=peer(r),
            device_id_type=MESH,
        )

    lax.fori_loop(1, tiles, lambda r, c: (copy(r, t).start(), c)[1], 0)
    everyone[t] = send[...]
    lax.fori_loop(
        1, tiles, lambda r, c: (copy(r, lax.rem(t - r + tiles, tiles)).wait_recv(), c)[1], 0
    )
    count = f32(parts * slab * ny * nz * tiles)
    square = jnp.sum(jnp.sum(everyone[...], axis=0), axis=1, keepdims=True) / count
    square_out[...] = jnp.broadcast_to(square, square_out.shape)
    lax.fori_loop(1, tiles, lambda r, c: (copy(r, t).wait_send(), c)[1], 0)


def finish(left, coefs, square, out, coef_out, norm_out, held, norm_row, sem):
    norm = jnp.sqrt(square[...])
    norm_row[...] = norm
    inverse = jnp.broadcast_to(1.0 / norm, left.shape[3:])
    copies = [
        pltpu.make_async_copy(norm_row, norm_out, sem.at[0]),
        pltpu.make_async_copy(coefs, coef_out, sem.at[1]),
    ]
    for c in range(left.shape[1]):
        for x in range(left.shape[2]):
            held[0, c, x] = left[0, c, x] * inverse
    copies.append(pltpu.make_async_copy(held, out, sem.at[2]))
    for copy in copies:
        copy.start()
    for copy in copies:
        copy.wait()


def on_device(groups, tiles, basis, snapshots, coupling):
    krylov, parts, slab, ny, nz = basis.shape
    local, fields = snapshots.shape[:2]
    steps = local * groups
    rim = 3 * steps
    planes = slab + 2 * rim
    count = len(spans(slab, rim))
    blocks, height = gram_blocks(krylov, nz)
    width = -(-(krylov + 1) // nz) * nz
    dma = pltpu.SemaphoreType.DMA
    field = pltpu.VMEM((parts, planes * ny, nz), f32)
    whole = pl.BlockSpec(memory_space=pltpu.VMEM)
    outside = pl.BlockSpec(memory_space=pltpu.HBM)
    results = pl.pallas_call(
        functools.partial(kernel, groups, tiles),
        name="propagate",
        out_shape=(
            jax.ShapeDtypeStruct((1, parts, slab, ny, nz), f32),
            jax.ShapeDtypeStruct((1, krylov), f32),
            jax.ShapeDtypeStruct((1, nz), f32),
            jax.ShapeDtypeStruct((1, nz), f32),
        ),
        in_specs=[outside] * 3,
        out_specs=(whole,) * 4,
        scratch_shapes=[
            pltpu.SMEM(coupling.shape, f32),
            pltpu.VMEM(basis.shape, bf16),
            pltpu.VMEM(basis.shape, f32),
            pltpu.VMEM((parts, planes, ny, nz), bf16),
            pltpu.VMEM((steps, fields, planes, ny, nz), bf16),
            field,
            field,
            field,
            pltpu.VMEM((steps, 12, planes, ny, nz), f32),
            pltpu.VMEM((krylov * ny, krylov * ny), f32),
            pltpu.VMEM((krylov, nz), f32),
            pltpu.VMEM((krylov, 8, nz), f32),
            pltpu.VMEM((height, blocks * krylov), f32),
            pltpu.VMEM((tiles, height, blocks * krylov), f32),
            pltpu.VMEM((1, width), f32),
            pltpu.VMEM((groups * tiles, 1, width), f32),
            dma((3 + local,)),
            dma((1,)),
            dma((count,)),
            dma((local,)),
            dma((local,)),
            dma((steps, count + 1)),
            dma((2,)),
            dma((2,)),
            dma((groups,)),
            dma((1,)),
            pltpu.SemaphoreType.REGULAR((tiles.bit_length() + 3 + -(-rim // slab),)),
        ],
        compiler_params=pltpu.CompilerParams(
            collective_id=0, has_side_effects=True, vmem_limit_bytes=48 << 20
        ),
    )(*(pltpu.with_memory_space_constraint(a, pltpu.HBM) for a in (coupling, basis, snapshots)))
    left, coefs, square, margin = results

    def scaled(left, coefs, square):
        return pl.pallas_call(
            finish,
            name="finish",
            out_shape=tuple(jax.ShapeDtypeStruct(a.shape, f32) for a in (left, coefs, square)),
            in_specs=[whole] * 3,
            out_specs=(outside,) * 3,
            scratch_shapes=[
                pltpu.VMEM(left.shape, f32),
                pltpu.VMEM(square.shape, f32),
                dma((3,)),
            ],
        )(left, coefs, square)

    def summed(left, coefs, square):
        exact = pl.pallas_call(
            functools.partial(square_kernel, tiles),
            name="exact_square",
            out_shape=jax.ShapeDtypeStruct((1, nz), f32),
            in_specs=[whole],
            out_specs=whole,
            scratch_shapes=[
                pltpu.VMEM((1, nz), f32),
                pltpu.VMEM((tiles, 1, nz), f32),
                dma((tiles,)),
                dma((tiles,)),
            ],
            compiler_params=pltpu.CompilerParams(collective_id=1, has_side_effects=True),
        )(left)
        return scaled(left, coefs, exact)

    new_vector, coefs, norms = lax.cond(margin[0, 0] > 0.0, scaled, summed, left, coefs, square)
    return new_vector, coefs, norms[0, :1]


def solution(mesh):
    placed = (P(None, None, "tile", None, None), P("grp", None, "tile", None, None), P())
    return jax.shard_map(
        functools.partial(on_device, mesh.shape["grp"], mesh.shape["tile"]),
        mesh=mesh,
        in_specs=placed,
        out_specs=(P("grp", None, "tile", None, None), P("grp", None), P("grp")),
        check_vma=False,
    )
```

```python
import functools

import jax
import jax.numpy as jnp
from jax import lax
from jax.experimental import pallas as pl
from jax.experimental.pallas import tpu as pltpu
from jax.sharding import PartitionSpec as P

viscosity = 0.5
time_step = 0.3
cancel_limit = 0.01
f32 = jnp.float32
bf16 = jnp.bfloat16
MESH = pl.DeviceIdType.MESH
HIGHEST = lax.Precision.HIGHEST


def spans(slab, rim):
    found = {}
    reach = -(-rim // slab)
    for d in range(1, reach + 1):
        width = min(slab, rim - (d - 1) * slab)
        found[-d] = (slab - width, slab)
        found[d] = (0, width)
    return found


def gram_blocks(krylov, lanes):
    blocks = max(lanes // krylov, 1)
    return (blocks, krylov // blocks) if krylov % (8 * blocks) == 0 else (1, krylov)


def stage(src, old, dst, rates, snap, step, coupling, lo, planes, keep, scale):
    rows, lanes = snap.shape[3], snap.shape[4]
    row = lax.broadcasted_iota(jnp.int32, (rows, lanes), 0)
    top = row == 0
    bottom = row == rows - 1
    mix = [[coupling[k, j] for j in range(5)] for k in range(5)]
    edge = viscosity * time_step

    def cells(field, k, p, shift=0):
        return field[k, pl.ds(p * rows + shift, rows)]

    def make_rates(p):
        base = [snap[step, n, p].astype(f32) for n in range(4)]
        half = [(0.5 * time_step) * base[n] for n in range(3)]
        pull = time_step * base[3]
        found = [edge - half[0], edge + half[0]]
        found += [jnp.where(bottom, 0.0, edge - half[1]), jnp.where(top, 0.0, edge + half[1])]
        found += [edge - half[2], edge + half[2], pull]
        own = 1.0 - 6.0 * edge
        found += [own - pull * mix[k][k] for k in range(5)]
        for n, rate in enumerate(found):
            rates[step, n, p] = rate
        return found

    def body(i, carry):
        p = lo + i
        now = [rates[step, n, p] for n in range(12)] if keep else make_rates(p)
        x_up, x_low, y_up, y_low, z_up, z_low, pull = now[:7]
        center = [cells(src, k, p) for k in range(5)]
        for k in range(5):
            q = center[k]
            others = [j for j in range(5) if j != k]
            coupled = mix[k][others[0]] * center[others[0]]
            for j in others[1:]:
                coupled = coupled + mix[k][j] * center[j]
            total = now[7 + k] * q - pull * coupled
            total = total + (x_up * cells(src, k, p + 1) + x_low * cells(src, k, p - 1))
            total = total + (y_up * cells(src, k, p, 1) + y_low * cells(src, k, p, -1))
            total = total + (z_up * pltpu.roll(q, lanes - 1, 1) + z_low * pltpu.roll(q, 1, 1))
            if keep:
                total = total + keep * cells(old, k, p)
            if scale != 1.0:
                total = total * scale
            dst[k, pl.ds(p * rows, rows)] = total
        return carry

    unroll = max(n for n in range(1, 9) if planes % n == 0)
    lax.fori_loop(0, planes, body, 0, unroll=unroll)


def kernel(
    groups, tiles, coupling_in, basis, snapshots,
    left_out, coef_out, square_out, margin_out,
    coupling, held, plain, start, snap, state, one, two, rates, cross, rows_k, spread,
    gram_send, gram_all, coef_send, coef_all,
    load_sem, start_send, start_recv, snap_send, relay_send, snap_recv,
    share_send, share_recv, pass_send, pass_recv, ready,
):
    g = lax.axis_index("grp")
    t = lax.axis_index("tile")
    krylov, parts, slab, ny, nz = basis.shape
    local = snapshots.shape[0]
    steps = local * groups
    rim = 3 * steps
    planes = slab + 2 * rim
    near = spans(slab, rim)
    offsets = sorted(near)
    position = krylov - groups + g
    levels = [b for b in range(tiles.bit_length() - 1) if (1 << b) in offsets]
    stride = 1 << len(levels)
    length = tiles // stride
    link = t // stride

    def at(group, offset):
        return {"grp": group, "tile": lax.rem(t + (offset % tiles), tiles)}

    def flipped(level):
        bit = 1 << level
        return {"grp": g, "tile": t + bit - 2 * bit * lax.rem(t // bit, 2)}

    def partner(other):
        return {"grp": lax.rem(g + other, groups), "tile": t}

    barrier = pltpu.get_barrier_semaphore()
    reach = max(offsets)

    def crosses(d):
        return t + d >= tiles if d > 0 else t + d < 0

    def greet(peer):
        pl.semaphore_signal(barrier, inc=1, device_id=peer, device_id_type=MESH)

    greeters = groups - 1
    for d in sorted(offsets, key=abs, reverse=True):
        if d > 0:
            greet(at(g, -d))
            greeters = greeters + 1 + jnp.where(crosses(d), groups - 1, 0)

            @pl.when(crosses(-d))
            def _():
                for other in range(1, groups):
                    greet(at(lax.rem(g + other, groups), -d))
        else:
            pl.when(jnp.logical_not(crosses(-d)))(functools.partial(greet, at(g, -d)))
            greeters = greeters + jnp.where(crosses(d), 0, 1)
    held_back = near[reach][1] - near[reach][0]
    carried = reach > 1 and held_back < slab and 2 * reach < tiles
    if carried:
        pl.when(t == reach)(functools.partial(greet, {"grp": g, "tile": tiles - 1}))
        greeters = greeters + jnp.where(t == tiles - 1, 1, 0)
    for other in range(1, groups):
        greet(partner(other))
    for way in (1, -1):
        last = link == (length - 1 if way > 0 else 0)
        greeters = greeters + jnp.where(last, 0, 1)

        @pl.when(jnp.logical_not(last))
        def _():
            greet(at(g, way * stride))

    chunk = 8 if krylov % 8 == 0 else 1
    own = pltpu.make_async_copy(basis.at[position], start.at[:, pl.ds(rim, slab)], load_sem.at[0])
    own.start()
    mix = pltpu.make_async_copy(coupling_in, coupling, load_sem.at[1])
    mix.start()
    for n in range(krylov // chunk):
        part = pl.ds(n * chunk, chunk)
        pltpu.make_async_copy(basis.at[part], held.at[part], load_sem.at[2]).start()

    def target(d, first, last):
        return pl.ds(rim + d * slab + first, last - first)

    start_copies = []
    for n, d in enumerate(offsets):
        first, last = near[d]
        start_copies.append(
            pltpu.make_async_remote_copy(
                src_ref=basis.at[position, :, pl.ds(first, last - first)],
                dst_ref=start.at[:, target(d, first, last)],
                send_sem=start_send.at[0],
                recv_sem=start_recv.at[n],
                device_id=at(g, -d),
                device_id_type=MESH,
            )
        )

    def snap_copy(s, n, d, other):
        first, last = (0, slab) if d == 0 else spans(slab, rim - 3 * s - 1)[d]
        return pltpu.make_async_remote_copy(
            src_ref=snapshots.at[s % local, :, pl.ds(first, last - first)],
            dst_ref=snap.at[s, :, target(d, first, last)],
            send_sem=snap_send.at[s % local],
            recv_sem=snap_recv.at[s, n],
            device_id=at(lax.rem(g + other, groups), -d),
            device_id_type=MESH,
        )

    def local_snap(s):
        return pltpu.make_async_copy(
            snapshots.at[s % local], snap.at[s, :, pl.ds(rim, slab)], load_sem.at[3 + s % local]
        )

    def snap_offsets(s):
        inside = spans(slab, rim - 3 * s - 1)
        return [(n, d) for n, d in enumerate([0] + offsets) if d == 0 or d in inside]

    def snap_each(s, ds, act):
        inside = {d: n for n, d in snap_offsets(s)}

        @pl.when(g == s // local)
        def _():
            for d in ds:
                if d in inside:
                    for other in range(1 if d else groups):
                        if d or other:
                            act(snap_copy(s, inside[d], d, other))
                    if d == reach:
                        @pl.when(crosses(-d))
                        def _():
                            for other in range(1, groups):
                                act(snap_copy(s, inside[d], d, other))

    def relay_copy(s, n, d, other):
        first, last = spans(slab, rim - 3 * s - 1)[d]
        cells = snap.at[s, :, target(d, first, last)]
        return pltpu.make_async_remote_copy(
            src_ref=cells,
            dst_ref=cells,
            send_sem=relay_send.at[s % local],
            recv_sem=snap_recv.at[s, n],
            device_id=at(lax.rem(g + other, groups), 0),
            device_id_type=MESH,
        )

    def relay(s, ds):
        @pl.when(g == s // local)
        def _():
            for n, d in snap_offsets(s):
                if d and d in ds:
                    snap_copy(s, n, d, 0).wait_recv()

                    def forward():
                        for other in range(1, groups):
                            relay_copy(s, n, d, other).start()

                    if d == reach:
                        pl.when(jnp.logical_not(crosses(d)))(forward)
                    else:
                        forward()
            if 0 in ds:
                local_snap(s).wait()

    def receive(s, ds):
        if groups > 1:
            @pl.when(g != s // local)
            def _():
                for n, d in snap_offsets(s):
                    if d in ds:
                        (relay_copy if d else snap_copy)(s, n, d, 1).wait_recv()

    for s in range(steps):
        @pl.when(g == s // local)
        def _():
            local_snap(s).start()

    pl.semaphore_wait(barrier, greeters)
    def send(s, ds):
        snap_each(s, ds, lambda copy: copy.start())
        if s == 0:
            for d in ds:
                if d:
                    start_copies[offsets.index(d)].start()

    def tell(n, peer):
        pl.semaphore_signal(ready.at[n], inc=1, device_id=peer, device_id_type=MESH)

    edge = len(levels) + 3

    for d in offsets:
        if d < 0:
            @pl.when(crosses(-d))
            def _():
                for other in range(groups):
                    tell(edge - d - 1, at(lax.rem(g + other, groups), -d))

    upper = t >= tiles // 2
    ahead = [d for d in offsets if d < 0]
    back = [-d for d in ahead]

    def send_some(s, soon):
        for d in sorted(offsets, key=abs):
            wanted = t - d >= tiles // 2 if d < 0 else t - d < tiles // 2
            wanted = wanted if soon else jnp.logical_not(wanted)
            if d > 0:
                wanted = wanted & jnp.logical_not(crosses(-d))
            pl.when(wanted)(functools.partial(send, s, [d]))

    def sided(act, *ds):
        for way, on in ((1, upper), (-1, jnp.logical_not(upper))):
            @pl.when(on)
            def _():
                act([way * d for d in ds])

    near_ds, far_ds = sorted(ahead, key=abs), sorted(back)

    turn = edge + len(back)
    if carried:
        pl.when(t == tiles - 1)(functools.partial(tell, turn, {"grp": g, "tile": reach}))

    def wait_far(d):
        pl.semaphore_wait(ready.at[edge + d - 1], groups)

    def start_copy(d, group, last):
        first = near[d][0]
        return pltpu.make_async_remote_copy(
            src_ref=basis.at[krylov - groups + group, :, pl.ds(first, last - first)],
            dst_ref=start.at[:, target(d, first, last)],
            send_sem=start_send.at[0],
            recv_sem=start_recv.at[offsets.index(d)],
            device_id=at(group, -d),
            device_id_type=MESH,
        )

    def send_first():
        wait_far(1)
        snap_each(0, [1], lambda copy: copy.start())
        start_copy(1, g, slab - held_back if carried else slab).start()
        for s in range(1, steps):
            send(s, [1])
        for d in sorted(back)[1:]:
            wait_far(d)
            for s in range(steps):
                snap_each(s, [d], lambda copy: copy.start())

    def send_second():
        for d in sorted(back)[1:]:
            for group in range(groups):
                start_copy(d, group, near[d][1]).start()

    def send_carried():
        start_copies[offsets.index(-reach)].wait_recv()
        pl.semaphore_wait(ready.at[turn], 1)
        pltpu.make_async_remote_copy(
            src_ref=start.at[:, target(-reach, slab - held_back, slab)],
            dst_ref=start.at[:, target(1, slab - held_back, slab)],
            send_sem=start_send.at[0],
            recv_sem=start_recv.at[offsets.index(1)],
            device_id={"grp": g, "tile": tiles - 1},
            device_id_type=MESH,
        ).start()

    def send_late():
        for d in sorted(back)[1:]:
            @pl.when((t > 0) & crosses(-d))
            def _():
                wait_far(d)
                for s in range(steps):
                    send(s, [d])

    for s in range(steps):
        snap_each(s, [0], lambda copy: copy.start())
        send_some(s, True)

    def send_far():
        for s in range(steps):
            send_some(s, False)

    pl.when(t == 0)(send_far)

    def flip_step(n):
        if n:
            pl.semaphore_wait(ready.at[n - 1], 1)
        if n < len(levels):
            tell(n, flipped(levels[n]))

    def pass_on(sem, way):
        head = link == (0 if way > 0 else length - 1)
        tail = link == (length - 1 if way > 0 else 0)

        @pl.when(jnp.logical_not(head))
        def _():
            pl.semaphore_wait(ready.at[sem], 1)

        @pl.when(jnp.logical_not(tail))
        def _():
            tell(sem, at(g, way * stride))

    def chain_step(n):
        if length > 1:
            upper = link >= length // 2
            for way in (1, -1):
                @pl.when(upper == (way < 0))
                def _():
                    mine = -way if n else way
                    pass_on(len(levels) + (mine < 0), mine)

    def tell_group():
        for other in range(1, groups):
            tell(len(levels) + 2, partner(other))

    pltpu.make_async_copy(basis, held, load_sem.at[2]).wait()

    def expand(k, carry):
        plain[k] = held[k].astype(f32)
        return carry

    lax.fori_loop(0, krylov, expand, 0)
    size = krylov * ny
    blocks, height = gram_blocks(krylov, nz)

    def gram_copy(other):
        return pltpu.make_async_remote_copy(
            src_ref=gram_send,
            dst_ref=gram_send,
            send_sem=pass_send.at[other],
            recv_sem=pass_recv.at[0],
            device_id=partner(other),
            device_id_type=MESH,
        )

    @pl.when(g == 0)
    def _():
        for c in range(parts):
            wide = jnp.concatenate([held[:, c, x].reshape(size, nz) for x in range(slab)], axis=1)
            piece = lax.dot_general(wide, wide, (((1,), (1,)), ((), ())), preferred_element_type=f32)
            cross[...] = cross[...] + piece if c else piece
            if c == parts // 2:
                pl.when(t > 0)(send_far)
        line = lax.broadcasted_iota(jnp.int32, (size, size), 0)
        column = lax.broadcasted_iota(jnp.int32, (size, size), 1)
        kept = jnp.where(lax.rem(line, ny) == lax.rem(column, ny), cross[...], 0.0)
        kept = jnp.sum(kept.reshape(krylov, ny, size), axis=1)
        pick = (
            lax.broadcasted_iota(jnp.int32, (size, krylov), 0) // ny
            == lax.broadcasted_iota(jnp.int32, (size, krylov), 1)
        ).astype(f32)
        gram = jnp.dot(kept, pick, precision=HIGHEST, preferred_element_type=f32)
        gram_send[...] = jnp.concatenate(
            [gram[n * height : (n + 1) * height] for n in range(blocks)], axis=1
        )
        for other in range(1, groups):
            gram_copy(other).start()

    @pl.when(g == groups - 1)
    def _():
        for n in range(len(levels) + 1):
            flip_step(n)

    pl.when((t > 0) & (g != 0))(send_far)

    @pl.when(g == groups - 1)
    def _():
        chain_step(0)

    pl.when(t == 0)(send_first)
    send_late()
    if carried:
        pl.when(t == reach)(send_carried)
    @pl.when(g == groups - 1)
    def _():
        chain_step(1)
        for other in range(1, groups):
            tell(len(levels) + 2, partner(other))

    def spread_out(n, send, everyone, reached):
        others = everyone.at[pl.ds(0, reached * tiles - 1)]
        place = t if reached == 1 else g * tiles + t

        def begin():
            def one(peer, carry):
                def to(other):
                    pltpu.make_async_remote_copy(
                        src_ref=send,
                        dst_ref=everyone.at[place],
                        send_sem=share_send.at[n],
                        recv_sem=share_recv.at[n],
                        device_id={"grp": lax.rem(g + other, groups), "tile": peer},
                        device_id_type=MESH,
                    ).start()

                pl.when(peer != t)(functools.partial(to, 0))
                for other in range(1, reached):
                    to(other)
                return carry

            lax.fori_loop(0, tiles, one, 0)
            everyone[place] = send[...]

        def arrive():
            pltpu.make_async_copy(others, others, share_recv.at[n]).wait()

        def drain():
            pltpu.make_async_copy(others, others, share_send.at[n]).wait()

        return begin, arrive, drain

    gram_begin, gram_arrive, gram_drain = spread_out(0, gram_send, gram_all, 1)
    coef_begin, coef_arrive, coef_drain = spread_out(1, coef_send, coef_all, groups)
    def widen(d):
        def one(p, carry):
            for k in range(parts):
                state[k, pl.ds(p * ny, ny)] = start[k, p].astype(f32)
            return carry

        lo, width = (rim, slab) if d == 0 else (rim + d * slab + near[d][0], near[d][1] - near[d][0])
        lax.fori_loop(lo, lo + width, one, 0)

    def arrive(ds):
        for d in ds:
            if d == -reach and carried:
                pl.when(t != reach)(start_copies[offsets.index(d)].wait_recv)
            elif d:
                start_copies[offsets.index(d)].wait_recv()
            else:
                own.wait()
                mix.wait()
            widen(d)

    keeps = (0.0, 3.0, 2.0)
    ways = ((state, one), (one, two), (two, state))

    def march(s, known, new):
        for n, (src, dst) in enumerate(ways):
            k = 3 * s + n + 1
            lo, hi = max(k, known - k), new - k
            if hi > lo:
                first = jnp.where(upper, lo, planes - hi) + t // tiles
                scale = 6.0 ** -steps if k == 3 * steps else 1.0
                stage(src, state, dst, rates, snap, s, coupling, first, hi - lo, keeps[n], scale)

    def relay_far(s, d, early):
        for way, on in ((1, upper), (-1, jnp.logical_not(upper))):
            seam = crosses(way * d)

            @pl.when(on & (jnp.logical_not(seam) if early else seam))
            def _():
                relay(s, [way * d])

    sided(lambda ds: relay(0, [0] + ds), *near_ds)
    sided(arrive, *near_ds)
    arrive([0])
    for s in range(1, steps):
        sided(lambda ds: relay(s, [0] + ds), *near_ds)
    sided(lambda ds: receive(0, [0] + ds), *near_ds)
    pl.when((t == 0) & (g == groups - 1))(send_second)
    known = 0
    for far in (False, True):
        if far:
            for d in far_ds:
                relay_far(0, d, False)
            sided(arrive, *far_ds)
            for s in range(1, steps):
                for d in far_ds:
                    relay_far(s, d, False)
            sided(lambda ds: receive(0, ds), *far_ds)
        new = planes if far else rim + slab
        for s in range(steps):
            if s:
                sided(lambda ds: receive(s, ds), *(far_ds if far else [0] + near_ds))
            march(s, known, new)
            if not far and s == 0:
                for d in far_ds:
                    relay_far(0, d, True)
                for later in range(1, steps):
                    for d in far_ds:
                        relay_far(later, d, True)
        known = new
        if not far:
            if groups > 1:
                @pl.when(g != groups - 1)
                def _():
                    pl.semaphore_wait(ready.at[len(levels) + 2], 1)

                @pl.when(g != 0)
                def _():
                    gram_copy(0).wait_recv()

            gram_begin()

    count = f32(parts * slab * ny * nz * tiles)

    group = 8 if krylov % 8 == 0 else 1

    def project(i, carry):
        totals = [jnp.zeros((ny, nz), f32) for _ in range(group)]
        for c in range(parts):
            for x in range(slab):
                field = state[c, pl.ds((rim + x) * ny, ny)]
                for n in range(group):
                    totals[n] = totals[n] + plain[i * group + n, c, x] * field
        for n in range(group):
            rows_k[pl.ds(i * group + n, 1), :] = jnp.sum(totals[n], axis=0, keepdims=True)
        return carry

    lax.fori_loop(0, krylov // group, project, 0, unroll=2 if krylov % (2 * group) == 0 else 1)
    ones = jnp.ones((8, nz), f32)
    inner = lax.dot_general(
        ones, rows_k[...], (((1,), (1,)), ((), ())), precision=HIGHEST, preferred_element_type=f32
    )
    own_square = jnp.zeros((ny, nz), f32)
    for c in range(parts):
        for x in range(slab):
            own_square = own_square + state[c, pl.ds((rim + x) * ny, ny)] * state[c, pl.ds((rim + x) * ny, ny)]
    own_square = jnp.sum(jnp.sum(own_square, axis=0, keepdims=True), axis=1, keepdims=True)
    coef_send[...] = jnp.concatenate(
        [inner[0:1], jnp.broadcast_to(own_square, (1, coef_send.shape[1] - krylov))], axis=1
    )
    coef_begin()
    def all_sent(cells, sem):
        pltpu.make_async_copy(cells, cells, sem).wait()

    moved = sum(near[d][1] - near[d][0] for d in sorted(back)[1:])
    spare = held_back if carried else 0
    all_sent(start.at[:, pl.ds(0, 2 * rim - moved - spare)], start_send.at[0])
    if moved + spare:
        @pl.when(t > 0)
        def _():
            all_sent(start.at[:, pl.ds(0, moved + spare)], start_send.at[0])

        @pl.when((t == 0) & (g == groups - 1))
        def _():
            for _ in range(groups):
                all_sent(start.at[:, pl.ds(0, moved)], start_send.at[0])

    if spare:
        @pl.when(t == reach)
        def _():
            all_sent(start.at[:, pl.ds(0, spare)], start_send.at[0])

    for s in range(steps):
        around = 2 * (rim - 3 * s - 1)

        @pl.when(g == s // local)
        def _():
            all_sent(snap.at[s, :, pl.ds(0, around)], snap_send.at[s % local])
            last = spans(slab, rim - 3 * s - 1).get(reach, (0, 0))
            last = last[1] - last[0]
            for other in range(1, groups):
                all_sent(snap.at[s, :, pl.ds(0, slab)], snap_send.at[s % local])
                all_sent(snap.at[s, :, pl.ds(0, around - last)], relay_send.at[s % local])
                if last:
                    @pl.when(crosses(-reach))
                    def _():
                        all_sent(snap.at[s, :, pl.ds(0, last)], snap_send.at[s % local])

                    @pl.when(jnp.logical_not(crosses(reach)))
                    def _():
                        all_sent(snap.at[s, :, pl.ds(0, last)], relay_send.at[s % local])

    gram_drain()

    @pl.when(g == 0)
    def _():
        for other in range(1, groups):
            gram_copy(other).wait_send()

    gram_arrive()
    packed = jnp.sum(gram_all[...], axis=0) / count
    gram = jnp.concatenate(
        [packed[:, n * krylov : (n + 1) * krylov] for n in range(blocks)], axis=0
    )
    same = lax.broadcasted_iota(jnp.int32, gram.shape, 0) == lax.broadcasted_iota(jnp.int32, gram.shape, 1)
    times = functools.partial(jnp.dot, precision=HIGHEST, preferred_element_type=f32)
    twice = jnp.where(same, 2.0, 0.0) - gram
    both = jnp.concatenate([twice, times(twice, gram)], axis=1)
    reach_row = jnp.sum(jnp.abs(gram), axis=0, keepdims=True)
    coef_arrive()
    sums = [jnp.sum(coef_all[n * tiles : (n + 1) * tiles], axis=0) / count for n in range(groups)]
    sums = jnp.concatenate(sums + [jnp.zeros((-groups % 8, sums[0].shape[1]), f32)], axis=0)
    first_rows, work_square = sums[:, :krylov], sums[:, krylov : krylov + 1]
    mixed = times(first_rows, both)
    every, turned = mixed[:, :krylov], mixed[:, krylov:]
    group_row = lax.broadcasted_iota(jnp.int32, work_square.shape, 0)
    own_every = jnp.sum(jnp.where(group_row == g, every, 0.0), axis=0, keepdims=True)
    for k in range(krylov):
        spread[k] = jnp.broadcast_to(own_every[:, k : k + 1], (8, nz))
    linear = 2.0 * every * first_rows
    bent = every * turned
    bound = jnp.abs(linear) + every * every * reach_row
    square = work_square + jnp.sum(bent - linear, axis=1, keepdims=True)
    bound = work_square + jnp.sum(bound, axis=1, keepdims=True)
    margin = jnp.where(group_row < groups, square - cancel_limit * bound, jnp.inf)
    margin_out[...] = jnp.broadcast_to(jnp.min(margin, axis=0, keepdims=True), margin_out.shape)
    square = jnp.sum(jnp.where(group_row == g, square, 0.0), axis=0, keepdims=True)
    square_out[...] = jnp.broadcast_to(square, square_out.shape)
    coef_out[...] = own_every
    for x in range(slab):
        removed = [jnp.zeros((ny // 8, 8, nz), f32) for _ in range(parts)]
        for k in range(krylov):
            factor = spread[k][None]
            for c in range(parts):
                removed[c] = removed[c] + factor * plain[k, c, x].reshape(ny // 8, 8, nz)
        for c in range(parts):
            left_out[0, c, x] = state[c, pl.ds((rim + x) * ny, ny)] - removed[c].reshape(ny, nz)
    coef_drain()


def square_kernel(tiles, left, square_out, send, everyone, ssem, rsem):
    g = lax.axis_index("grp")
    t = lax.axis_index("tile")
    _, parts, slab, ny, nz = left.shape
    barrier = pltpu.get_barrier_semaphore()

    def peer(r):
        return {"grp": g, "tile": lax.rem(t + r, tiles)}

    def greet(r, carry):
        pl.semaphore_signal(barrier, inc=1, device_id=peer(r), device_id_type=MESH)
        return carry

    lax.fori_loop(1, tiles, greet, 0)
    pl.semaphore_wait(barrier, tiles - 1)
    total = jnp.zeros((ny, nz), f32)
    for c in range(parts):
        for x in range(slab):
            total = total + left[0, c, x] * left[0, c, x]
    send[...] = jnp.sum(total, axis=0, keepdims=True)

    def copy(r, sender):
        return pltpu.make_async_remote_copy(
            src_ref=send,
            dst_ref=everyone.at[sender],
            send_sem=ssem.at[r],
            recv_sem=rsem.at[r],
            device_id=peer(r),
            device_id_type=MESH,
        )

    lax.fori_loop(1, tiles, lambda r, c: (copy(r, t).start(), c)[1], 0)
    everyone[t] = send[...]
    lax.fori_loop(
        1, tiles, lambda r, c: (copy(r, lax.rem(t - r + tiles, tiles)).wait_recv(), c)[1], 0
    )
    count = f32(parts * slab * ny * nz * tiles)
    square = jnp.sum(jnp.sum(everyone[...], axis=0), axis=1, keepdims=True) / count
    square_out[...] = jnp.broadcast_to(square, square_out.shape)
    lax.fori_loop(1, tiles, lambda r, c: (copy(r, t).wait_send(), c)[1], 0)


def finish(left, coefs, square, out, coef_out, norm_out, held, norm_row, sem):
    norm = jnp.sqrt(square[...])
    norm_row[...] = norm
    inverse = jnp.broadcast_to(1.0 / norm, left.shape[3:])
    copies = [
        pltpu.make_async_copy(norm_row, norm_out, sem.at[0]),
        pltpu.make_async_copy(coefs, coef_out, sem.at[1]),
    ]
    for c in range(left.shape[1]):
        for x in range(left.shape[2]):
            held[0, c, x] = left[0, c, x] * inverse
    copies.append(pltpu.make_async_copy(held, out, sem.at[2]))
    for copy in copies:
        copy.start()
    for copy in copies:
        copy.wait()


def on_device(groups, tiles, basis, snapshots, coupling):
    krylov, parts, slab, ny, nz = basis.shape
    local, fields = snapshots.shape[:2]
    steps = local * groups
    rim = 3 * steps
    planes = slab + 2 * rim
    count = len(spans(slab, rim))
    blocks, height = gram_blocks(krylov, nz)
    width = -(-(krylov + 1) // nz) * nz
    dma = pltpu.SemaphoreType.DMA
    field = pltpu.VMEM((parts, planes * ny, nz), f32)
    whole = pl.BlockSpec(memory_space=pltpu.VMEM)
    outside = pl.BlockSpec(memory_space=pltpu.HBM)
    results = pl.pallas_call(
        functools.partial(kernel, groups, tiles),
        name="propagate",
        out_shape=(
            jax.ShapeDtypeStruct((1, parts, slab, ny, nz), f32),
            jax.ShapeDtypeStruct((1, krylov), f32),
            jax.ShapeDtypeStruct((1, nz), f32),
            jax.ShapeDtypeStruct((1, nz), f32),
        ),
        in_specs=[outside] * 3,
        out_specs=(whole,) * 4,
        scratch_shapes=[
            pltpu.SMEM(coupling.shape, f32),
            pltpu.VMEM(basis.shape, bf16),
            pltpu.VMEM(basis.shape, f32),
            pltpu.VMEM((parts, planes, ny, nz), bf16),
            pltpu.VMEM((steps, fields, planes, ny, nz), bf16),
            field,
            field,
            field,
            pltpu.VMEM((steps, 12, planes, ny, nz), f32),
            pltpu.VMEM((krylov * ny, krylov * ny), f32),
            pltpu.VMEM((krylov, nz), f32),
            pltpu.VMEM((krylov, 8, nz), f32),
            pltpu.VMEM((height, blocks * krylov), f32),
            pltpu.VMEM((tiles, height, blocks * krylov), f32),
            pltpu.VMEM((1, width), f32),
            pltpu.VMEM((groups * tiles, 1, width), f32),
            dma((3 + local,)),
            dma((1,)),
            dma((count,)),
            dma((local,)),
            dma((local,)),
            dma((steps, count + 1)),
            dma((2,)),
            dma((2,)),
            dma((groups,)),
            dma((1,)),
            pltpu.SemaphoreType.REGULAR((min(tiles.bit_length() - 1, (-(-rim // slab)).bit_length()) + 4 + -(-rim // slab),)),
        ],
        compiler_params=pltpu.CompilerParams(
            collective_id=0, has_side_effects=True, vmem_limit_bytes=48 << 20
        ),
    )(*(pltpu.with_memory_space_constraint(a, pltpu.HBM) for a in (coupling, basis, snapshots)))
    left, coefs, square, margin = results

    def scaled(left, coefs, square):
        return pl.pallas_call(
            finish,
            name="finish",
            out_shape=tuple(jax.ShapeDtypeStruct(a.shape, f32) for a in (left, coefs, square)),
            in_specs=[whole] * 3,
            out_specs=(outside,) * 3,
            scratch_shapes=[
                pltpu.VMEM(left.shape, f32),
                pltpu.VMEM(square.shape, f32),
                dma((3,)),
            ],
        )(left, coefs, square)

    def summed(left, coefs, square):
        exact = pl.pallas_call(
            functools.partial(square_kernel, tiles),
            name="exact_square",
            out_shape=jax.ShapeDtypeStruct((1, nz), f32),
            in_specs=[whole],
            out_specs=whole,
            scratch_shapes=[
                pltpu.VMEM((1, nz), f32),
                pltpu.VMEM((tiles, 1, nz), f32),
                dma((tiles,)),
                dma((tiles,)),
            ],
            compiler_params=pltpu.CompilerParams(collective_id=1, has_side_effects=True),
        )(left)
        return scaled(left, coefs, exact)

    new_vector, coefs, norms = lax.cond(margin[0, 0] > 0.0, scaled, summed, left, coefs, square)
    return new_vector, coefs, norms[0, :1]


def solution(mesh):
    placed = (P(None, None, "tile", None, None), P("grp", None, "tile", None, None), P())
    return jax.shard_map(
        functools.partial(on_device, mesh.shape["grp"], mesh.shape["tile"]),
        mesh=mesh,
        in_specs=placed,
        out_specs=(P("grp", None, "tile", None, None), P("grp", None), P("grp")),
        check_vma=False,
    )
```

```python
import functools

import jax
import jax.numpy as jnp
from jax import lax
from jax.experimental import pallas as pl
from jax.experimental.pallas import tpu as pltpu
from jax.sharding import PartitionSpec as P

viscosity = 0.5
time_step = 0.3
cancel_limit = 0.01
f32 = jnp.float32
bf16 = jnp.bfloat16
MESH = pl.DeviceIdType.MESH
HIGHEST = lax.Precision.HIGHEST


def spans(slab, rim):
    found = {}
    reach = -(-rim // slab)
    for d in range(1, reach + 1):
        width = min(slab, rim - (d - 1) * slab)
        found[-d] = (slab - width, slab)
        found[d] = (0, width)
    return found


def gram_blocks(krylov, lanes):
    blocks = max(lanes // krylov, 1)
    return (blocks, krylov // blocks) if krylov % (8 * blocks) == 0 else (1, krylov)


def stage(src, old, dst, rates, snap, step, coupling, lo, planes, keep, scale):
    rows, lanes = snap.shape[3], snap.shape[4]
    row = lax.broadcasted_iota(jnp.int32, (rows, lanes), 0)
    top = row == 0
    bottom = row == rows - 1
    mix = [[coupling[k, j] for j in range(5)] for k in range(5)]
    edge = viscosity * time_step

    def cells(field, k, p, shift=0):
        return field[k, pl.ds(p * rows + shift, rows)]

    def make_rates(p):
        base = [snap[step, n, p].astype(f32) for n in range(4)]
        half = [(0.5 * time_step) * base[n] for n in range(3)]
        pull = time_step * base[3]
        found = [edge - half[0], edge + half[0]]
        found += [jnp.where(bottom, 0.0, edge - half[1]), jnp.where(top, 0.0, edge + half[1])]
        found += [edge - half[2], edge + half[2], pull]
        own = 1.0 - 6.0 * edge
        found += [own - pull * mix[k][k] for k in range(5)]
        for n, rate in enumerate(found):
            rates[step, n, p] = rate
        return found

    def body(i, carry):
        p = lo + i
        now = [rates[step, n, p] for n in range(12)] if keep else make_rates(p)
        x_up, x_low, y_up, y_low, z_up, z_low, pull = now[:7]
        center = [cells(src, k, p) for k in range(5)]
        for k in range(5):
            q = center[k]
            others = [j for j in range(5) if j != k]
            coupled = mix[k][others[0]] * center[others[0]]
            for j in others[1:]:
                coupled = coupled + mix[k][j] * center[j]
            total = now[7 + k] * q - pull * coupled
            total = total + (x_up * cells(src, k, p + 1) + x_low * cells(src, k, p - 1))
            total = total + (y_up * cells(src, k, p, 1) + y_low * cells(src, k, p, -1))
            total = total + (z_up * pltpu.roll(q, lanes - 1, 1) + z_low * pltpu.roll(q, 1, 1))
            if keep:
                total = total + keep * cells(old, k, p)
            if scale != 1.0:
                total = total * scale
            dst[k, pl.ds(p * rows, rows)] = total
        return carry

    unroll = max(n for n in range(1, 9) if planes % n == 0)
    lax.fori_loop(0, planes, body, 0, unroll=unroll)


def kernel(
    groups, tiles, coupling_in, basis, snapshots,
    left_out, coef_out, square_out, margin_out,
    coupling, held, plain, start, snap, state, one, two, rates, cross, rows_k, spread,
    gram_send, gram_all, coef_send, coef_all,
    load_sem, start_send, start_recv, snap_send, relay_send, snap_recv,
    share_send, share_recv, pass_send, pass_recv, ready,
):
    g = lax.axis_index("grp")
    t = lax.axis_index("tile")
    krylov, parts, slab, ny, nz = basis.shape
    local = snapshots.shape[0]
    steps = local * groups
    rim = 3 * steps
    planes = slab + 2 * rim
    near = spans(slab, rim)
    offsets = sorted(near)
    position = krylov - groups + g
    levels = [b for b in range(tiles.bit_length() - 1) if (1 << b) in offsets]
    stride = 1 << len(levels)
    length = tiles // stride
    link = t // stride

    def at(group, offset):
        return {"grp": group, "tile": lax.rem(t + (offset % tiles), tiles)}

    def flipped(level):
        bit = 1 << level
        return {"grp": g, "tile": t + bit - 2 * bit * lax.rem(t // bit, 2)}

    def partner(other):
        return {"grp": lax.rem(g + other, groups), "tile": t}

    barrier = pltpu.get_barrier_semaphore()
    reach = max(offsets)

    def crosses(d):
        return t + d >= tiles if d > 0 else t + d < 0

    def greet(peer):
        pl.semaphore_signal(barrier, inc=1, device_id=peer, device_id_type=MESH)

    greeters = groups - 1
    for d in sorted(offsets, key=abs, reverse=True):
        if d > 0:
            greet(at(g, -d))
            greeters = greeters + 1 + jnp.where(crosses(d), groups - 1, 0)

            @pl.when(crosses(-d))
            def _():
                for other in range(1, groups):
                    greet(at(lax.rem(g + other, groups), -d))
        else:
            pl.when(jnp.logical_not(crosses(-d)))(functools.partial(greet, at(g, -d)))
            greeters = greeters + jnp.where(crosses(d), 0, 1)
    held_back = near[reach][1] - near[reach][0]
    carried = reach > 1 and held_back < slab and 2 * reach < tiles
    if carried:
        pl.when(t == reach)(functools.partial(greet, {"grp": g, "tile": tiles - 1}))
        greeters = greeters + jnp.where(t == tiles - 1, 1, 0)
    for other in range(1, groups):
        greet(partner(other))
    for way in (1, -1):
        last = link == (length - 1 if way > 0 else 0)
        greeters = greeters + jnp.where(last, 0, 1)

        @pl.when(jnp.logical_not(last))
        def _():
            greet(at(g, way * stride))

    chunk = 8 if krylov % 8 == 0 else 1
    own = pltpu.make_async_copy(basis.at[position], start.at[:, pl.ds(rim, slab)], load_sem.at[0])
    own.start()
    mix = pltpu.make_async_copy(coupling_in, coupling, load_sem.at[1])
    mix.start()
    for n in range(krylov // chunk):
        part = pl.ds(n * chunk, chunk)
        pltpu.make_async_copy(basis.at[part], held.at[part], load_sem.at[2]).start()

    def target(d, first, last):
        return pl.ds(rim + d * slab + first, last - first)

    start_copies = []
    for n, d in enumerate(offsets):
        first, last = near[d]
        start_copies.append(
            pltpu.make_async_remote_copy(
                src_ref=basis.at[position, :, pl.ds(first, last - first)],
                dst_ref=start.at[:, target(d, first, last)],
                send_sem=start_send.at[0],
                recv_sem=start_recv.at[n],
                device_id=at(g, -d),
                device_id_type=MESH,
            )
        )

    def snap_copy(s, n, d, other):
        first, last = (0, slab) if d == 0 else spans(slab, rim - 3 * s - 1)[d]
        return pltpu.make_async_remote_copy(
            src_ref=snapshots.at[s % local, :, pl.ds(first, last - first)],
            dst_ref=snap.at[s, :, target(d, first, last)],
            send_sem=snap_send.at[s % local],
            recv_sem=snap_recv.at[s, n],
            device_id=at(lax.rem(g + other, groups), -d),
            device_id_type=MESH,
        )

    def local_snap(s):
        return pltpu.make_async_copy(
            snapshots.at[s % local], snap.at[s, :, pl.ds(rim, slab)], load_sem.at[3 + s % local]
        )

    def snap_offsets(s):
        inside = spans(slab, rim - 3 * s - 1)
        return [(n, d) for n, d in enumerate([0] + offsets) if d == 0 or d in inside]

    def snap_each(s, ds, act):
        inside = {d: n for n, d in snap_offsets(s)}

        @pl.when(g == s // local)
        def _():
            for d in ds:
                if d in inside:
                    for other in range(1 if d else groups):
                        if d or other:
                            act(snap_copy(s, inside[d], d, other))
                    if d == reach:
                        @pl.when(crosses(-d))
                        def _():
                            for other in range(1, groups):
                                act(snap_copy(s, inside[d], d, other))

    def relay_copy(s, n, d, other):
        first, last = spans(slab, rim - 3 * s - 1)[d]
        cells = snap.at[s, :, target(d, first, last)]
        return pltpu.make_async_remote_copy(
            src_ref=cells,
            dst_ref=cells,
            send_sem=relay_send.at[s % local],
            recv_sem=snap_recv.at[s, n],
            device_id=at(lax.rem(g + other, groups), 0),
            device_id_type=MESH,
        )

    def relay(s, ds):
        @pl.when(g == s // local)
        def _():
            for n, d in snap_offsets(s):
                if d and d in ds:
                    snap_copy(s, n, d, 0).wait_recv()

                    def forward():
                        for other in range(1, groups):
                            relay_copy(s, n, d, other).start()

                    if d == reach:
                        pl.when(jnp.logical_not(crosses(d)))(forward)
                    else:
                        forward()
            if 0 in ds:
                local_snap(s).wait()

    def receive(s, ds):
        if groups > 1:
            @pl.when(g != s // local)
            def _():
                for n, d in snap_offsets(s):
                    if d in ds:
                        (relay_copy if d else snap_copy)(s, n, d, 1).wait_recv()

    for s in range(steps):
        @pl.when(g == s // local)
        def _():
            local_snap(s).start()

    pl.semaphore_wait(barrier, greeters)
    def send(s, ds):
        snap_each(s, ds, lambda copy: copy.start())
        if s == 0:
            for d in ds:
                if d:
                    start_copies[offsets.index(d)].start()

    def tell(n, peer):
        pl.semaphore_signal(ready.at[n], inc=1, device_id=peer, device_id_type=MESH)

    edge = len(levels) + 3

    for d in offsets:
        if d < 0:
            @pl.when(crosses(-d))
            def _():
                for other in range(groups):
                    tell(edge - d - 1, at(lax.rem(g + other, groups), -d))

    upper = t >= tiles // 2
    ahead = [d for d in offsets if d < 0]
    back = [-d for d in ahead]

    def send_some(s, soon):
        for d in sorted(offsets, key=abs):
            wanted = t - d >= tiles // 2 if d < 0 else t - d < tiles // 2
            wanted = wanted if soon else jnp.logical_not(wanted)
            if d > 0:
                wanted = wanted & jnp.logical_not(crosses(-d))
            pl.when(wanted)(functools.partial(send, s, [d]))

    def sided(act, *ds):
        for way, on in ((1, upper), (-1, jnp.logical_not(upper))):
            @pl.when(on)
            def _():
                act([way * d for d in ds])

    near_ds, far_ds = sorted(ahead, key=abs), sorted(back)

    turn = edge + len(back)
    if carried:
        pl.when(t == tiles - 1)(functools.partial(tell, turn, {"grp": g, "tile": reach}))

    def wait_far(d):
        pl.semaphore_wait(ready.at[edge + d - 1], groups)

    def start_copy(d, group, last):
        first = near[d][0]
        return pltpu.make_async_remote_copy(
            src_ref=basis.at[krylov - groups + group, :, pl.ds(first, last - first)],
            dst_ref=start.at[:, target(d, first, last)],
            send_sem=start_send.at[0],
            recv_sem=start_recv.at[offsets.index(d)],
            device_id=at(group, -d),
            device_id_type=MESH,
        )

    def send_first():
        wait_far(1)
        snap_each(0, [1], lambda copy: copy.start())
        start_copy(1, g, slab - held_back if carried else slab).start()
        for s in range(1, steps):
            send(s, [1])
        for d in sorted(back)[1:]:
            wait_far(d)
            for s in range(steps):
                snap_each(s, [d], lambda copy: copy.start())

    def send_second():
        for d in sorted(back)[1:]:
            for group in range(groups):
                start_copy(d, group, near[d][1]).start()

    def send_carried():
        start_copies[offsets.index(-reach)].wait_recv()
        pl.semaphore_wait(ready.at[turn], 1)
        pltpu.make_async_remote_copy(
            src_ref=start.at[:, target(-reach, slab - held_back, slab)],
            dst_ref=start.at[:, target(1, slab - held_back, slab)],
            send_sem=start_send.at[0],
            recv_sem=start_recv.at[offsets.index(1)],
            device_id={"grp": g, "tile": tiles - 1},
            device_id_type=MESH,
        ).start()

    def send_late():
        for d in sorted(back)[1:]:
            @pl.when((t > 0) & crosses(-d))
            def _():
                wait_far(d)
                for s in range(steps):
                    send(s, [d])

    for s in range(steps):
        snap_each(s, [0], lambda copy: copy.start())
        send_some(s, True)

    def send_far():
        for s in range(steps):
            send_some(s, False)

    at_end = (t < reach) | (t >= tiles - reach)
    pl.when(at_end)(send_far)

    def flip_step(n):
        if n:
            pl.semaphore_wait(ready.at[n - 1], 1)
        if n < len(levels):
            tell(n, flipped(levels[n]))

    def pass_on(sem, way):
        head = link == (0 if way > 0 else length - 1)
        tail = link == (length - 1 if way > 0 else 0)

        @pl.when(jnp.logical_not(head))
        def _():
            pl.semaphore_wait(ready.at[sem], 1)

        @pl.when(jnp.logical_not(tail))
        def _():
            tell(sem, at(g, way * stride))

    def chain_step(n):
        if length > 1:
            upper = link >= length // 2
            for way in (1, -1):
                @pl.when(upper == (way < 0))
                def _():
                    mine = -way if n else way
                    pass_on(len(levels) + (mine < 0), mine)

    def tell_group():
        for other in range(1, groups):
            tell(len(levels) + 2, partner(other))

    pltpu.make_async_copy(basis, held, load_sem.at[2]).wait()

    def expand(k, carry):
        plain[k] = held[k].astype(f32)
        return carry

    lax.fori_loop(0, krylov, expand, 0)
    size = krylov * ny
    blocks, height = gram_blocks(krylov, nz)

    def gram_copy(other):
        return pltpu.make_async_remote_copy(
            src_ref=gram_send,
            dst_ref=gram_send,
            send_sem=pass_send.at[other],
            recv_sem=pass_recv.at[0],
            device_id=partner(other),
            device_id_type=MESH,
        )

    @pl.when(g == 0)
    def _():
        for c in range(parts):
            wide = jnp.concatenate([held[:, c, x].reshape(size, nz) for x in range(slab)], axis=1)
            piece = lax.dot_general(wide, wide, (((1,), (1,)), ((), ())), preferred_element_type=f32)
            cross[...] = cross[...] + piece if c else piece
            if c == parts // 2:
                pl.when(jnp.logical_not(at_end))(send_far)
        line = lax.broadcasted_iota(jnp.int32, (size, size), 0)
        column = lax.broadcasted_iota(jnp.int32, (size, size), 1)
        kept = jnp.where(lax.rem(line, ny) == lax.rem(column, ny), cross[...], 0.0)
        kept = jnp.sum(kept.reshape(krylov, ny, size), axis=1)
        pick = (
            lax.broadcasted_iota(jnp.int32, (size, krylov), 0) // ny
            == lax.broadcasted_iota(jnp.int32, (size, krylov), 1)
        ).astype(f32)
        gram = jnp.dot(kept, pick, precision=HIGHEST, preferred_element_type=f32)
        gram_send[...] = jnp.concatenate(
            [gram[n * height : (n + 1) * height] for n in range(blocks)], axis=1
        )
        for other in range(1, groups):
            gram_copy(other).start()

    @pl.when(g == groups - 1)
    def _():
        for n in range(len(levels) + 1):
            flip_step(n)

    pl.when(jnp.logical_not(at_end) & (g != 0))(send_far)

    @pl.when(g == groups - 1)
    def _():
        chain_step(0)

    pl.when(t == 0)(send_first)
    send_late()
    if carried:
        pl.when(t == reach)(send_carried)
    @pl.when(g == groups - 1)
    def _():
        chain_step(1)
        for other in range(1, groups):
            tell(len(levels) + 2, partner(other))

    def spread_out(n, send, everyone, reached):
        others = everyone.at[pl.ds(0, reached * tiles - 1)]
        place = t if reached == 1 else g * tiles + t

        def begin():
            def one(peer, carry):
                def to(other):
                    pltpu.make_async_remote_copy(
                        src_ref=send,
                        dst_ref=everyone.at[place],
                        send_sem=share_send.at[n],
                        recv_sem=share_recv.at[n],
                        device_id={"grp": lax.rem(g + other, groups), "tile": peer},
                        device_id_type=MESH,
                    ).start()

                pl.when(peer != t)(functools.partial(to, 0))
                for other in range(1, reached):
                    to(other)
                return carry

            lax.fori_loop(0, tiles, one, 0)
            everyone[place] = send[...]

        def arrive():
            pltpu.make_async_copy(others, others, share_recv.at[n]).wait()

        def drain():
            pltpu.make_async_copy(others, others, share_send.at[n]).wait()

        return begin, arrive, drain

    gram_begin, gram_arrive, gram_drain = spread_out(0, gram_send, gram_all, 1)
    coef_begin, coef_arrive, coef_drain = spread_out(1, coef_send, coef_all, groups)
    def widen(d):
        def one(p, carry):
            for k in range(parts):
                state[k, pl.ds(p * ny, ny)] = start[k, p].astype(f32)
            return carry

        lo, width = (rim, slab) if d == 0 else (rim + d * slab + near[d][0], near[d][1] - near[d][0])
        lax.fori_loop(lo, lo + width, one, 0)

    def arrive(ds):
        for d in ds:
            if d == -reach and carried:
                pl.when(t != reach)(start_copies[offsets.index(d)].wait_recv)
            elif d:
                start_copies[offsets.index(d)].wait_recv()
            else:
                own.wait()
                mix.wait()
            widen(d)

    keeps = (0.0, 3.0, 2.0)
    ways = ((state, one), (one, two), (two, state))

    def march(s, known, new):
        for n, (src, dst) in enumerate(ways):
            k = 3 * s + n + 1
            lo, hi = max(k, known - k), new - k
            if hi > lo:
                first = jnp.where(upper, lo, planes - hi) + t // tiles
                scale = 6.0 ** -steps if k == 3 * steps else 1.0
                stage(src, state, dst, rates, snap, s, coupling, first, hi - lo, keeps[n], scale)

    def relay_far(s, d, early):
        for way, on in ((1, upper), (-1, jnp.logical_not(upper))):
            seam = crosses(way * d)

            @pl.when(on & (jnp.logical_not(seam) if early else seam))
            def _():
                relay(s, [way * d])

    sided(lambda ds: relay(0, [0] + ds), *near_ds)
    sided(arrive, *near_ds)
    arrive([0])
    for s in range(1, steps):
        sided(lambda ds: relay(s, [0] + ds), *near_ds)
    sided(lambda ds: receive(0, [0] + ds), *near_ds)
    pl.when((t == 0) & (g == groups - 1))(send_second)
    known = 0
    for far in (False, True):
        if far:
            for d in far_ds:
                relay_far(0, d, False)
            sided(arrive, *far_ds)
            for s in range(1, steps):
                for d in far_ds:
                    relay_far(s, d, False)
            sided(lambda ds: receive(0, ds), *far_ds)
        new = planes if far else rim + slab
        for s in range(steps):
            if s:
                sided(lambda ds: receive(s, ds), *(far_ds if far else [0] + near_ds))
            march(s, known, new)
            if not far and s == 0:
                for d in far_ds:
                    relay_far(0, d, True)
                for later in range(1, steps):
                    for d in far_ds:
                        relay_far(later, d, True)
        known = new
        if not far:
            if groups > 1:
                @pl.when(g != groups - 1)
                def _():
                    pl.semaphore_wait(ready.at[len(levels) + 2], 1)

                @pl.when(g != 0)
                def _():
                    gram_copy(0).wait_recv()

            gram_begin()

    count = f32(parts * slab * ny * nz * tiles)

    group = 8 if krylov % 8 == 0 else 1

    def project(i, carry):
        totals = [jnp.zeros((ny, nz), f32) for _ in range(group)]
        for c in range(parts):
            for x in range(slab):
                field = state[c, pl.ds((rim + x) * ny, ny)]
                for n in range(group):
                    totals[n] = totals[n] + plain[i * group + n, c, x] * field
        for n in range(group):
            rows_k[pl.ds(i * group + n, 1), :] = jnp.sum(totals[n], axis=0, keepdims=True)
        return carry

    lax.fori_loop(0, krylov // group, project, 0, unroll=2 if krylov % (2 * group) == 0 else 1)
    ones = jnp.ones((8, nz), f32)
    inner = lax.dot_general(
        ones, rows_k[...], (((1,), (1,)), ((), ())), precision=HIGHEST, preferred_element_type=f32
    )
    own_square = jnp.zeros((ny, nz), f32)
    for c in range(parts):
        for x in range(slab):
            own_square = own_square + state[c, pl.ds((rim + x) * ny, ny)] * state[c, pl.ds((rim + x) * ny, ny)]
    own_square = jnp.sum(jnp.sum(own_square, axis=0, keepdims=True), axis=1, keepdims=True)
    coef_send[...] = jnp.concatenate(
        [inner[0:1], jnp.broadcast_to(own_square, (1, coef_send.shape[1] - krylov))], axis=1
    )
    coef_begin()
    def all_sent(cells, sem):
        pltpu.make_async_copy(cells, cells, sem).wait()

    moved = sum(near[d][1] - near[d][0] for d in sorted(back)[1:])
    spare = held_back if carried else 0
    all_sent(start.at[:, pl.ds(0, 2 * rim - moved - spare)], start_send.at[0])
    if moved + spare:
        @pl.when(t > 0)
        def _():
            all_sent(start.at[:, pl.ds(0, moved + spare)], start_send.at[0])

        @pl.when((t == 0) & (g == groups - 1))
        def _():
            for _ in range(groups):
                all_sent(start.at[:, pl.ds(0, moved)], start_send.at[0])

    if spare:
        @pl.when(t == reach)
        def _():
            all_sent(start.at[:, pl.ds(0, spare)], start_send.at[0])

    for s in range(steps):
        around = 2 * (rim - 3 * s - 1)

        @pl.when(g == s // local)
        def _():
            all_sent(snap.at[s, :, pl.ds(0, around)], snap_send.at[s % local])
            last = spans(slab, rim - 3 * s - 1).get(reach, (0, 0))
            last = last[1] - last[0]
            for other in range(1, groups):
                all_sent(snap.at[s, :, pl.ds(0, slab)], snap_send.at[s % local])
                all_sent(snap.at[s, :, pl.ds(0, around - last)], relay_send.at[s % local])
                if last:
                    @pl.when(crosses(-reach))
                    def _():
                        all_sent(snap.at[s, :, pl.ds(0, last)], snap_send.at[s % local])

                    @pl.when(jnp.logical_not(crosses(reach)))
                    def _():
                        all_sent(snap.at[s, :, pl.ds(0, last)], relay_send.at[s % local])

    gram_drain()

    @pl.when(g == 0)
    def _():
        for other in range(1, groups):
            gram_copy(other).wait_send()

    gram_arrive()
    packed = jnp.sum(gram_all[...], axis=0) / count
    gram = jnp.concatenate(
        [packed[:, n * krylov : (n + 1) * krylov] for n in range(blocks)], axis=0
    )
    same = lax.broadcasted_iota(jnp.int32, gram.shape, 0) == lax.broadcasted_iota(jnp.int32, gram.shape, 1)
    times = functools.partial(jnp.dot, precision=HIGHEST, preferred_element_type=f32)
    twice = jnp.where(same, 2.0, 0.0) - gram
    both = jnp.concatenate([twice, times(twice, gram)], axis=1)
    reach_row = jnp.sum(jnp.abs(gram), axis=0, keepdims=True)
    coef_arrive()
    sums = [jnp.sum(coef_all[n * tiles : (n + 1) * tiles], axis=0) / count for n in range(groups)]
    sums = jnp.concatenate(sums + [jnp.zeros((-groups % 8, sums[0].shape[1]), f32)], axis=0)
    first_rows, work_square = sums[:, :krylov], sums[:, krylov : krylov + 1]
    mixed = times(first_rows, both)
    every, turned = mixed[:, :krylov], mixed[:, krylov:]
    group_row = lax.broadcasted_iota(jnp.int32, work_square.shape, 0)
    own_every = jnp.sum(jnp.where(group_row == g, every, 0.0), axis=0, keepdims=True)
    for k in range(krylov):
        spread[k] = jnp.broadcast_to(own_every[:, k : k + 1], (8, nz))
    linear = 2.0 * every * first_rows
    bent = every * turned
    bound = jnp.abs(linear) + every * every * reach_row
    square = work_square + jnp.sum(bent - linear, axis=1, keepdims=True)
    bound = work_square + jnp.sum(bound, axis=1, keepdims=True)
    margin = jnp.where(group_row < groups, square - cancel_limit * bound, jnp.inf)
    margin_out[...] = jnp.broadcast_to(jnp.min(margin, axis=0, keepdims=True), margin_out.shape)
    square = jnp.sum(jnp.where(group_row == g, square, 0.0), axis=0, keepdims=True)
    square_out[...] = jnp.broadcast_to(square, square_out.shape)
    coef_out[...] = own_every
    for x in range(slab):
        removed = [jnp.zeros((ny // 8, 8, nz), f32) for _ in range(parts)]
        for k in range(krylov):
            factor = spread[k][None]
            for c in range(parts):
                removed[c] = removed[c] + factor * plain[k, c, x].reshape(ny // 8, 8, nz)
        for c in range(parts):
            left_out[0, c, x] = state[c, pl.ds((rim + x) * ny, ny)] - removed[c].reshape(ny, nz)
    coef_drain()


def square_kernel(tiles, left, square_out, send, everyone, ssem, rsem):
    g = lax.axis_index("grp")
    t = lax.axis_index("tile")
    _, parts, slab, ny, nz = left.shape
    barrier = pltpu.get_barrier_semaphore()

    def peer(r):
        return {"grp": g, "tile": lax.rem(t + r, tiles)}

    def greet(r, carry):
        pl.semaphore_signal(barrier, inc=1, device_id=peer(r), device_id_type=MESH)
        return carry

    lax.fori_loop(1, tiles, greet, 0)
    pl.semaphore_wait(barrier, tiles - 1)
    total = jnp.zeros((ny, nz), f32)
    for c in range(parts):
        for x in range(slab):
            total = total + left[0, c, x] * left[0, c, x]
    send[...] = jnp.sum(total, axis=0, keepdims=True)

    def copy(r, sender):
        return pltpu.make_async_remote_copy(
            src_ref=send,
            dst_ref=everyone.at[sender],
            send_sem=ssem.at[r],
            recv_sem=rsem.at[r],
            device_id=peer(r),
            device_id_type=MESH,
        )

    lax.fori_loop(1, tiles, lambda r, c: (copy(r, t).start(), c)[1], 0)
    everyone[t] = send[...]
    lax.fori_loop(
        1, tiles, lambda r, c: (copy(r, lax.rem(t - r + tiles, tiles)).wait_recv(), c)[1], 0
    )
    count = f32(parts * slab * ny * nz * tiles)
    square = jnp.sum(jnp.sum(everyone[...], axis=0), axis=1, keepdims=True) / count
    square_out[...] = jnp.broadcast_to(square, square_out.shape)
    lax.fori_loop(1, tiles, lambda r, c: (copy(r, t).wait_send(), c)[1], 0)


def finish(left, coefs, square, out, coef_out, norm_out, held, norm_row, sem):
    norm = jnp.sqrt(square[...])
    norm_row[...] = norm
    inverse = jnp.broadcast_to(1.0 / norm, left.shape[3:])
    copies = [
        pltpu.make_async_copy(norm_row, norm_out, sem.at[0]),
        pltpu.make_async_copy(coefs, coef_out, sem.at[1]),
    ]
    for c in range(left.shape[1]):
        for x in range(left.shape[2]):
            held[0, c, x] = left[0, c, x] * inverse
    copies.append(pltpu.make_async_copy(held, out, sem.at[2]))
    for copy in copies:
        copy.start()
    for copy in copies:
        copy.wait()


def on_device(groups, tiles, basis, snapshots, coupling):
    krylov, parts, slab, ny, nz = basis.shape
    local, fields = snapshots.shape[:2]
    steps = local * groups
    rim = 3 * steps
    planes = slab + 2 * rim
    count = len(spans(slab, rim))
    blocks, height = gram_blocks(krylov, nz)
    width = -(-(krylov + 1) // nz) * nz
    dma = pltpu.SemaphoreType.DMA
    field = pltpu.VMEM((parts, planes * ny, nz), f32)
    whole = pl.BlockSpec(memory_space=pltpu.VMEM)
    outside = pl.BlockSpec(memory_space=pltpu.HBM)
    results = pl.pallas_call(
        functools.partial(kernel, groups, tiles),
        name="propagate",
        out_shape=(
            jax.ShapeDtypeStruct((1, parts, slab, ny, nz), f32),
            jax.ShapeDtypeStruct((1, krylov), f32),
            jax.ShapeDtypeStruct((1, nz), f32),
            jax.ShapeDtypeStruct((1, nz), f32),
        ),
        in_specs=[outside] * 3,
        out_specs=(whole,) * 4,
        scratch_shapes=[
            pltpu.SMEM(coupling.shape, f32),
            pltpu.VMEM(basis.shape, bf16),
            pltpu.VMEM(basis.shape, f32),
            pltpu.VMEM((parts, planes, ny, nz), bf16),
            pltpu.VMEM((steps, fields, planes, ny, nz), bf16),
            field,
            field,
            field,
            pltpu.VMEM((steps, 12, planes, ny, nz), f32),
            pltpu.VMEM((krylov * ny, krylov * ny), f32),
            pltpu.VMEM((krylov, nz), f32),
            pltpu.VMEM((krylov, 8, nz), f32),
            pltpu.VMEM((height, blocks * krylov), f32),
            pltpu.VMEM((tiles, height, blocks * krylov), f32),
            pltpu.VMEM((1, width), f32),
            pltpu.VMEM((groups * tiles, 1, width), f32),
            dma((3 + local,)),
            dma((1,)),
            dma((count,)),
            dma((local,)),
            dma((local,)),
            dma((steps, count + 1)),
            dma((2,)),
            dma((2,)),
            dma((groups,)),
            dma((1,)),
            pltpu.SemaphoreType.REGULAR((min(tiles.bit_length() - 1, (-(-rim // slab)).bit_length()) + 4 + -(-rim // slab),)),
        ],
        compiler_params=pltpu.CompilerParams(
            collective_id=0, has_side_effects=True, vmem_limit_bytes=48 << 20
        ),
    )(*(pltpu.with_memory_space_constraint(a, pltpu.HBM) for a in (coupling, basis, snapshots)))
    left, coefs, square, margin = results

    def scaled(left, coefs, square):
        return pl.pallas_call(
            finish,
            name="finish",
            out_shape=tuple(jax.ShapeDtypeStruct(a.shape, f32) for a in (left, coefs, square)),
            in_specs=[whole] * 3,
            out_specs=(outside,) * 3,
            scratch_shapes=[
                pltpu.VMEM(left.shape, f32),
                pltpu.VMEM(square.shape, f32),
                dma((3,)),
            ],
        )(left, coefs, square)

    def summed(left, coefs, square):
        exact = pl.pallas_call(
            functools.partial(square_kernel, tiles),
            name="exact_square",
            out_shape=jax.ShapeDtypeStruct((1, nz), f32),
            in_specs=[whole],
            out_specs=whole,
            scratch_shapes=[
                pltpu.VMEM((1, nz), f32),
                pltpu.VMEM((tiles, 1, nz), f32),
                dma((tiles,)),
                dma((tiles,)),
            ],
            compiler_params=pltpu.CompilerParams(collective_id=1, has_side_effects=True),
        )(left)
        return scaled(left, coefs, exact)

    new_vector, coefs, norms = lax.cond(margin[0, 0] > 0.0, scaled, summed, left, coefs, square)
    return new_vector, coefs, norms[0, :1]


def solution(mesh):
    placed = (P(None, None, "tile", None, None), P("grp", None, "tile", None, None), P())
    return jax.shard_map(
        functools.partial(on_device, mesh.shape["grp"], mesh.shape["tile"]),
        mesh=mesh,
        in_specs=placed,
        out_specs=(P("grp", None, "tile", None, None), P("grp", None), P("grp")),
        check_vma=False,
    )
```

```python
import functools

import jax
import jax.numpy as jnp
from jax import lax
from jax.experimental import pallas as pl
from jax.experimental.pallas import tpu as pltpu
from jax.sharding import PartitionSpec as P

viscosity = 0.5
time_step = 0.3
cancel_limit = 0.01
f32 = jnp.float32
bf16 = jnp.bfloat16
MESH = pl.DeviceIdType.MESH
HIGHEST = lax.Precision.HIGHEST


def spans(slab, rim):
    found = {}
    reach = -(-rim // slab)
    for d in range(1, reach + 1):
        width = min(slab, rim - (d - 1) * slab)
        found[-d] = (slab - width, slab)
        found[d] = (0, width)
    return found


def gram_blocks(krylov, lanes):
    blocks = max(lanes // krylov, 1)
    return (blocks, krylov // blocks) if krylov % (8 * blocks) == 0 else (1, krylov)


def stage(src, old, dst, rates, snap, step, coupling, lo, planes, keep, scale):
    rows, lanes = snap.shape[3], snap.shape[4]
    row = lax.broadcasted_iota(jnp.int32, (rows, lanes), 0)
    top = row == 0
    bottom = row == rows - 1
    mix = [[coupling[k, j] for j in range(5)] for k in range(5)]
    edge = viscosity * time_step

    def cells(field, k, p, shift=0):
        return field[k, pl.ds(p * rows + shift, rows)]

    def make_rates(p):
        base = [snap[step, n, p].astype(f32) for n in range(4)]
        half = [(0.5 * time_step) * base[n] for n in range(3)]
        pull = time_step * base[3]
        found = [edge - half[0], edge + half[0]]
        found += [jnp.where(bottom, 0.0, edge - half[1]), jnp.where(top, 0.0, edge + half[1])]
        found += [edge - half[2], edge + half[2], pull]
        own = 1.0 - 6.0 * edge
        found += [own - pull * mix[k][k] for k in range(5)]
        for n, rate in enumerate(found):
            rates[step, n, p] = rate
        return found

    def body(i, carry):
        p = lo + i
        now = [rates[step, n, p] for n in range(12)] if keep else make_rates(p)
        x_up, x_low, y_up, y_low, z_up, z_low, pull = now[:7]
        center = [cells(src, k, p) for k in range(5)]
        for k in range(5):
            q = center[k]
            others = [j for j in range(5) if j != k]
            coupled = mix[k][others[0]] * center[others[0]]
            for j in others[1:]:
                coupled = coupled + mix[k][j] * center[j]
            total = now[7 + k] * q - pull * coupled
            total = total + (x_up * cells(src, k, p + 1) + x_low * cells(src, k, p - 1))
            total = total + (y_up * cells(src, k, p, 1) + y_low * cells(src, k, p, -1))
            total = total + (z_up * pltpu.roll(q, lanes - 1, 1) + z_low * pltpu.roll(q, 1, 1))
            if keep:
                total = total + keep * cells(old, k, p)
            if scale != 1.0:
                total = total * scale
            dst[k, pl.ds(p * rows, rows)] = total
        return carry

    unroll = max(n for n in range(1, 9) if planes % n == 0)
    lax.fori_loop(0, planes, body, 0, unroll=unroll)


def kernel(
    groups, tiles, coupling_in, basis, snapshots,
    left_out, coef_out, square_out, margin_out,
    coupling, held, plain, start, snap, state, one, two, rates, cross, rows_k, spread,
    gram_send, gram_all, coef_send, coef_all,
    load_sem, start_send, start_recv, snap_send, relay_send, snap_recv,
    share_send, share_recv, pass_send, pass_recv, ready,
):
    g = lax.axis_index("grp")
    t = lax.axis_index("tile")
    krylov, parts, slab, ny, nz = basis.shape
    local = snapshots.shape[0]
    steps = local * groups
    rim = 3 * steps
    planes = slab + 2 * rim
    near = spans(slab, rim)
    offsets = sorted(near)
    position = krylov - groups + g
    levels = [b for b in range(tiles.bit_length() - 1) if (1 << b) in offsets]
    stride = 1 << len(levels)
    length = tiles // stride
    link = t // stride

    def at(group, offset):
        return {"grp": group, "tile": lax.rem(t + (offset % tiles), tiles)}

    def flipped(level):
        bit = 1 << level
        return {"grp": g, "tile": t + bit - 2 * bit * lax.rem(t // bit, 2)}

    def partner(other):
        return {"grp": lax.rem(g + other, groups), "tile": t}

    barrier = pltpu.get_barrier_semaphore()
    reach = max(offsets)

    def crosses(d):
        return t + d >= tiles if d > 0 else t + d < 0

    def greet(peer):
        pl.semaphore_signal(barrier, inc=1, device_id=peer, device_id_type=MESH)

    greeters = groups - 1
    for d in sorted(offsets, key=abs, reverse=True):
        if d > 0:
            greet(at(g, -d))
            greeters = greeters + 1 + jnp.where(crosses(d), groups - 1, 0)

            @pl.when(crosses(-d))
            def _():
                for other in range(1, groups):
                    greet(at(lax.rem(g + other, groups), -d))
        else:
            pl.when(jnp.logical_not(crosses(-d)))(functools.partial(greet, at(g, -d)))
            greeters = greeters + jnp.where(crosses(d), 0, 1)
    held_back = near[reach][1] - near[reach][0]
    carried = reach > 1 and held_back < slab and 2 * reach < tiles
    if carried:
        pl.when(t == reach)(functools.partial(greet, {"grp": g, "tile": tiles - 1}))
        greeters = greeters + jnp.where(t == tiles - 1, 1, 0)
    for other in range(1, groups):
        greet(partner(other))
    for way in (1, -1):
        last = link == (length - 1 if way > 0 else 0)
        greeters = greeters + jnp.where(last, 0, 1)

        @pl.when(jnp.logical_not(last))
        def _():
            greet(at(g, way * stride))

    chunk = 8 if krylov % 8 == 0 else 1
    own = pltpu.make_async_copy(basis.at[position], start.at[:, pl.ds(rim, slab)], load_sem.at[0])
    own.start()
    mix = pltpu.make_async_copy(coupling_in, coupling, load_sem.at[1])
    mix.start()
    for n in range(krylov // chunk):
        part = pl.ds(n * chunk, chunk)
        pltpu.make_async_copy(basis.at[part], held.at[part], load_sem.at[2]).start()

    def target(d, first, last):
        return pl.ds(rim + d * slab + first, last - first)

    start_copies = []
    for n, d in enumerate(offsets):
        first, last = near[d]
        start_copies.append(
            pltpu.make_async_remote_copy(
                src_ref=basis.at[position, :, pl.ds(first, last - first)],
                dst_ref=start.at[:, target(d, first, last)],
                send_sem=start_send.at[0],
                recv_sem=start_recv.at[n],
                device_id=at(g, -d),
                device_id_type=MESH,
            )
        )

    def snap_copy(s, n, d, other):
        first, last = (0, slab) if d == 0 else spans(slab, rim - 3 * s - 1)[d]
        return pltpu.make_async_remote_copy(
            src_ref=snapshots.at[s % local, :, pl.ds(first, last - first)],
            dst_ref=snap.at[s, :, target(d, first, last)],
            send_sem=snap_send.at[s % local],
            recv_sem=snap_recv.at[s, n],
            device_id=at(lax.rem(g + other, groups), -d),
            device_id_type=MESH,
        )

    def local_snap(s):
        return pltpu.make_async_copy(
            snapshots.at[s % local], snap.at[s, :, pl.ds(rim, slab)], load_sem.at[3 + s % local]
        )

    def snap_offsets(s):
        inside = spans(slab, rim - 3 * s - 1)
        return [(n, d) for n, d in enumerate([0] + offsets) if d == 0 or d in inside]

    def snap_each(s, ds, act):
        inside = {d: n for n, d in snap_offsets(s)}

        @pl.when(g == s // local)
        def _():
            for d in ds:
                if d in inside:
                    for other in range(1 if d else groups):
                        if d or other:
                            act(snap_copy(s, inside[d], d, other))
                    if d == reach:
                        @pl.when(crosses(-d))
                        def _():
                            for other in range(1, groups):
                                act(snap_copy(s, inside[d], d, other))

    def relay_copy(s, n, d, other):
        first, last = spans(slab, rim - 3 * s - 1)[d]
        cells = snap.at[s, :, target(d, first, last)]
        return pltpu.make_async_remote_copy(
            src_ref=cells,
            dst_ref=cells,
            send_sem=relay_send.at[s % local],
            recv_sem=snap_recv.at[s, n],
            device_id=at(lax.rem(g + other, groups), 0),
            device_id_type=MESH,
        )

    def relay(s, ds):
        @pl.when(g == s // local)
        def _():
            for n, d in snap_offsets(s):
                if d and d in ds:
                    snap_copy(s, n, d, 0).wait_recv()

                    def forward():
                        for other in range(1, groups):
                            relay_copy(s, n, d, other).start()

                    if d == reach:
                        pl.when(jnp.logical_not(crosses(d)))(forward)
                    else:
                        forward()
            if 0 in ds:
                local_snap(s).wait()

    def receive(s, ds):
        if groups > 1:
            @pl.when(g != s // local)
            def _():
                for n, d in snap_offsets(s):
                    if d in ds:
                        (relay_copy if d else snap_copy)(s, n, d, 1).wait_recv()

    for s in range(steps):
        @pl.when(g == s // local)
        def _():
            local_snap(s).start()

    pl.semaphore_wait(barrier, greeters)
    def send(s, ds):
        snap_each(s, ds, lambda copy: copy.start())
        if s == 0:
            for d in ds:
                if d:
                    start_copies[offsets.index(d)].start()

    def tell(n, peer):
        pl.semaphore_signal(ready.at[n], inc=1, device_id=peer, device_id_type=MESH)

    edge = len(levels) + 3

    for d in offsets:
        if d < 0:
            @pl.when(crosses(-d))
            def _():
                for other in range(groups):
                    tell(edge - d - 1, at(lax.rem(g + other, groups), -d))

    upper = t >= tiles // 2
    ahead = [d for d in offsets if d < 0]
    back = [-d for d in ahead]

    def send_some(s, soon):
        for d in sorted(offsets, key=abs):
            wanted = t - d >= tiles // 2 if d < 0 else t - d < tiles // 2
            wanted = wanted if soon else jnp.logical_not(wanted)
            if d > 0:
                wanted = wanted & jnp.logical_not(crosses(-d))
            pl.when(wanted)(functools.partial(send, s, [d]))

    def sided(act, *ds):
        for way, on in ((1, upper), (-1, jnp.logical_not(upper))):
            @pl.when(on)
            def _():
                act([way * d for d in ds])

    near_ds, far_ds = sorted(ahead, key=abs), sorted(back)

    turn = edge + len(back)
    if carried:
        pl.when(t == tiles - 1)(functools.partial(tell, turn, {"grp": g, "tile": reach}))

    def wait_far(d):
        pl.semaphore_wait(ready.at[edge + d - 1], groups)

    def start_copy(d, group, last):
        first = near[d][0]
        return pltpu.make_async_remote_copy(
            src_ref=basis.at[krylov - groups + group, :, pl.ds(first, last - first)],
            dst_ref=start.at[:, target(d, first, last)],
            send_sem=start_send.at[0],
            recv_sem=start_recv.at[offsets.index(d)],
            device_id=at(group, -d),
            device_id_type=MESH,
        )

    def send_first():
        wait_far(1)
        snap_each(0, [1], lambda copy: copy.start())
        start_copy(1, g, slab - held_back if carried else slab).start()
        for s in range(1, steps):
            send(s, [1])
        for d in sorted(back)[1:]:
            wait_far(d)
            for s in range(steps):
                snap_each(s, [d], lambda copy: copy.start())

    def send_second():
        for d in sorted(back)[1:]:
            for group in range(groups):
                start_copy(d, group, near[d][1]).start()

    def send_carried():
        start_copies[offsets.index(-reach)].wait_recv()
        pl.semaphore_wait(ready.at[turn], 1)
        pltpu.make_async_remote_copy(
            src_ref=start.at[:, target(-reach, slab - held_back, slab)],
            dst_ref=start.at[:, target(1, slab - held_back, slab)],
            send_sem=start_send.at[0],
            recv_sem=start_recv.at[offsets.index(1)],
            device_id={"grp": g, "tile": tiles - 1},
            device_id_type=MESH,
        ).start()

    def send_late():
        for d in sorted(back)[1:]:
            @pl.when((t > 0) & crosses(-d))
            def _():
                wait_far(d)
                for s in range(steps):
                    send(s, [d])

    for s in range(steps):
        snap_each(s, [0], lambda copy: copy.start())
        send_some(s, True)

    def send_far():
        for s in range(steps):
            send_some(s, False)

    at_end = (t < reach) | (t >= tiles - reach)
    pl.when(at_end)(send_far)

    def flip_step(n):
        if n:
            pl.semaphore_wait(ready.at[n - 1], 1)
        if n < len(levels):
            tell(n, flipped(levels[n]))

    def pass_on(sem, way):
        head = link == (0 if way > 0 else length - 1)
        tail = link == (length - 1 if way > 0 else 0)

        @pl.when(jnp.logical_not(head))
        def _():
            pl.semaphore_wait(ready.at[sem], 1)

        @pl.when(jnp.logical_not(tail))
        def _():
            tell(sem, at(g, way * stride))

    def chain_step(n):
        if length > 1:
            upper = link >= length // 2
            for way in (1, -1):
                @pl.when(upper == (way < 0))
                def _():
                    mine = -way if n else way
                    pass_on(len(levels) + (mine < 0), mine)

    def tell_group():
        for other in range(1, groups):
            tell(len(levels) + 2, partner(other))

    pltpu.make_async_copy(basis, held, load_sem.at[2]).wait()

    def expand(k, carry):
        plain[k] = held[k].astype(f32)
        return carry

    lax.fori_loop(0, krylov, expand, 0)
    size = krylov * ny
    blocks, height = gram_blocks(krylov, nz)

    def gram_copy(other):
        return pltpu.make_async_remote_copy(
            src_ref=gram_send,
            dst_ref=gram_send,
            send_sem=pass_send.at[other],
            recv_sem=pass_recv.at[0],
            device_id=partner(other),
            device_id_type=MESH,
        )

    @pl.when(g == 0)
    def _():
        for c in range(parts):
            wide = jnp.concatenate([held[:, c, x].reshape(size, nz) for x in range(slab)], axis=1)
            piece = lax.dot_general(wide, wide, (((1,), (1,)), ((), ())), preferred_element_type=f32)
            cross[...] = cross[...] + piece if c else piece
            if c == parts // 2:
                pl.when(jnp.logical_not(at_end))(send_far)
        line = lax.broadcasted_iota(jnp.int32, (size, size), 0)
        column = lax.broadcasted_iota(jnp.int32, (size, size), 1)
        kept = jnp.where(lax.rem(line, ny) == lax.rem(column, ny), cross[...], 0.0)
        kept = jnp.sum(kept.reshape(krylov, ny, size), axis=1)
        pick = (
            lax.broadcasted_iota(jnp.int32, (size, krylov), 0) // ny
            == lax.broadcasted_iota(jnp.int32, (size, krylov), 1)
        ).astype(f32)
        gram = jnp.dot(kept, pick, precision=HIGHEST, preferred_element_type=f32)
        gram_send[...] = jnp.concatenate(
            [gram[n * height : (n + 1) * height] for n in range(blocks)], axis=1
        )
        for other in range(1, groups):
            gram_copy(other).start()

    @pl.when(g == groups - 1)
    def _():
        for n in range(len(levels) + 1):
            flip_step(n)

    pl.when(jnp.logical_not(at_end) & (g != 0))(send_far)

    @pl.when(g == groups - 1)
    def _():
        chain_step(0)

    pl.when(t == 0)(send_first)
    send_late()
    if carried:
        pl.when(t == reach)(send_carried)
    @pl.when(g == groups - 1)
    def _():
        chain_step(1)
        for other in range(1, groups):
            tell(len(levels) + 2, partner(other))

    def spread_out(n, send, everyone, reached):
        others = everyone.at[pl.ds(0, reached * tiles - 1)]
        place = t if reached == 1 else g * tiles + t

        def begin():
            def one(peer, carry):
                def to(other):
                    pltpu.make_async_remote_copy(
                        src_ref=send,
                        dst_ref=everyone.at[place],
                        send_sem=share_send.at[n],
                        recv_sem=share_recv.at[n],
                        device_id={"grp": lax.rem(g + other, groups), "tile": peer},
                        device_id_type=MESH,
                    ).start()

                pl.when(peer != t)(functools.partial(to, 0))
                for other in range(1, reached):
                    to(other)
                return carry

            lax.fori_loop(0, tiles, one, 0)
            everyone[place] = send[...]

        def arrive():
            pltpu.make_async_copy(others, others, share_recv.at[n]).wait()

        def drain():
            pltpu.make_async_copy(others, others, share_send.at[n]).wait()

        return begin, arrive, drain

    gram_begin, gram_arrive, gram_drain = spread_out(0, gram_send, gram_all, 1)
    coef_begin, coef_arrive, coef_drain = spread_out(1, coef_send, coef_all, groups)
    def widen(d):
        def one(p, carry):
            for k in range(parts):
                state[k, pl.ds(p * ny, ny)] = start[k, p].astype(f32)
            return carry

        lo, width = (rim, slab) if d == 0 else (rim + d * slab + near[d][0], near[d][1] - near[d][0])
        lax.fori_loop(lo, lo + width, one, 0)

    def arrive(ds):
        for d in ds:
            if d == -reach and carried:
                pl.when(t != reach)(start_copies[offsets.index(d)].wait_recv)
            elif d:
                start_copies[offsets.index(d)].wait_recv()
            else:
                own.wait()
                mix.wait()
            widen(d)

    keeps = (0.0, 3.0, 2.0)
    ways = ((state, one), (one, two), (two, state))

    def march(s, known, new):
        for n, (src, dst) in enumerate(ways):
            k = 3 * s + n + 1
            lo, hi = max(k, known - k), new - k
            if hi > lo:
                first = jnp.where(upper, lo, planes - hi) + t // tiles
                scale = 6.0 ** -steps if k == 3 * steps else 1.0
                stage(src, state, dst, rates, snap, s, coupling, first, hi - lo, keeps[n], scale)

    def relay_far(s, d, early):
        for way, on in ((1, upper), (-1, jnp.logical_not(upper))):
            seam = crosses(way * d)

            @pl.when(on & (jnp.logical_not(seam) if early else seam))
            def _():
                relay(s, [way * d])

    sided(lambda ds: relay(0, [0] + ds), *near_ds)
    sided(arrive, *near_ds)
    arrive([0])
    for s in range(1, steps):
        sided(lambda ds: relay(s, [0] + ds), *near_ds)
    sided(lambda ds: receive(0, [0] + ds), *near_ds)
    pl.when((t == 0) & (g == groups - 1))(send_second)
    known = 0
    for far in (False, True):
        if far:
            for d in far_ds:
                relay_far(0, d, False)
            sided(arrive, *far_ds)
            for s in range(1, steps):
                for d in far_ds:
                    relay_far(s, d, False)
            sided(lambda ds: receive(0, ds), *far_ds)
        new = planes if far else rim + slab
        for s in range(steps):
            if s:
                sided(lambda ds: receive(s, ds), *(far_ds if far else [0] + near_ds))
            march(s, known, new)
            if not far and s == 0:
                for d in far_ds:
                    relay_far(0, d, True)
                for later in range(1, steps):
                    for d in far_ds:
                        relay_far(later, d, True)
        known = new
        if not far:
            if groups > 1:
                @pl.when(g != groups - 1)
                def _():
                    pl.semaphore_wait(ready.at[len(levels) + 2], 1)

                @pl.when(g != 0)
                def _():
                    gram_copy(0).wait_recv()

            gram_begin()

    count = f32(parts * slab * ny * nz * tiles)

    group = 8 if krylov % 8 == 0 else 1

    def project(i, carry):
        totals = [jnp.zeros((ny, nz), f32) for _ in range(group)]
        for c in range(parts):
            for x in range(slab):
                field = state[c, pl.ds((rim + x) * ny, ny)]
                for n in range(group):
                    totals[n] = totals[n] + plain[i * group + n, c, x] * field
        for n in range(group):
            rows_k[pl.ds(i * group + n, 1), :] = jnp.sum(totals[n], axis=0, keepdims=True)
        return carry

    lax.fori_loop(0, krylov // group, project, 0, unroll=2 if krylov % (2 * group) == 0 else 1)
    ones = jnp.ones((8, nz), f32)
    inner = lax.dot_general(
        ones, rows_k[...], (((1,), (1,)), ((), ())), precision=HIGHEST, preferred_element_type=f32
    )
    own_square = jnp.zeros((ny, nz), f32)
    for c in range(parts):
        for x in range(slab):
            own_square = own_square + state[c, pl.ds((rim + x) * ny, ny)] * state[c, pl.ds((rim + x) * ny, ny)]
    own_square = jnp.sum(jnp.sum(own_square, axis=0, keepdims=True), axis=1, keepdims=True)
    coef_send[...] = jnp.concatenate(
        [inner[0:1], jnp.broadcast_to(own_square, (1, coef_send.shape[1] - krylov))], axis=1
    )
    coef_begin()
    def all_sent(cells, sem):
        pltpu.make_async_copy(cells, cells, sem).wait()

    moved = sum(near[d][1] - near[d][0] for d in sorted(back)[1:])
    spare = held_back if carried else 0
    all_sent(start.at[:, pl.ds(0, 2 * rim - moved - spare)], start_send.at[0])
    if moved + spare:
        @pl.when(t > 0)
        def _():
            all_sent(start.at[:, pl.ds(0, moved + spare)], start_send.at[0])

        @pl.when((t == 0) & (g == groups - 1))
        def _():
            for _ in range(groups):
                all_sent(start.at[:, pl.ds(0, moved)], start_send.at[0])

    if spare:
        @pl.when(t == reach)
        def _():
            all_sent(start.at[:, pl.ds(0, spare)], start_send.at[0])

    for s in range(steps):
        around = 2 * (rim - 3 * s - 1)

        @pl.when(g == s // local)
        def _():
            all_sent(snap.at[s, :, pl.ds(0, around)], snap_send.at[s % local])
            last = spans(slab, rim - 3 * s - 1).get(reach, (0, 0))
            last = last[1] - last[0]
            for other in range(1, groups):
                all_sent(snap.at[s, :, pl.ds(0, slab)], snap_send.at[s % local])
                all_sent(snap.at[s, :, pl.ds(0, around - last)], relay_send.at[s % local])
                if last:
                    @pl.when(crosses(-reach))
                    def _():
                        all_sent(snap.at[s, :, pl.ds(0, last)], snap_send.at[s % local])

                    @pl.when(jnp.logical_not(crosses(reach)))
                    def _():
                        all_sent(snap.at[s, :, pl.ds(0, last)], relay_send.at[s % local])

    gram_drain()

    @pl.when(g == 0)
    def _():
        for other in range(1, groups):
            gram_copy(other).wait_send()

    gram_arrive()
    packed = jnp.sum(gram_all[...], axis=0) / count
    gram = jnp.concatenate(
        [packed[:, n * krylov : (n + 1) * krylov] for n in range(blocks)], axis=0
    )
    same = lax.broadcasted_iota(jnp.int32, gram.shape, 0) == lax.broadcasted_iota(jnp.int32, gram.shape, 1)
    times = functools.partial(jnp.dot, precision=HIGHEST, preferred_element_type=f32)
    twice = jnp.where(same, 2.0, 0.0) - gram
    both = jnp.concatenate([twice, times(twice, gram)], axis=1)
    reach_row = jnp.sum(jnp.abs(gram), axis=0, keepdims=True)
    coef_arrive()
    sums = [jnp.sum(coef_all[n * tiles : (n + 1) * tiles], axis=0) / count for n in range(groups)]
    sums = jnp.concatenate(sums + [jnp.zeros((-groups % 8, sums[0].shape[1]), f32)], axis=0)
    first_rows, work_square = sums[:, :krylov], sums[:, krylov : krylov + 1]
    mixed = times(first_rows, both)
    every, turned = mixed[:, :krylov], mixed[:, krylov:]
    group_row = lax.broadcasted_iota(jnp.int32, work_square.shape, 0)
    own_every = jnp.sum(jnp.where(group_row == g, every, 0.0), axis=0, keepdims=True)
    for k in range(krylov):
        spread[k] = jnp.broadcast_to(own_every[:, k : k + 1], (8, nz))
    for x in range(slab):
        removed = [jnp.zeros((ny // 8, 8, nz), f32) for _ in range(parts)]
        for k in range(krylov):
            factor = spread[k][None]
            for c in range(parts):
                removed[c] = removed[c] + factor * plain[k, c, x].reshape(ny // 8, 8, nz)
        for c in range(parts):
            left_out[0, c, x] = state[c, pl.ds((rim + x) * ny, ny)] - removed[c].reshape(ny, nz)
    linear = 2.0 * every * first_rows
    bent = every * turned
    bound = jnp.abs(linear) + every * every * reach_row
    square = work_square + jnp.sum(bent - linear, axis=1, keepdims=True)
    bound = work_square + jnp.sum(bound, axis=1, keepdims=True)
    margin = jnp.where(group_row < groups, square - cancel_limit * bound, jnp.inf)
    margin_out[...] = jnp.broadcast_to(jnp.min(margin, axis=0, keepdims=True), margin_out.shape)
    square = jnp.sum(jnp.where(group_row == g, square, 0.0), axis=0, keepdims=True)
    square_out[...] = jnp.broadcast_to(square, square_out.shape)
    coef_out[...] = own_every
    coef_drain()


def square_kernel(tiles, left, square_out, send, everyone, ssem, rsem):
    g = lax.axis_index("grp")
    t = lax.axis_index("tile")
    _, parts, slab, ny, nz = left.shape
    barrier = pltpu.get_barrier_semaphore()

    def peer(r):
        return {"grp": g, "tile": lax.rem(t + r, tiles)}

    def greet(r, carry):
        pl.semaphore_signal(barrier, inc=1, device_id=peer(r), device_id_type=MESH)
        return carry

    lax.fori_loop(1, tiles, greet, 0)
    pl.semaphore_wait(barrier, tiles - 1)
    total = jnp.zeros((ny, nz), f32)
    for c in range(parts):
        for x in range(slab):
            total = total + left[0, c, x] * left[0, c, x]
    send[...] = jnp.sum(total, axis=0, keepdims=True)

    def copy(r, sender):
        return pltpu.make_async_remote_copy(
            src_ref=send,
            dst_ref=everyone.at[sender],
            send_sem=ssem.at[r],
            recv_sem=rsem.at[r],
            device_id=peer(r),
            device_id_type=MESH,
        )

    lax.fori_loop(1, tiles, lambda r, c: (copy(r, t).start(), c)[1], 0)
    everyone[t] = send[...]
    lax.fori_loop(
        1, tiles, lambda r, c: (copy(r, lax.rem(t - r + tiles, tiles)).wait_recv(), c)[1], 0
    )
    count = f32(parts * slab * ny * nz * tiles)
    square = jnp.sum(jnp.sum(everyone[...], axis=0), axis=1, keepdims=True) / count
    square_out[...] = jnp.broadcast_to(square, square_out.shape)
    lax.fori_loop(1, tiles, lambda r, c: (copy(r, t).wait_send(), c)[1], 0)


def finish(left, coefs, square, out, coef_out, norm_out, held, norm_row, sem):
    norm = jnp.sqrt(square[...])
    norm_row[...] = norm
    inverse = jnp.broadcast_to(1.0 / norm, left.shape[3:])
    copies = [
        pltpu.make_async_copy(norm_row, norm_out, sem.at[0]),
        pltpu.make_async_copy(coefs, coef_out, sem.at[1]),
    ]
    for c in range(left.shape[1]):
        for x in range(left.shape[2]):
            held[0, c, x] = left[0, c, x] * inverse
    copies.append(pltpu.make_async_copy(held, out, sem.at[2]))
    for copy in copies:
        copy.start()
    for copy in copies:
        copy.wait()


def on_device(groups, tiles, basis, snapshots, coupling):
    krylov, parts, slab, ny, nz = basis.shape
    local, fields = snapshots.shape[:2]
    steps = local * groups
    rim = 3 * steps
    planes = slab + 2 * rim
    count = len(spans(slab, rim))
    blocks, height = gram_blocks(krylov, nz)
    width = -(-(krylov + 1) // nz) * nz
    dma = pltpu.SemaphoreType.DMA
    field = pltpu.VMEM((parts, planes * ny, nz), f32)
    whole = pl.BlockSpec(memory_space=pltpu.VMEM)
    outside = pl.BlockSpec(memory_space=pltpu.HBM)
    results = pl.pallas_call(
        functools.partial(kernel, groups, tiles),
        name="propagate",
        out_shape=(
            jax.ShapeDtypeStruct((1, parts, slab, ny, nz), f32),
            jax.ShapeDtypeStruct((1, krylov), f32),
            jax.ShapeDtypeStruct((1, nz), f32),
            jax.ShapeDtypeStruct((1, nz), f32),
        ),
        in_specs=[outside] * 3,
        out_specs=(whole,) * 4,
        scratch_shapes=[
            pltpu.SMEM(coupling.shape, f32),
            pltpu.VMEM(basis.shape, bf16),
            pltpu.VMEM(basis.shape, f32),
            pltpu.VMEM((parts, planes, ny, nz), bf16),
            pltpu.VMEM((steps, fields, planes, ny, nz), bf16),
            field,
            field,
            field,
            pltpu.VMEM((steps, 12, planes, ny, nz), f32),
            pltpu.VMEM((krylov * ny, krylov * ny), f32),
            pltpu.VMEM((krylov, nz), f32),
            pltpu.VMEM((krylov, 8, nz), f32),
            pltpu.VMEM((height, blocks * krylov), f32),
            pltpu.VMEM((tiles, height, blocks * krylov), f32),
            pltpu.VMEM((1, width), f32),
            pltpu.VMEM((groups * tiles, 1, width), f32),
            dma((3 + local,)),
            dma((1,)),
            dma((count,)),
            dma((local,)),
            dma((local,)),
            dma((steps, count + 1)),
            dma((2,)),
            dma((2,)),
            dma((groups,)),
            dma((1,)),
            pltpu.SemaphoreType.REGULAR((min(tiles.bit_length() - 1, (-(-rim // slab)).bit_length()) + 4 + -(-rim // slab),)),
        ],
        compiler_params=pltpu.CompilerParams(
            collective_id=0, has_side_effects=True, vmem_limit_bytes=48 << 20
        ),
    )(*(pltpu.with_memory_space_constraint(a, pltpu.HBM) for a in (coupling, basis, snapshots)))
    left, coefs, square, margin = results

    def scaled(left, coefs, square):
        return pl.pallas_call(
            finish,
            name="finish",
            out_shape=tuple(jax.ShapeDtypeStruct(a.shape, f32) for a in (left, coefs, square)),
            in_specs=[whole] * 3,
            out_specs=(outside,) * 3,
            scratch_shapes=[
                pltpu.VMEM(left.shape, f32),
                pltpu.VMEM(square.shape, f32),
                dma((3,)),
            ],
        )(left, coefs, square)

    def summed(left, coefs, square):
        exact = pl.pallas_call(
            functools.partial(square_kernel, tiles),
            name="exact_square",
            out_shape=jax.ShapeDtypeStruct((1, nz), f32),
            in_specs=[whole],
            out_specs=whole,
            scratch_shapes=[
                pltpu.VMEM((1, nz), f32),
                pltpu.VMEM((tiles, 1, nz), f32),
                dma((tiles,)),
                dma((tiles,)),
            ],
            compiler_params=pltpu.CompilerParams(collective_id=1, has_side_effects=True),
        )(left)
        return scaled(left, coefs, exact)

    new_vector, coefs, norms = lax.cond(margin[0, 0] > 0.0, scaled, summed, left, coefs, square)
    return new_vector, coefs, norms[0, :1]


def solution(mesh):
    placed = (P(None, None, "tile", None, None), P("grp", None, "tile", None, None), P())
    return jax.shard_map(
        functools.partial(on_device, mesh.shape["grp"], mesh.shape["tile"]),
        mesh=mesh,
        in_specs=placed,
        out_specs=(P("grp", None, "tile", None, None), P("grp", None), P("grp")),
        check_vma=False,
    )
```
